32 devices in a mesh: dp: 16 (over z, y, x), zero: 2 (over core).
Axes of the slice: x: 2, y: 2, z: 4, core: 2. Of those that a mesh axis runs over, the one named last changes fastest.
Arguments:
- inputs: bfloat16 [31360, 768], P(('dp', 'zero')), may hold values from -6 to 6
- cotangent: bfloat16 [31360, 768], P(('dp', 'zero')), may hold values from -6 to 6
- master_joint: float32 [768, 2304], P('zero'), may hold values from -0.28867513 to 0.28867513
- master_merge: float32 [768, 768], P('zero'), may hold values from -1.4433757 to 1.4433757
- master_expand: float32 [768, 3072], P('zero'), may hold values from -0.28867513 to 0.28867513
- master_reduce: float32 [3072, 768], P('zero'), may hold values from -0.14433757 to 0.14433757
- master_vectors: float32 [12, 768], P(None, 'zero'), may hold values from -1.25 to 1.25
- moment_joint: float32 [768, 2304], P('zero'), may hold values from -22.135944 to 22.135944
- moment_merge: float32 [768, 768], P('zero'), may hold values from -22.135944 to 22.135944
- moment_expand: float32 [768, 3072], P('zero'), may hold values from -22.135944 to 22.135944
- moment_reduce: float32 [3072, 768], P('zero'), may hold values from -22.135944 to 22.135944
- moment_vectors: float32 [12, 768], P(None, 'zero'), may hold values from -44.27189 to 44.27189
- square_joint: float32 [768, 2304], P('zero'), may hold values from 7.65625 to 30.625
- square_merge: float32 [768, 768], P('zero'), may hold values from 7.65625 to 30.625
- square_expand: float32 [768, 3072], P('zero'), may hold values from 7.65625 to 30.625
- square_reduce: float32 [3072, 768], P('zero'), may hold values from 7.65625 to 30.625
- square_vectors: float32 [12, 768], P(None, 'zero'), may hold values from 30.625 to 122.5
Outputs:
- outputs: bfloat16 [31360, 768], P(('dp', 'zero'))
- input_grad: float32 [31360, 768], P(('dp', 'zero'))
- grad_joint: float32 [768, 2304], P('zero')
- grad_merge: float32 [768, 768], P('zero')
- grad_expand: float32 [768, 3072], P('zero')
- grad_reduce: float32 [3072, 768], P('zero')
- grad_vectors: float32 [12, 768], P(None, 'zero')
- weight_joint: float32 [768, 2304], P('zero')
- weight_merge: float32 [768, 768], P('zero')
- weight_expand: float32 [768, 3072], P('zero')
- weight_reduce: float32 [3072, 768], P('zero')
- weight_vectors: float32 [12, 768], P(None, 'zero')
- first_joint: float32 [768, 2304], P('zero')
- first_merge: float32 [768, 768], P('zero')
- first_expand: float32 [768, 3072], P('zero')
- first_reduce: float32 [3072, 768], P('zero')
- first_vectors: float32 [12, 768], P(None, 'zero')
- second_joint: float32 [768, 2304], P('zero')
- second_merge: float32 [768, 768], P('zero')
- second_expand: float32 [768, 3072], P('zero')
- second_reduce: float32 [3072, 768], P('zero')
- second_vectors: float32 [12, 768], P(None, 'zero')
- copy_joint: bfloat16 [768, 2304], P('zero')
- copy_merge: bfloat16 [768, 768], P('zero')
- copy_expand: bfloat16 [768, 3072], P('zero')
- copy_reduce: bfloat16 [3072, 768], P('zero')
- copy_vectors: bfloat16 [12, 768], P(None, 'zero')
- norm_values: float32 [8], replicated
The draws below stay inside these ranges and needn't reach their ends.
All inputs are finite; a program needn't handle non-finite values.
Results may differ from the reference program's by a relative error of at most 0.013.
The reference program's roundings to bfloat16 on the way count: a program that leaves them out, or rounds other values in their place, can miss the bound.
Values may be sent and summed in bfloat16 or wider, within the bound.
No kernel may reach another device: no remote copies, remote signals or barrier semaphores. Data moves between devices by JAX's collectives and lax.ppermute only.
A program may use at most 320 MiB of HBM per device.

```python
import jax
import jax.numpy as jnp
from jax import lax

D = 768
HEADS = 12
HD = 64
FF = 3072
FRAME = 196
FR_DEV = 5
STEP = 4
TOKENS = 31360
N_DP = 16
N_ZERO = 2


def rising(length, low_end, high_end):
    position = jnp.arange(length, dtype=jnp.float32) / max(length - 1, 1)
    return low_end + (high_end - low_end) * position


def row_lift(length):
    return rising(length, 0.6, 1.8)


def entries(key, array_shape):
    return jnp.clip(jax.random.normal(key, array_shape, jnp.float32), -4.0, 4.0)


def grad_size(weight):
    return weight * FR_DEV * FRAME / TOKENS ** 0.5


def master_draw(key, salt_value, row_count, col_count, factor):
    fresh_key = jax.random.fold_in(key, salt_value)
    lift_factor = row_lift(row_count)[:, None]
    return entries(fresh_key, (row_count, col_count)) * lift_factor * (factor * row_count ** (-0.5))


def moment_draw(key, salt_value, row_count, col_count, weight, along_rows):
    fresh_key = jax.random.fold_in(key, salt_value)
    if along_rows:
        lift_factor = row_lift(row_count)[:, None]
    else:
        lift_factor = row_lift(col_count)[None, :]
    return entries(fresh_key, (row_count, col_count)) * lift_factor * (0.5 * grad_size(weight))


def square_draw(key, salt_value, row_count, col_count, weight):
    fresh_key = jax.random.fold_in(key, salt_value)
    spread = jax.random.uniform(fresh_key, (row_count, col_count), jnp.float32, 1.0, 4.0)
    return spread * grad_size(weight) ** 2


def draw_master_joint(key, part):
    return master_draw(key, 1, D, 3 * D, 1.0)


def draw_master_merge(key, part):
    return master_draw(key, 2, D, D, 5.0)


def draw_master_expand(key, part):
    return master_draw(key, 3, D, FF, 1.0)


def draw_master_reduce(key, part):
    return master_draw(key, 4, FF, D, 1.0)


def draw_moment_joint(key, part):
    return moment_draw(key, 11, D, 3 * D, 0.5, True)


def draw_moment_merge(key, part):
    return moment_draw(key, 12, D, D, 0.5, True)


def draw_moment_expand(key, part):
    return moment_draw(key, 13, D, FF, 0.5, True)


def draw_moment_reduce(key, part):
    return moment_draw(key, 14, FF, D, 0.5, True)


def draw_moment_vectors(key, part):
    return moment_draw(key, 15, 12, D, 1.0, False)


def draw_square_joint(key, part):
    return square_draw(key, 21, D, 3 * D, 0.5)


def draw_square_merge(key, part):
    return square_draw(key, 22, D, D, 0.5)


def draw_square_expand(key, part):
    return square_draw(key, 23, D, FF, 0.5)


def draw_square_reduce(key, part):
    return square_draw(key, 24, FF, D, 0.5)


def draw_square_vectors(key, part):
    return square_draw(key, 25, 12, D, 1.0)


def block_scale(rng, shape, split, least, top_value):
    factor_of = 1.0
    for dim, shards_of in split:
        draws = jax.random.uniform(jax.random.fold_in(jax.random.fold_in(rng, 6), dim), (shards_of,), jnp.float32, least / len(split), top_value / len(split))
        factor_of = factor_of * jnp.repeat(jnp.exp(draws), shape[dim] // shards_of).reshape((-1,) + (1,) * (len(shape) - 1 - dim))
    return factor_of


def noise(rng, dims, deviation, reach, split=(), kind=jnp.bfloat16):
    factor_of = block_scale(rng, dims, split, -0.22, 0.18) if split else 1.0
    array = jax.random.normal(rng, dims, jnp.float32) * deviation * factor_of
    return jnp.minimum(jnp.maximum(array, -reach), reach).astype(kind)


def setup_inputs(seed: int = 0) -> dict:
    splits = jax.random.split(jax.random.key(seed), 18)
    inputs = noise(splits[0], (TOKENS, D), 1.0, 6.0, ((0, 32),))
    cotangent = noise(splits[1], (TOKENS, D), 1.0, 6.0, ((0, 32),))
    master_joint = draw_master_joint(jax.random.fold_in(splits[17], 71), 0)
    master_merge = draw_master_merge(jax.random.fold_in(splits[17], 71), 0)
    master_expand = draw_master_expand(jax.random.fold_in(splits[17], 71), 0)
    master_reduce = draw_master_reduce(jax.random.fold_in(splits[17], 71), 0)
    master_vectors = noise(splits[6], (12, D), 0.2, 1.25, ((1, 2),), jnp.float32)
    moment_joint = draw_moment_joint(jax.random.fold_in(splits[17], 71), 0)
    moment_merge = draw_moment_merge(jax.random.fold_in(splits[17], 71), 0)
    moment_expand = draw_moment_expand(jax.random.fold_in(splits[17], 71), 0)
    moment_reduce = draw_moment_reduce(jax.random.fold_in(splits[17], 71), 0)
    moment_vectors = draw_moment_vectors(jax.random.fold_in(splits[17], 71), 0)
    square_joint = draw_square_joint(jax.random.fold_in(splits[17], 71), 0)
    square_merge = draw_square_merge(jax.random.fold_in(splits[17], 71), 0)
    square_expand = draw_square_expand(jax.random.fold_in(splits[17], 71), 0)
    square_reduce = draw_square_reduce(jax.random.fold_in(splits[17], 71), 0)
    square_vectors = draw_square_vectors(jax.random.fold_in(splits[17], 71), 0)
    return dict(inputs=inputs, cotangent=cotangent, master_joint=master_joint, master_merge=master_merge, master_expand=master_expand, master_reduce=master_reduce, master_vectors=master_vectors, moment_joint=moment_joint, moment_merge=moment_merge, moment_expand=moment_expand, moment_reduce=moment_reduce, moment_vectors=moment_vectors, square_joint=square_joint, square_merge=square_merge, square_expand=square_expand, square_reduce=square_reduce, square_vectors=square_vectors)


@jax.custom_vjp
def low(v):
    return lax.optimization_barrier(v.astype(jnp.bfloat16)).astype(jnp.float32)

@jax.custom_vjp
def low_back(v):
    return v

def low_keep(v):
    return (low(v), None)

def low_pass(kept, grad):
    return (grad,)

def back_keep(v):
    return (v, None)

def back_low(kept, grad):
    return (low(grad),)
low.defvjp(low_keep, low_pass)
low_back.defvjp(back_keep, back_low)
highest = lax.Precision.HIGHEST
norm_eps = 1e-06
adam_eps = 1e-06
decay_rate = 0.5
weight_decay = 0.01
matrix_rate = 0.5
vector_rate = 0.1

def layer_norm(values, gain_row, shift_row):
    row_mean = lax.optimization_barrier(jnp.mean(values, axis=-1, keepdims=True))
    centred = values - row_mean
    spread = lax.optimization_barrier(jnp.mean(centred * centred, axis=-1, keepdims=True))
    return centred * lax.rsqrt(spread + norm_eps) * (1.0 + gain_row) + shift_row

def product(left_op, right_op):
    return jnp.dot(left_op, right_op, precision=highest, preferred_element_type=jnp.float32)

def attend(frame_block):
    queries = frame_block[:, :, 0]
    key_rows = frame_block[:, :, 1]
    values = frame_block[:, :, 2]
    scores = jnp.einsum('fqhd,fkhd->fhqk', queries, key_rows, precision=highest) * HD ** (-0.5)
    scores = low_back(scores)
    prob_low = low(jax.nn.softmax(scores, axis=-1))
    mixed = jnp.einsum('fhqk,fkhd->fqhd', prob_low, values, precision=highest)
    return mixed.reshape(FR_DEV, FRAME, HEADS * HD)

def forward(inputs, w_joint, w_merge, w_expand, w_reduce, vectors):
    tok_count = inputs.shape[0]
    normed = low(layer_norm(inputs, vectors[0], vectors[1]))
    joint_bias = jnp.concatenate([vectors[2], jnp.zeros_like(vectors[2]), vectors[3]])
    joint = low(low_back(product(normed, w_joint) + joint_bias))
    blocks = joint.reshape(tok_count // (FR_DEV * FRAME), FR_DEV, FRAME, 3, HEADS, HD)
    mixed = lax.map(jax.checkpoint(attend), blocks).reshape(tok_count, D)
    mixed = low(low_back(mixed))
    middle = inputs + low_back(product(mixed, w_merge) + vectors[4])
    normed_two = low(layer_norm(middle, vectors[5], vectors[6]))
    hidden = low_back(product(normed_two, w_expand) + vectors[7:11].reshape(FF))
    active = low(jax.nn.gelu(hidden, approximate=False))
    return middle + low_back(product(active, w_reduce) + vectors[11])

def lamb_moments(gradient, first_old, second_old):
    correction = 1.0 - decay_rate ** STEP
    first_new = decay_rate * first_old + (1.0 - decay_rate) * gradient
    second_new = decay_rate * second_old + (1.0 - decay_rate) * gradient * gradient
    direction = first_new / correction / (jnp.sqrt(second_new / correction) + adam_eps)
    return (first_new, second_new, direction)

def reference(inputs, cotangent, master_joint, master_merge, master_expand, master_reduce, master_vectors, moment_joint, moment_merge, moment_expand, moment_reduce, moment_vectors, square_joint, square_merge, square_expand, square_reduce, square_vectors):
    masters = [master_joint, master_merge, master_expand, master_reduce, master_vectors]
    moments = [moment_joint, moment_merge, moment_expand, moment_reduce, moment_vectors]
    squares = [square_joint, square_merge, square_expand, square_reduce, square_vectors]
    rounded = [matrix.astype(jnp.bfloat16).astype(jnp.float32) for matrix in masters]
    result, pullback = jax.vjp(forward, inputs.astype(jnp.float32), rounded[0], rounded[1], rounded[2], rounded[3], rounded[4])
    pulled = pullback(cotangent.astype(jnp.float32))
    devices = N_DP * N_ZERO
    grads = [gradient / devices for gradient in pulled[1:]]
    weight_norms = []
    step_norms = []
    new_masters = []
    firsts = []
    seconds = []
    for matrix_index in range(4):
        first_new, second_new, direction = lamb_moments(grads[matrix_index], moments[matrix_index], squares[matrix_index])
        direction = direction + weight_decay * masters[matrix_index]
        weight_norm = jnp.sqrt(jnp.sum(masters[matrix_index] * masters[matrix_index]))
        step_norm = jnp.sqrt(jnp.sum(direction * direction))
        new_masters.append(masters[matrix_index] - matrix_rate * (weight_norm / step_norm) * direction)
        weight_norms.append(weight_norm)
        step_norms.append(step_norm)
        firsts.append(first_new)
        seconds.append(second_new)
    first_new, second_new, direction = lamb_moments(grads[4], moments[4], squares[4])
    new_masters.append(masters[4] - vector_rate * direction)
    firsts.append(first_new)
    seconds.append(second_new)
    copies = [matrix.astype(jnp.bfloat16) for matrix in new_masters]
    norm_values = jnp.stack(weight_norms + step_norms)
    return (result.astype(jnp.bfloat16), pulled[0], grads[0], grads[1], grads[2], grads[3], grads[4], new_masters[0], new_masters[1], new_masters[2], new_masters[3], new_masters[4], firsts[0], firsts[1], firsts[2], firsts[3], firsts[4], seconds[0], seconds[1], seconds[2], seconds[3], seconds[4], copies[0], copies[1], copies[2], copies[3], copies[4], norm_values)
```

```python
import functools

import jax
import jax.numpy as jnp
from jax import lax
from jax.experimental import pallas as pl
from jax.experimental.pallas import tpu as pltpu
from jax.sharding import PartitionSpec as P

HD = 64
FRAME = 196
STEP = 4
BLK = 96

norm_eps = 1e-06
adam_eps = 1e-06
decay_rate = 0.5
weight_decay = 0.01
matrix_rate = 0.5
vector_rate = 0.1
BF = jnp.bfloat16
F32 = jnp.float32
VM = pl.BlockSpec(memory_space=pltpu.VMEM)
SM = pl.BlockSpec(memory_space=pltpu.SMEM)
HB = pl.BlockSpec(memory_space=pl.ANY)
INV_SQRT2 = 0.7071067811865476
INV_SQRT2PI = 0.3989422804014327


def padded_rows(rows):
    return (rows + 15) // 16 * 16


def row_chunks(rows):
    edges = list(range(0, rows, 192))
    if rows - edges[-1] < 96 and len(edges) > 1:
        edges.pop()
    return [(s, (edges[i + 1] if i + 1 < len(edges) else rows) - s) for i, s in enumerate(edges)]


def row_halves(zs):
    return 2 if zs == 2 else 1


def dot_nn(a, b):
    return lax.dot_general(a, b, (((1,), (0,)), ((), ())), preferred_element_type=F32)


def dot_nt(a, b):
    return lax.dot_general(a, b, (((1,), (1,)), ((), ())), preferred_element_type=F32)


def dot_tn(a, b):
    return lax.dot_general(a, b, (((0,), (0,)), ((), ())), preferred_element_type=F32)


def stats(v):
    mean = jnp.mean(v, axis=-1, keepdims=True)
    c = v - mean
    r = lax.rsqrt(jnp.mean(c * c, axis=-1, keepdims=True) + norm_eps)
    return c * r, r


def piece_copies(own_ref, pieces, w_ref, sems, width):
    own_rows = width // len(pieces)
    copies = []
    for col, (first, count) in enumerate(((0, 3 * width), (3 * width, width))):
        cols = pl.ds(first, count)
        for kk, piece in enumerate(pieces):
            rws = pl.ds(pl.multiple_of(own_ref[kk] * own_rows, own_rows), own_rows)
            copies.append(
                pltpu.make_async_copy(
                    piece.at[pl.ds(0, own_rows), cols], w_ref.at[rws, cols], sems.at[col, kk]
                )
            )
    return copies[: len(pieces)], copies[len(pieces) :]


def forward_kernel(zs, own_ref, x_ref, vec_ref, *refs):
    pieces = refs[:zs]
    a_ref, j_ref, o_ref, h_ref, b_ref, w_ref, sems = refs[zs:]
    rows, width = x_ref.shape
    joint_in, merge_in = piece_copies(own_ref, pieces, w_ref, sems, width)
    for copy in joint_in + merge_in:
        copy.start()
    pad = a_ref.shape[0]
    frames = rows // FRAME
    heads = width // HD
    win = (FRAME + 12 + 15) // 16 * 16
    scale = HD ** (-0.5)
    tail = pad - 16
    a_ref[tail:pad] = jnp.zeros((16, width), BF)
    o_ref[tail:pad] = jnp.zeros((16, width), BF)
    for s, n in row_chunks(rows):
        norm, _ = stats(x_ref[s : s + n].astype(F32))
        a_ref[s : s + n] = (norm * (1.0 + vec_ref[0:1]) + vec_ref[1:2]).astype(BF)
    for copy in joint_in:
        copy.wait()
    step = 256

    def joint_cols(c, _):
        cols = pl.ds(pl.multiple_of(c * step, step), step)
        per = width // step
        which = c // per
        lane = pl.ds(pl.multiple_of((c % per) * step, step), step)
        row = jnp.where(which == 0, vec_ref[2:3, lane], jnp.where(which == 2, vec_ref[3:4, lane], 0.0))
        j_ref[:, cols] = (dot_nn(a_ref[...], w_ref[:, cols]) + row).astype(BF)
        return 0

    lax.fori_loop(0, 3 * width // step, joint_cols, 0)
    key_at = lax.broadcasted_iota(jnp.int32, (win, win), 1)
    row_at = lax.broadcasted_iota(jnp.int32, (win, 2 * HD), 0)
    low = lax.broadcasted_iota(jnp.int32, (win, 2 * HD), 1) < HD

    def frame_body(f, _):
        start = pl.multiple_of((f * FRAME) // 16 * 16, 16)
        off = f * FRAME - start
        rws = pl.ds(start, win)
        keep = (key_at >= off) & (key_at < off + FRAME)
        rkeep = (row_at >= off) & (row_at < off + FRAME)
        for p in range(heads // 2):
            q2 = j_ref[rws, 2 * HD * p : 2 * HD * (p + 1)]
            k2 = j_ref[rws, width + 2 * HD * p : width + 2 * HD * (p + 1)]
            v2 = j_ref[rws, 2 * width + 2 * HD * p : 2 * width + 2 * HD * (p + 1)]
            parts = []
            for side in range(2):
                qs = jnp.where(low if side == 0 else jnp.logical_not(low), q2, jnp.zeros_like(q2))
                sc = jnp.where(keep, dot_nt(qs, k2) * scale, -1e30)
                e = jnp.exp(sc - jnp.max(sc, axis=-1, keepdims=True))
                pb = (e / jnp.sum(e, axis=-1, keepdims=True)).astype(BF)
                parts.append(dot_nn(pb, v2))
            o2 = jnp.where(low, parts[0], parts[1])
            sl = slice(2 * HD * p, 2 * HD * (p + 1))
            o_ref[rws, sl] = jnp.where(rkeep, o2, o_ref[rws, sl].astype(F32)).astype(BF)
        return 0

    lax.fori_loop(0, frames, frame_body, 0)
    for copy in merge_in:
        copy.wait()
    for s, n in row_chunks(rows):
        m = n if s + n < rows else pad - s
        hv = dot_nn(o_ref[s : s + m], w_ref[:, 3 * width :]) + vec_ref[4:5]
        hv = hv[:n] + x_ref[s : s + n].astype(F32)
        norm, _ = stats(hv)
        h_ref[s : s + n] = hv
        bv = (norm * (1.0 + vec_ref[5:6]) + vec_ref[6:7]).astype(BF)
        if m != n:
            h_ref[tail:pad] = jnp.zeros((16, width), F32)
            b_ref[tail:pad] = jnp.zeros((16, width), BF)
            h_ref[s : s + n] = hv
        b_ref[s : s + n] = bv


def forward_call(owners, x, vec, pieces):
    rows, width = x.shape
    pad = padded_rows(rows)
    zs = len(pieces)
    return pl.pallas_call(
        functools.partial(forward_kernel, zs),
        out_shape=(
            jax.ShapeDtypeStruct((pad, width), BF),
            jax.ShapeDtypeStruct((pad, 3 * width), BF),
            jax.ShapeDtypeStruct((pad, width), BF),
            jax.ShapeDtypeStruct((pad, width), F32),
            jax.ShapeDtypeStruct((pad, width), BF),
        ),
        in_specs=[SM, VM, VM] + [HB] * zs,
        out_specs=(VM,) * 5,
        scratch_shapes=[pltpu.VMEM((width, 4 * width), BF), pltpu.SemaphoreType.DMA((2, zs))],
        cost_estimate=pl.CostEstimate(flops=10**10, bytes_accessed=6 * 10**7, transcendentals=10**6),
        compiler_params=pltpu.CompilerParams(vmem_limit_bytes=56 << 20),
        name="forward_attention",
    )(owners, x, vec, *pieces)


def gelu_parts(u):
    phi = 0.5 * (1.0 + lax.erf(u * INV_SQRT2))
    return u * phi, phi + u * (jnp.exp(u * u * -0.5) * INV_SQRT2PI)


def ffn_kernel(first, last, zs, tiles, own_ref, slot_ref, *refs):
    refs = list(refs)
    b_ref, e_ref = refs[:2]
    we_in = refs[2 : 2 + zs]
    wr_in = refs[2 + zs : 2 + 2 * zs]
    bu_ref, vec_ref = refs[2 + 2 * zs : 4 + 2 * zs]
    refs = refs[4 + 2 * zs :]
    h_ref = refs.pop(0) if last else None
    acc_in, db_in = (None, None) if first else (refs.pop(0), refs.pop(0))
    g_refs = [refs.pop(0) for _ in range(zs)]
    bug_ref = refs.pop(0)
    if last:
        out_ref, dh_ref, dz_ref, sums_ref = [refs.pop(0) for _ in range(4)]
        acc_ref, db_ref = None, None
    else:
        acc_ref, db_ref = refs.pop(0), refs.pop(0)
    es_ref, bt_ref, gs_ref, du_ref, we_ref, wr_ref = refs[:6]
    if last:
        acc_ref, db_ref = refs[6:8]
    rows, width = e_ref.shape
    pad = b_ref.shape[0]
    tf = we_ref.shape[1]
    k, t = pl.program_id(0), pl.program_id(1)
    begin = jnp.logical_and(k == 0, t == 0)
    own_rows = width // zs
    per_owner = tf * tiles
    nh = row_halves(zs)
    nwr = per_owner // BLK
    rbn = own_rows // BLK
    nblk = nwr + (per_owner * zs // width) * rbn
    chunk = [(0, 256), (256, 256), (512, 256), (768, pad - 768)] if pad == 992 else [(0, pad)]

    @pl.when(begin)
    def _():
        es_ref[pad - 16 : pad] = jnp.zeros((16, width), BF)
        es_ref[0:rows] = e_ref[...]
        for c in range(0, width, 256):
            bt_ref[c : c + 256, :] = b_ref[:, c : c + 256].T
        if not first:
            acc_ref[...] = acc_in[...]
            db_ref[...] = db_in[...]
        else:
            acc_ref[...] = jnp.zeros_like(acc_ref)
            db_ref[...] = jnp.zeros_like(db_ref)

    for kk in range(zs):
        rws = pl.ds(pl.multiple_of(own_ref[kk] * own_rows, own_rows), own_rows)
        we_ref[rws, :] = we_in[kk][...]

        @pl.when(k == kk)
        def _(kk=kk):
            wr_ref[...] = wr_in[kk][...]

    total = jnp.zeros((1, tf), F32)
    for s, n in chunk:
        u = dot_nn(b_ref[s : s + n], we_ref[...]) + bu_ref[...]
        g, d = gelu_parts(u)
        gs_ref[s : s + n] = g.astype(BF)
        du = (dot_nt(es_ref[s : s + n], wr_ref[...]) * d).astype(BF)
        du_ref[s : s + n] = du
        total = total + jnp.sum(du.astype(F32), axis=0, keepdims=True)
    owner = own_ref[k]
    bug_ref[pl.ds(owner, 1), pl.ds(pl.multiple_of(t * tf, 128), tf)] = total
    acc_ref[...] += dot_nn(gs_ref[...], wr_ref[...])
    db_ref[...] += dot_nt(du_ref[...], we_ref[...])
    gwr = dot_tn(gs_ref[...], es_ref[...]).astype(BF)
    for i in range(tf // BLK):
        for kk in range(zs):
            @pl.when(k == kk)
            def _(kk=kk, i=i):
                row = t * (tf // BLK) + i
                slot = slot_ref[kk * nblk + row // (nwr // nh) * (nblk // nh) + row % (nwr // nh)]
                g_refs[kk][pl.ds(pl.multiple_of(slot * BLK, BLK), BLK), :] = gwr[i * BLK : (i + 1) * BLK]
    col = owner * per_owner + t * tf
    cb = col // width
    lane = pl.ds(pl.multiple_of(col % width, 128), tf)
    for kk in range(zs):
        rws = pl.ds(pl.multiple_of(own_ref[kk] * own_rows, own_rows), own_rows)
        gwe = dot_nn(bt_ref[rws, :], du_ref[...]).astype(BF)
        for i in range(rbn):
            part = rbn // nh
            slot = slot_ref[kk * nblk + i // part * (nblk // nh) + nwr // nh + cb * part + i % part]
            g_refs[kk][pl.ds(pl.multiple_of(slot * BLK, BLK), BLK), lane] = gwe[i * BLK : (i + 1) * BLK]

    if last:
        @pl.when(jnp.logical_and(k == zs - 1, t == tiles - 1))
        def _():
            da = jnp.zeros((1, width), F32)
            dc = jnp.zeros((1, width), F32)
            de = jnp.zeros((1, width), F32)
            for s, n in chunk:
                hv = h_ref[s : s + n]
                norm, r = stats(hv)
                db = db_ref[s : s + n]
                da = da + jnp.sum(db * norm, axis=0, keepdims=True)
                dc = dc + jnp.sum(db, axis=0, keepdims=True)
                g = db * (1.0 + vec_ref[5:6])
                ev = es_ref[s : s + n].astype(F32)
                de = de + jnp.sum(ev, axis=0, keepdims=True)
                dh = ev + r * (
                    g - jnp.mean(g, axis=-1, keepdims=True) - norm * jnp.mean(g * norm, axis=-1, keepdims=True)
                )
                dh_ref[s : s + n] = dh
                dz_ref[s : s + n] = dh.astype(BF)
                ov = (hv + (acc_ref[s : s + n] + vec_ref[11:12])).astype(BF)
                m = min(n, rows - s)
                out_ref[s : s + m] = ov[:m]
            sums_ref[0:1] = da
            sums_ref[1:2] = dc
            sums_ref[2:3] = de


def ffn_call(first, last, half, halves, tf, owners, slots, b, e, we, wr, bu, vec, h=None, acc=None, db=None):
    zs = owners.shape[0]
    pad, width = b.shape
    rows = e.shape[0]
    ff = we[0].shape[1]
    per = ff // zs // halves
    tiles = per // tf
    nrow = per + per * zs // width * (width // zs)

    def ffcol(k, t, own, sl):
        return own[k] * (halves * tiles) + half * tiles + t

    def wr_row(kk, k, t, own, sl):
        tile = jnp.where(k < kk, 0, jnp.where(k > kk, tiles - 1, t))
        return half * tiles + tile, 0

    whole = lambda shape: pl.BlockSpec(shape, lambda k, t, own, sl: (0, 0))
    in_specs = [
        whole((pad, width)),
        whole((rows, width)),
        *[pl.BlockSpec((width // zs, tf), lambda k, t, own, sl: (0, ffcol(k, t, own, sl)))] * zs,
        *[pl.BlockSpec((tf, width), functools.partial(wr_row, kk)) for kk in range(zs)],
        pl.BlockSpec((1, tf), lambda k, t, own, sl: (0, ffcol(k, t, own, sl))),
        whole(vec.shape),
    ]
    args = [b, e, *we, *wr, bu, vec]
    if last:
        in_specs.append(whole((pad, width)))
        args.append(h)
    if not first:
        in_specs += [whole((pad, width))] * 2
        args += [acc, db]
    outs = [jax.ShapeDtypeStruct((nrow, width), BF)] * zs + [jax.ShapeDtypeStruct((zs, per), F32)]
    scratch = [
        pltpu.VMEM((pad, width), BF),
        pltpu.VMEM((width, pad), BF),
        pltpu.VMEM((pad, tf), BF),
        pltpu.VMEM((pad, tf), BF),
        pltpu.VMEM((width, tf), BF),
        pltpu.VMEM((tf, width), BF),
    ]
    if last:
        outs += [
            jax.ShapeDtypeStruct((rows, width), BF),
            jax.ShapeDtypeStruct((pad, width), F32),
            jax.ShapeDtypeStruct((pad, width), BF),
            jax.ShapeDtypeStruct((8, width), F32),
        ]
        scratch += [pltpu.VMEM((pad, width), F32)] * 2
    else:
        outs += [jax.ShapeDtypeStruct((pad, width), F32)] * 2
    return pl.pallas_call(
        functools.partial(ffn_kernel, first, last, zs, tiles),
        out_shape=tuple(outs),
        grid_spec=pltpu.PrefetchScalarGridSpec(
            num_scalar_prefetch=2,
            grid=(zs, tiles),
            in_specs=in_specs,
            out_specs=tuple(whole(o.shape) for o in outs),
            scratch_shapes=scratch,
        ),
        cost_estimate=pl.CostEstimate(flops=15 * 10**9, bytes_accessed=8 * 10**7, transcendentals=10**6),
        compiler_params=pltpu.CompilerParams(vmem_limit_bytes=60 << 20),
        name="ffn",
    )(owners, slots, *args)


def first_frames(frames):
    return (frames + 1) // 2


def attend_back(lo, hi, base, j_ref, do_ref, dj_ref, dj_base, width):
    win = (FRAME + 12 + 15) // 16 * 16
    scale = HD ** (-0.5)
    key_at = lax.broadcasted_iota(jnp.int32, (win, win), 0)
    qry_at = lax.broadcasted_iota(jnp.int32, (win, win), 1)
    low_side = lax.broadcasted_iota(jnp.int32, (win, 2 * HD), 1) < HD

    def frame_body(f, _):
        start = (f * FRAME) // 16 * 16
        off = f * FRAME - start
        rws = pl.ds(pl.multiple_of(start - base, 16), win)
        drws = pl.ds(pl.multiple_of(start - dj_base, 16), win)
        kkeep = (key_at >= off) & (key_at < off + FRAME)
        keep = kkeep & (qry_at >= off) & (qry_at < off + FRAME)
        for p in range(width // HD // 2):
            sl = [slice(w * width + 2 * HD * p, w * width + 2 * HD * (p + 1)) for w in range(3)]
            q2, k2, v2 = (j_ref[rws, sl[w]] for w in range(3))
            do2 = do_ref[rws, sl[0]]
            res = []
            for side in range(2):
                m = low_side if side == 0 else jnp.logical_not(low_side)
                zero = jnp.zeros_like(k2)
                sc = jnp.where(kkeep, dot_nt(jnp.where(m, k2, zero), q2) * scale, -1e30)
                e = jnp.exp(sc - jnp.max(sc, axis=0, keepdims=True))
                pt = jnp.where(keep, e / jnp.sum(e, axis=0, keepdims=True), 0.0)
                dp = dot_nt(jnp.where(m, v2, zero), do2)
                ds = (pt * (dp - jnp.sum(pt * dp, axis=0, keepdims=True))).astype(BF)
                res.append((dot_tn(ds, k2) * scale, dot_nn(ds, q2) * scale, dot_nn(pt.astype(BF), do2)))
            for w in range(3):
                val = jnp.where(low_side, res[0][w], res[1][w])
                dj_ref[drws, sl[w]] = (dj_ref[drws, sl[w]].astype(F32) + val).astype(BF)
        return 0

    lax.fori_loop(lo, hi, frame_body, 0)


def merge_copies(own_ref, pieces, w_ref, sems, width, first, count):
    own_rows = width // len(pieces)
    copies = []
    for kk, piece in enumerate(pieces):
        rws = pl.ds(pl.multiple_of(own_ref[kk] * own_rows, own_rows), own_rows)
        copies.append(
            pltpu.make_async_copy(piece.at[pl.ds(0, own_rows), pl.ds(first, count)], w_ref.at[rws, :], sems.at[kk])
        )
    return copies


def back_first_kernel(zs, frames, own_ref, j_ref, dz_ref, *refs):
    pieces = refs[:zs]
    dj_ref, do_ref, w_ref, sems = refs[zs:]
    width = dz_ref.shape[1]
    copies = merge_copies(own_ref, pieces, w_ref, sems, width, 3 * width, width)
    for copy in copies:
        copy.start()
    dj_ref[...] = jnp.zeros_like(dj_ref)
    for copy in copies:
        copy.wait()
    do_ref[...] = dot_nt(dz_ref[...], w_ref[...]).astype(BF)
    attend_back(0, first_frames(frames), 0, j_ref, do_ref, dj_ref, 0, width)


def back_first_call(owners, j, dz, pieces, frames):
    zs = len(pieces)
    width = dz.shape[1]
    last = first_frames(frames) - 1
    rows = (last * FRAME) // 16 * 16 + (FRAME + 12 + 15) // 16 * 16
    return pl.pallas_call(
        functools.partial(back_first_kernel, zs, frames),
        grid=(1,),
        out_shape=jax.ShapeDtypeStruct((rows, 3 * width), BF),
        in_specs=[
            SM,
            pl.BlockSpec((rows, 3 * width), lambda i: (0, 0)),
            pl.BlockSpec((rows, width), lambda i: (0, 0)),
        ]
        + [HB] * zs,
        out_specs=pl.BlockSpec((rows, 3 * width), lambda i: (0, 0)),
        scratch_shapes=[
            pltpu.VMEM((rows, width), BF),
            pltpu.VMEM((width, width), BF),
            pltpu.SemaphoreType.DMA((zs,)),
        ],
        cost_estimate=pl.CostEstimate(flops=10**10, bytes_accessed=7 * 10**7, transcendentals=10**6),
        compiler_params=pltpu.CompilerParams(vmem_limit_bytes=60 << 20),
        name="back_first",
    )(owners, j, dz, *pieces)


def back_second_kernel(zs, frames, own_ref, slot_ref, a_ref, o_ref, dz_ref, j_hbm, djp_hbm, *refs):
    pieces = refs[:zs]
    g_refs = refs[zs : 2 * zs]
    dj_ref, sums_ref, j_ref, do_ref, t_ref, w_ref, sems, more = refs[2 * zs :]
    pad, width = a_ref.shape
    done = djp_hbm.shape[0]
    base = (first_frames(frames) * FRAME) // 16 * 16
    own_rows = width // zs
    rbn = own_rows // BLK
    copies = merge_copies(own_ref, pieces, w_ref, sems, width, 3 * width, width)
    copies.append(pltpu.make_async_copy(j_hbm.at[pl.ds(base, pad - base), :], j_ref, more.at[0]))
    earlier = pltpu.make_async_copy(djp_hbm, dj_ref.at[pl.ds(0, done), :], more.at[1])
    for copy in copies:
        copy.start()
    earlier.start()
    dj_ref[done:pad] = jnp.zeros((pad - done, 3 * width), BF)
    sums_ref[...] = jnp.zeros_like(sums_ref)
    for c in range(0, width, 256):
        t_ref[c : c + 256, :] = o_ref[:, c : c + 256].T
    sums_ref[0:1] = jnp.sum(dz_ref[...].astype(F32), axis=0, keepdims=True)
    part = rbn // row_halves(zs)

    def put(kk, region, i, val):
        slot = slot_ref[kk * 4 * rbn + i // part * (4 * part) + region * part + i % part]
        g_refs[kk][pl.ds(pl.multiple_of(slot * BLK, BLK), BLK), :] = val

    for kk in range(zs):
        rws = pl.ds(pl.multiple_of(own_ref[kk] * own_rows, own_rows), own_rows)
        gm = dot_nn(t_ref[rws, :], dz_ref[...]).astype(BF)
        for i in range(rbn):
            put(kk, 0, i, gm[i * BLK : (i + 1) * BLK])
    for copy in copies:
        copy.wait()
    do_ref[...] = dot_nt(dz_ref[base:pad], w_ref[...]).astype(BF)
    earlier.wait()
    attend_back(first_frames(frames), frames, base, j_ref, do_ref, dj_ref, 0, width)
    for c in range(0, width, 256):
        t_ref[c : c + 256, :] = a_ref[:, c : c + 256].T
    for w in range(3):
        cols = slice(w * width, (w + 1) * width)
        if w != 1:
            row = 1 if w == 0 else 2
            sums_ref[row : row + 1] = jnp.sum(dj_ref[:, cols].astype(F32), axis=0, keepdims=True)
        for kk in range(zs):
            rws = pl.ds(pl.multiple_of(own_ref[kk] * own_rows, own_rows), own_rows)
            gj = dot_nn(t_ref[rws, :], dj_ref[:, cols]).astype(BF)
            for i in range(rbn):
                put(kk, 1 + w, i, gj[i * BLK : (i + 1) * BLK])


def back_second_call(owners, slots, a, o, dz, j, dj_part, pieces, frames):
    zs = len(pieces)
    pad, width = a.shape
    base = (first_frames(frames) * FRAME) // 16 * 16
    nrow = 4 * (width // zs)
    return pl.pallas_call(
        functools.partial(back_second_kernel, zs, frames),
        out_shape=(jax.ShapeDtypeStruct((nrow, width), BF),) * zs
        + (jax.ShapeDtypeStruct((pad, 3 * width), BF), jax.ShapeDtypeStruct((8, width), F32)),
        in_specs=[SM] * 2 + [VM] * 3 + [HB] * (2 + zs),
        out_specs=(VM,) * (zs + 2),
        scratch_shapes=[
            pltpu.VMEM((pad - base, 3 * width), BF),
            pltpu.VMEM((pad - base, width), BF),
            pltpu.VMEM((width, pad), BF),
            pltpu.VMEM((width, width), BF),
            pltpu.SemaphoreType.DMA((zs,)),
            pltpu.SemaphoreType.DMA((2,)),
        ],
        cost_estimate=pl.CostEstimate(flops=10**10, bytes_accessed=6 * 10**7, transcendentals=10**6),
        compiler_params=pltpu.CompilerParams(vmem_limit_bytes=60 << 20),
        name="back_second",
    )(owners, slots, a, o, dz, j, dj_part, *pieces)


def back_last_kernel(zs, own_ref, x_ref, dh_ref, dj_ref, vec_ref, *refs):
    pieces = refs[:zs]
    ig_ref, sums_ref, w_ref, sems = refs[zs:]
    rows, width = x_ref.shape
    pad = dj_ref.shape[0]
    copies = merge_copies(own_ref, pieces, w_ref, sems, width, 0, 3 * width)
    for copy in copies:
        copy.start()
    sums_ref[...] = jnp.zeros_like(sums_ref)
    for copy in copies:
        copy.wait()
    chunk = [(0, 256), (256, 256), (512, 256), (768, pad - 768)] if pad == 992 else [(0, pad)]
    da = jnp.zeros((1, width), F32)
    dc = jnp.zeros((1, width), F32)
    for s, n in chunk:
        m = min(n, rows - s)
        dv = dot_nt(dj_ref[s : s + n], w_ref[...])[:m]
        norm, r = stats(x_ref[s : s + m].astype(F32))
        da = da + jnp.sum(dv * norm, axis=0, keepdims=True)
        dc = dc + jnp.sum(dv, axis=0, keepdims=True)
        g = dv * (1.0 + vec_ref[0:1])
        ig_ref[s : s + m] = dh_ref[s : s + m] + r * (
            g - jnp.mean(g, axis=-1, keepdims=True) - norm * jnp.mean(g * norm, axis=-1, keepdims=True)
        )
    sums_ref[0:1] = da
    sums_ref[1:2] = dc


def back_last_call(owners, x, dh, dj, vec, pieces):
    zs = len(pieces)
    rows, width = x.shape
    return pl.pallas_call(
        functools.partial(back_last_kernel, zs),
        out_shape=(jax.ShapeDtypeStruct((rows, width), F32), jax.ShapeDtypeStruct((8, width), F32)),
        in_specs=[SM] + [VM] * 4 + [HB] * zs,
        out_specs=(VM,) * 2,
        scratch_shapes=[pltpu.VMEM((width, 3 * width), BF), pltpu.SemaphoreType.DMA((zs,))],
        cost_estimate=pl.CostEstimate(flops=4 * 10**9, bytes_accessed=3 * 10**7, transcendentals=0),
        compiler_params=pltpu.CompilerParams(vmem_limit_bytes=60 << 20),
        name="back_last",
    )(owners, x, dh, dj, vec, *pieces)


def lamb_math(g, w, m, s, devices):
    scale = 1.0 / (1.0 - decay_rate**STEP)
    g = g.astype(F32) * (1.0 / devices)
    first = decay_rate * m + (1.0 - decay_rate) * g
    second = decay_rate * s + (1.0 - decay_rate) * g * g
    ratio = (first * scale) / (jnp.sqrt(second * scale) + adam_eps)
    return g, first, second, ratio


def norms_kernel(spots, rows, devices, meta_ref, *refs):
    out_ref = refs[-1]
    lane = meta_ref[0]
    out_ref[...] = jnp.zeros_like(out_ref)
    at = 0
    for regions, places in zip(spots, rows):
        y = refs[at][...]
        at += 1
        for inside, row in zip(regions, places):
            w, m, s = (refs[at + k][...] for k in range(3))
            at += 3
            upd = lamb_math(y, w, m, s, devices)[3] + weight_decay * w
            use = jnp.where(inside(lane), 1.0, 0.0)
            out_ref[row : row + 1] += jnp.full((1, 128), jnp.sum(w * w) * use)
            out_ref[row + 4 : row + 5] += jnp.full((1, 128), jnp.sum(upd * upd) * use)


def norms_call(meta, shards, regions, rows, devices):
    width = shards[0].shape[1]
    specs, args = [], []
    for shard, parts in zip(shards, regions):
        specs.append(pl.BlockSpec((BLK, width), lambda i, meta: (0, 0)))
        args.append(shard)
        for _, place, mat in parts:
            specs += [pl.BlockSpec((BLK, width), lambda i, meta, place=place: place(meta[0]))] * 3
            args += list(mat)
    spots = [[part[0] for part in parts] for parts in regions]
    return pl.pallas_call(
        functools.partial(norms_kernel, spots, rows, devices),
        out_shape=jax.ShapeDtypeStruct((8, 128), F32),
        grid_spec=pltpu.PrefetchScalarGridSpec(
            num_scalar_prefetch=1,
            grid=(1,),
            in_specs=specs,
            out_specs=pl.BlockSpec((8, 128), lambda i, meta: (0, 0)),
        ),
        cost_estimate=pl.CostEstimate(flops=10**7, bytes_accessed=6 * 10**6, transcendentals=0),
        compiler_params=pltpu.CompilerParams(vmem_limit_bytes=60 << 20),
        name="norms",
    )(meta, *args)


LAMB_IN = 4
LAMB_OUT = 3


def lamb_kernel(counts, places, rows, lead, n_half, devices, n_alias, meta_ref, slot_ref, total_ref, *refs):
    nbh = sum(counts)
    ys = refs[:n_half]
    ins = refs[n_half : n_half + 6]
    outs = refs[n_half + 6 + n_alias : n_half + 16 + n_alias]
    in_buf, y_buf, out_buf, copy_buf, in_sem, y_sem, out_sem = refs[n_half + 16 + n_alias :]
    bs = in_buf.shape[2]
    width = in_buf.shape[3]
    per = bs // BLK
    steps = nbh * n_half
    half_blk = ys[0].shape[0] // BLK

    def where(i):
        rel, q = i // nbh, i % nbh
        return rel, (rel + lead) ^ meta_ref[1], q

    def window(p, half, q):
        row, col = places[p](half, q - (counts[0] if p else 0))
        return pl.ds(pl.multiple_of(row * bs, bs), bs), pl.ds(pl.multiple_of(col * width, width), width)

    def loads(i, start):
        rel, half, q = where(i)
        b = i % LAMB_IN
        for p in range(2):
            @pl.when((q >= counts[0]) == (p == 1))
            def _(p=p):
                at = window(p, half, q)
                for k in range(3):
                    copy = pltpu.make_async_copy(ins[3 * p + k].at[at], in_buf.at[b, k], in_sem.at[b, k])
                    copy.start() if start else copy.wait()
        for r in range(n_half):
            @pl.when(rel == r)
            def _(r=r):
                for k in range(per):
                    slot = slot_ref[half * half_blk + q * per + k] - (r + lead) * half_blk
                    copy = pltpu.make_async_copy(
                        ys[r].at[pl.ds(pl.multiple_of(slot * BLK, BLK), BLK), :],
                        y_buf.at[b, pl.ds(k * BLK, BLK)], y_sem.at[b, k],
                    )
                    copy.start() if start else copy.wait()

    def stores(i, start):
        _, half, q = where(i)
        b = i % LAMB_OUT
        for p in range(2):
            @pl.when((q >= counts[0]) == (p == 1))
            def _(p=p):
                at = window(p, half, q)
                for k in range(5):
                    src = copy_buf.at[b] if k == 4 else out_buf.at[b, k]
                    copy = pltpu.make_async_copy(src, outs[5 * p + k].at[at], out_sem.at[b, k])
                    copy.start() if start else copy.wait()

    for i in range(LAMB_IN - 1):
        loads(jnp.int32(i), True)

    def step(i, _):
        b, o = i % LAMB_IN, i % LAMB_OUT

        @pl.when(i + LAMB_IN - 1 < steps)
        def _():
            loads(i + LAMB_IN - 1, True)

        loads(i, False)

        @pl.when(i >= LAMB_OUT)
        def _():
            stores(i - LAMB_OUT, False)

        _, _, q = where(i)
        row = jnp.where(q >= counts[0], rows[1], rows[0])
        trust = jnp.sqrt(total_ref[pl.ds(row, 1), 0:1]) / jnp.sqrt(total_ref[pl.ds(row + 4, 1), 0:1])

        def chunk(c, _):
            at = pl.ds(pl.multiple_of(c * 32, 32), 32)
            w = in_buf[b, 0, at]
            g, first, second, ratio = lamb_math(y_buf[b, at], w, in_buf[b, 1, at], in_buf[b, 2, at], devices)
            weight = w - (matrix_rate * trust) * (ratio + weight_decay * w)
            out_buf[o, 0, at] = g
            out_buf[o, 1, at] = weight
            out_buf[o, 2, at] = first
            out_buf[o, 3, at] = second
            copy_buf[o, at] = weight.astype(BF)
            return 0

        lax.fori_loop(0, bs // 32, chunk, 0)
        stores(i, True)
        return 0

    lax.fori_loop(0, steps, step, 0)
    for i in range(max(0, steps - LAMB_OUT), steps):
        stores(jnp.int32(i), False)


def lamb_call(meta, slots, ys, lead, total, counts, places, rows, mats, bs, devices, before):
    width = ys[0].shape[1]
    flat = [array for mat in mats for array in mat]
    dtypes = (F32, F32, F32, F32, BF)
    out_shape = tuple(jax.ShapeDtypeStruct(mat[0].shape, dt) for mat in mats for dt in dtypes)
    aliased = list(before) if before is not None else []
    aliases = {3 + len(ys) + len(flat) + i: i for i in range(len(aliased))}
    return pl.pallas_call(
        functools.partial(lamb_kernel, counts, places, rows, lead, len(ys), devices, len(aliased)),
        out_shape=out_shape,
        in_specs=[SM, SM, VM] + [HB] * (len(ys) + len(flat) + len(aliased)),
        out_specs=(HB,) * len(out_shape),
        scratch_shapes=[
            pltpu.VMEM((LAMB_IN, 3, bs, width), F32),
            pltpu.VMEM((LAMB_IN, bs, width), BF),
            pltpu.VMEM((LAMB_OUT, 4, bs, width), F32),
            pltpu.VMEM((LAMB_OUT, bs, width), BF),
            pltpu.SemaphoreType.DMA((LAMB_IN, 3)),
            pltpu.SemaphoreType.DMA((LAMB_IN, bs // BLK)),
            pltpu.SemaphoreType.DMA((LAMB_OUT, 5)),
        ],
        input_output_aliases=aliases,
        cost_estimate=pl.CostEstimate(flops=10**8, bytes_accessed=4 * 10**7, transcendentals=0),
        compiler_params=pltpu.CompilerParams(vmem_limit_bytes=60 << 20),
        name="lamb",
    )(meta, slots, total, *ys, *flat, *aliased)


def bits_of(n):
    return n.bit_length() - 1


class Order:

    def __init__(self):
        self.last = None

    def run(self, fn, *args):
        if self.last is not None:
            args, _ = lax.optimization_barrier((args, self.last))
        out = fn(*args)
        leaves = jax.tree.leaves(out)
        self.last = leaves[0]
        return out


def add_bf(a, b):
    return (a.astype(F32) + b.astype(F32)).astype(BF)


def add_split(a, b):
    half = a.shape[0] // 2
    return add_bf(a[:half], b[:half]), add_bf(a[half:], b[half:])


class Exchange:

    def __init__(self, ds):
        self.ds = ds
        self.z, self.d = lax.axis_index("zero"), lax.axis_index("dp")
        self.stages = bits_of(ds)
        order = list(range(self.stages))
        self.orders = [order, [1, 0] + order[2:]]
        lanes = [
            sum((((self.d >> bit) & 1) << (self.stages - 1 - k)) for k, bit in enumerate(order)) for order in self.orders
        ]
        self.mine = jnp.where(self.z == 0, lanes[0], lanes[1]).astype(jnp.int32)
        self.other = jnp.where(self.z == 0, lanes[1], lanes[0]).astype(jnp.int32)
        self.owners = jnp.stack([1 - self.z, self.z]).astype(jnp.int32)
        base = jnp.arange(ds, dtype=jnp.int32)
        self.own_slots = base ^ self.mine
        self.slots = jnp.concatenate([base ^ self.other, self.own_slots])
        self.meta = jnp.stack([self.mine, self.mine >> (self.stages - 1)]).astype(jnp.int32)

    def swap(self, a):
        return lax.ppermute(a, "zero", [(0, 1), (1, 0)])

    def hop(self, a, stage):
        pairs = []
        for d in range(self.ds):
            for c in range(2):
                pairs.append((d * 2 + c, (d ^ (1 << self.orders[c][stage])) * 2 + c))
        return lax.ppermute(a, ("dp", "zero"), pairs)


class Chain:

    def __init__(self, ex, parts):
        self.ex, self.mine, self.stage = ex, parts[1], 0
        self.recv = ex.swap(parts[0])

    def reduce(self, order):
        ex = self.ex
        if self.stage == ex.stages:
            self.shard = self.own = order.run(add_bf, self.mine, self.recv)
            self.recv = ex.hop(self.own, ex.stages - 1)
        else:
            self.mine, send = order.run(add_split, self.mine, self.recv)
            self.recv = ex.hop(send, self.stage)
        self.stage += 1

    def gather(self, order):
        ex = self.ex
        self.own = order.run(lambda a, b: jnp.concatenate([a, b], axis=0), self.own, self.recv)
        self.stage += 1
        self.recv = ex.hop(self.own, 2 * ex.stages - self.stage)


    def step(self, order):
        self.reduce(order) if self.stage <= self.ex.stages else self.gather(order)


class Total:

    def __init__(self, ex, mine, theirs):
        self.ex, self.total, self.stage = ex, mine, 0
        self.recv = ex.swap(theirs)

    def step(self, order):
        self.total = order.run(jnp.add, self.total, self.recv)
        if self.stage < self.ex.stages:
            self.recv = self.ex.hop(self.total, self.stage)
        self.stage += 1


PLAN = (
    "2 1 3 v",
    "1 2 v",
    "3 1 2 v",
    "3 2 1 v nf",
    "3 1 2 v f",
    "3 na 1 2 f",
    "3 2 a f",
    "3 f a f L10",
    "3 a L20 a L11 a L21 L30 L31",
)


def lamb_moments(gradient, first_old, second_old):
    correction = 1.0 - decay_rate**STEP
    first_new = decay_rate * first_old + (1.0 - decay_rate) * gradient
    second_new = decay_rate * second_old + (1.0 - decay_rate) * gradient * gradient
    direction = first_new / correction / (jnp.sqrt(second_new / correction) + adam_eps)
    return (first_new, second_new, direction)


def low(v):
    return lax.reduce_precision(v, exponent_bits=8, mantissa_bits=7)


def per_device(
    inputs,
    cotangent,
    master_joint,
    master_merge,
    master_expand,
    master_reduce,
    master_vectors,
    moment_joint,
    moment_merge,
    moment_expand,
    moment_reduce,
    moment_vectors,
    square_joint,
    square_merge,
    square_expand,
    square_reduce,
    square_vectors,
):
    zs = lax.axis_size("zero")
    ds = lax.axis_size("dp")
    devices = zs * ds
    width = inputs.shape[1]
    own_rows = master_joint.shape[0]
    ff = master_expand.shape[1]
    per_owner = ff // zs
    halves = 2 if zs == 2 else 1
    per = per_owner // halves
    tf = min(per, width)
    rbn = own_rows // BLK
    nwr = per // BLK
    ncb = per * zs // width
    fast = zs == 2 and ds & (ds - 1) == 0 and 4 * rbn == ds and nwr + ncb * rbn == ds
    masters = [master_joint, master_merge, master_expand, master_reduce]
    moments = [moment_joint, moment_merge, moment_expand, moment_reduce]
    squares = [square_joint, square_merge, square_expand, square_reduce]
    mats = list(zip(masters, moments, squares))

    if fast:
        ex = Exchange(ds)
        owners, ffn_slots, attn_slots = ex.owners, ex.slots, ex.slots
        pieces = lambda own: [ex.swap(own), own]
    else:
        owners = jnp.arange(zs, dtype=jnp.int32)
        ffn_slots = jnp.tile(jnp.arange(nwr + ncb * rbn, dtype=jnp.int32), zs)
        attn_slots = jnp.tile(jnp.arange(4 * rbn, dtype=jnp.int32), zs)

        def pieces(own):
            full = lax.all_gather(own, "zero", axis=0)
            return [full[i] for i in range(zs)]

    head = jnp.pad(low(master_vectors), ((0, 4), (0, 4 * width - master_vectors.shape[1])))
    attn_own = jnp.concatenate([jnp.concatenate([master_joint, master_merge], axis=1), head], axis=0).astype(BF)
    attn = pieces(attn_own)
    expand = pieces(master_expand.astype(BF))
    reduce = pieces(master_reduce.astype(BF))
    vecs = [piece[own_rows : own_rows + 12, : width // zs].astype(F32) for piece in attn]
    if fast:
        vecs[1] = low(master_vectors)
        vec = jnp.where(ex.z == 0, jnp.concatenate([vecs[1], vecs[0]], 1), jnp.concatenate(vecs, 1))
    else:
        vec = jnp.concatenate(vecs, axis=1)
    bias_up = vec[7:11].reshape(1, ff)

    order = Order()
    normed, joint, mixed, middle, normed_two = order.run(forward_call, owners, inputs, vec, attn)
    carry = ()
    chains = []
    ffn_grads = []
    bias_sums = []
    for half in range(halves):
        last = half == halves - 1
        res = order.run(
            functools.partial(ffn_call, half == 0, last, half, halves, tf),
            owners, ffn_slots, normed_two, cotangent, expand, reduce, bias_up, vec, middle if last else None, *carry,
        )
        if fast:
            chains.append(Chain(ex, res[:zs]))
        ffn_grads.append(list(res[:zs]))
        bias_sums.append(res[zs])
        carry = res[zs + 1 :]
    outputs, middle_grad, merge_grad, ffn_sums = carry
    frames = inputs.shape[0] // FRAME
    if fast:
        chains[0].reduce(order)
    joint_part = order.run(functools.partial(back_first_call, frames=frames), owners, joint, merge_grad, attn)
    if fast:
        chains[1].reduce(order)
        chains[0].reduce(order)
    res = order.run(
        functools.partial(back_second_call, frames=frames),
        owners, attn_slots, normed, mixed, merge_grad, joint, joint_part, attn,
    )
    attn_grads = list(res[:zs])
    joint_grad, attn_sums = res[zs:]
    if fast:
        chains.append(Chain(ex, attn_grads))
    input_grad, last_sums = order.run(back_last_call, owners, inputs, middle_grad, joint_grad, vec, attn)
    rows = jnp.concatenate(
        [
            last_sums[0:2],
            attn_sums[1:3],
            attn_sums[0:1],
            ffn_sums[0:2],
            jnp.stack(bias_sums, axis=1).reshape(ff // width, width),
            ffn_sums[2:3],
        ],
        axis=0,
    )
    own_cols = width // zs
    if fast:
        ffn_one, ffn_two, attn_chain = chains

        def reduce_place(half):
            return lambda lane: (half * nwr + lane // (ds // 2) * (nwr // 2) + jnp.clip(lane % (ds // 2), 0, nwr // 2 - 1), 0)

        def expand_place(half):
            def place(lane):
                q = jnp.clip(lane % (ds // 2) - nwr // 2, 0, ncb * rbn // 2 - 1)
                cb, i = q // (rbn // 2), q % (rbn // 2)
                return lane // (ds // 2) * (rbn // 2) + i, cb * (per_owner // width) + half * (per // width)
            return place

        def joint_place(lane):
            q = jnp.clip(lane % (ds // 2) - rbn // 2, 0, 3 * rbn // 2 - 1)
            return lane // (ds // 2) * (rbn // 2) + q % (rbn // 2), q // (rbn // 2)

        def merge_place(lane):
            return lane // (ds // 2) * (rbn // 2) + jnp.clip(lane % (ds // 2), 0, rbn // 2 - 1), 0

        in_reduce = lambda lane: lane % (ds // 2) < nwr // 2
        in_expand = lambda lane: lane % (ds // 2) >= nwr // 2
        in_merge = lambda lane: lane % (ds // 2) < rbn // 2
        in_joint = lambda lane: lane % (ds // 2) >= rbn // 2
        regions = [
            [(in_merge, merge_place, mats[1]), (in_joint, joint_place, mats[0])],
            [(in_reduce, reduce_place(0), mats[3]), (in_expand, expand_place(0), mats[2])],
            [(in_reduce, reduce_place(1), mats[3]), (in_expand, expand_place(1), mats[2])],
        ]
        bs = 2 * BLK
        count_r = per // bs // 2
        nrb = own_rows // bs // 2

        def lamb_reduce(half):
            return lambda h, q: (half * (per // bs) + h * count_r + q, 0)

        def lamb_expand(half):
            return lambda h, q: (
                h * nrb + q % nrb, q // nrb * (per_owner // width) + half * (per // width)
            )

        lamb_merge = lambda h, q: (h * nrb + q, 0)
        lamb_joint = lambda h, q: (h * nrb + q % nrb, q // nrb)
        mine = jnp.where(ex.z == 0, rows[:, :own_cols], rows[:, own_cols:])
        theirs = jnp.where(ex.z == 0, rows[:, own_cols:], rows[:, :own_cols])
        sums = {"v": Total(ex, mine, theirs)}
        state = {"f": None, "a": None}

        def ffn_lamb(half, lead):
            chain = chains[half]
            state["f"] = order.run(
                lambda meta, slots, y, total, mats, before: lamb_call(
                    meta, slots, [y], lead, total, [count_r, ncb * nrb], [lamb_reduce(half), lamb_expand(half)],
                    [3, 2], mats, bs, devices, before,
                ),
                ex.meta, ex.own_slots, (chain.own, chain.recv)[lead], sums["f"].total, (mats[3], mats[2]), state["f"],
            )

        def attn_lamb(lead):
            state["a"] = order.run(
                lambda meta, slots, y, total, mats, before: lamb_call(
                    meta, slots, [y], lead, total, [nrb, 3 * nrb], [lamb_merge, lamb_joint], [1, 0], mats, bs,
                    devices, before,
                ),
                ex.meta, ex.own_slots, (attn_chain.own, attn_chain.recv)[lead], sums["a"].total, (mats[1], mats[0]),
                state["a"],
            )

        def norms_of(key):
            groups, parts, at = {
                "f": ((ffn_one, ffn_two), regions[1:], [[3, 2]] * 2), "a": ((attn_chain,), regions[:1], [[1, 0]])
            }[key]
            part = order.run(
                lambda meta, *shards: norms_call(meta, shards, parts, at, devices),
                ex.meta, *[chain.shard for chain in groups],
            )
            sums[key] = Total(ex, part, part)

        for word in PLAN:
            for act in word.split():
                kind, rest = act[0], act[1:]
                if kind in "123":
                    chains[int(kind) - 1].step(order)
                elif kind in "vfa":
                    sums[kind].step(order)
                elif kind == "n":
                    norms_of(rest)
                elif kind == "L":
                    lead = int(rest[1])
                    attn_lamb(lead) if rest[0] == "3" else ffn_lamb(int(rest[0]) - 1, lead)
        ffn_out, attn_out = state["f"], state["a"]
        vec_total = sums["v"].total
        norm_values = jnp.sqrt(sums["f"].total[:, 0] + sums["a"].total[:, 0])
        outs = [attn_out[5:10], attn_out[0:5], ffn_out[5:10], ffn_out[0:5]]
    else:
        def summed(parts):
            stack = lax.psum_scatter(jnp.concatenate(parts, axis=0), "zero", scatter_dimension=0, tiled=True)
            stack = lax.psum_scatter(stack, "dp", scatter_dimension=0, tiled=True)
            return lax.all_gather(stack, "dp", axis=0, tiled=True).astype(F32) / devices

        def side_by_side(stack):
            return stack.reshape(-1, own_rows, width).transpose(1, 0, 2).reshape(own_rows, -1)

        ffn = summed(ffn_grads[0])
        attn_sum = summed(attn_grads)
        grads = [
            side_by_side(attn_sum[own_rows:]), attn_sum[:own_rows], side_by_side(ffn[per:]), ffn[:per]
        ]
        blocks = rows.reshape(12, zs, own_cols).transpose(1, 0, 2)
        vec_total = lax.psum(lax.psum_scatter(blocks, "zero", scatter_dimension=0, tiled=True)[0], "dp")
        moved = [lamb_moments(g, m, s) for g, m, s in zip(grads, moments, squares)]
        upds = [move[2] + weight_decay * w for move, w in zip(moved, masters)]
        local = jnp.stack([jnp.sum(w * w) for w in masters] + [jnp.sum(u * u) for u in upds])
        norm_values = jnp.sqrt(lax.psum(local, "zero"))
        outs = []
        for k in range(4):
            weight = masters[k] - matrix_rate * (norm_values[k] / norm_values[k + 4]) * upds[k]
            outs.append((grads[k], weight, moved[k][0], moved[k][1], weight.astype(BF)))

    grad_vec = vec_total / devices
    first_vec, second_vec, vec_direction = lamb_moments(grad_vec, moment_vectors, square_vectors)
    new_vectors = master_vectors - vector_rate * vec_direction
    vector_out = (grad_vec, new_vectors, first_vec, second_vec, new_vectors.astype(BF))
    result = [outputs, input_grad]
    for k in range(5):
        result += [out[k] for out in outs] + [vector_out[k]]
    return (*result, norm_values)


def solution(mesh):
    tokens = P(("dp", "zero"), None)
    matrix = P("zero", None)
    vector = P(None, "zero")
    five = (matrix,) * 4 + (vector,)
    return jax.shard_map(
        per_device,
        mesh=mesh,
        in_specs=(tokens, tokens) + five * 3,
        out_specs=(tokens, tokens) + five * 5 + (P(),),
        check_vma=False,
    )
```

```python
import functools

import jax
import jax.numpy as jnp
from jax import lax
from jax.experimental import pallas as pl
from jax.experimental.pallas import tpu as pltpu
from jax.sharding import PartitionSpec as P

HD = 64
FRAME = 196
STEP = 4
BLK = 96

norm_eps = 1e-06
adam_eps = 1e-06
decay_rate = 0.5
weight_decay = 0.01
matrix_rate = 0.5
vector_rate = 0.1
BF = jnp.bfloat16
F32 = jnp.float32
VM = pl.BlockSpec(memory_space=pltpu.VMEM)
SM = pl.BlockSpec(memory_space=pltpu.SMEM)
HB = pl.BlockSpec(memory_space=pl.ANY)
HEAVY = pl.CostEstimate(flops=5 * 10**10, bytes_accessed=10**8, transcendentals=0)
LIGHT = pl.CostEstimate(flops=1000, bytes_accessed=1000, transcendentals=0)
INV_SQRT2 = 0.7071067811865476
INV_SQRT2PI = 0.3989422804014327


def padded_rows(rows):
    return (rows + 15) // 16 * 16


def row_chunks(rows):
    edges = list(range(0, rows, 192))
    if rows - edges[-1] < 96 and len(edges) > 1:
        edges.pop()
    return [(s, (edges[i + 1] if i + 1 < len(edges) else rows) - s) for i, s in enumerate(edges)]


def row_halves(zs):
    return 2 if zs == 2 else 1


def dot_nn(a, b):
    return lax.dot_general(a, b, (((1,), (0,)), ((), ())), preferred_element_type=F32)


def dot_nt(a, b):
    return lax.dot_general(a, b, (((1,), (1,)), ((), ())), preferred_element_type=F32)


def dot_tn(a, b):
    return lax.dot_general(a, b, (((0,), (0,)), ((), ())), preferred_element_type=F32)


def stats(v):
    mean = jnp.mean(v, axis=-1, keepdims=True)
    c = v - mean
    r = lax.rsqrt(jnp.mean(c * c, axis=-1, keepdims=True) + norm_eps)
    return c * r, r


def piece_copies(own_ref, pieces, w_ref, sems, width):
    own_rows = width // len(pieces)
    copies = []
    for col, (first, count) in enumerate(((0, 3 * width), (3 * width, width))):
        cols = pl.ds(first, count)
        for kk, piece in enumerate(pieces):
            rws = pl.ds(pl.multiple_of(own_ref[kk] * own_rows, own_rows), own_rows)
            copies.append(
                pltpu.make_async_copy(
                    piece.at[pl.ds(0, own_rows), cols], w_ref.at[rws, cols], sems.at[col, kk]
                )
            )
    return copies[: len(pieces)], copies[len(pieces) :]


def forward_kernel(zs, own_ref, x_ref, vec_ref, *refs):
    pieces = refs[:zs]
    a_ref, j_ref, o_ref, h_ref, b_ref, w_ref, sems = refs[zs:]
    rows, width = x_ref.shape
    joint_in, merge_in = piece_copies(own_ref, pieces, w_ref, sems, width)
    for copy in joint_in + merge_in:
        copy.start()
    pad = a_ref.shape[0]
    frames = rows // FRAME
    heads = width // HD
    win = (FRAME + 12 + 15) // 16 * 16
    scale = HD ** (-0.5)
    tail = pad - 16
    a_ref[tail:pad] = jnp.zeros((16, width), BF)
    o_ref[tail:pad] = jnp.zeros((16, width), BF)
    for s, n in row_chunks(rows):
        norm, _ = stats(x_ref[s : s + n].astype(F32))
        a_ref[s : s + n] = (norm * (1.0 + vec_ref[0:1]) + vec_ref[1:2]).astype(BF)
    for copy in joint_in:
        copy.wait()
    step = 256

    def joint_cols(c, _):
        cols = pl.ds(pl.multiple_of(c * step, step), step)
        per = width // step
        which = c // per
        lane = pl.ds(pl.multiple_of((c % per) * step, step), step)
        row = jnp.where(which == 0, vec_ref[2:3, lane], jnp.where(which == 2, vec_ref[3:4, lane], 0.0))
        j_ref[:, cols] = (dot_nn(a_ref[...], w_ref[:, cols]) + row).astype(BF)
        return 0

    lax.fori_loop(0, 3 * width // step, joint_cols, 0)
    key_at = lax.broadcasted_iota(jnp.int32, (win, win), 1)
    row_at = lax.broadcasted_iota(jnp.int32, (win, 2 * HD), 0)
    low = lax.broadcasted_iota(jnp.int32, (win, 2 * HD), 1) < HD

    def frame_body(f, _):
        start = pl.multiple_of((f * FRAME) // 16 * 16, 16)
        off = f * FRAME - start
        rws = pl.ds(start, win)
        keep = (key_at >= off) & (key_at < off + FRAME)
        rkeep = (row_at >= off) & (row_at < off + FRAME)
        for p in range(heads // 2):
            q2 = j_ref[rws, 2 * HD * p : 2 * HD * (p + 1)]
            k2 = j_ref[rws, width + 2 * HD * p : width + 2 * HD * (p + 1)]
            v2 = j_ref[rws, 2 * width + 2 * HD * p : 2 * width + 2 * HD * (p + 1)]
            parts = []
            for side in range(2):
                qs = jnp.where(low if side == 0 else jnp.logical_not(low), q2, jnp.zeros_like(q2))
                sc = jnp.where(keep, dot_nt(qs, k2) * scale, -1e30)
                e = jnp.exp(sc - jnp.max(sc, axis=-1, keepdims=True))
                pb = (e / jnp.sum(e, axis=-1, keepdims=True)).astype(BF)
                parts.append(dot_nn(pb, v2))
            o2 = jnp.where(low, parts[0], parts[1])
            sl = slice(2 * HD * p, 2 * HD * (p + 1))
            o_ref[rws, sl] = jnp.where(rkeep, o2, o_ref[rws, sl].astype(F32)).astype(BF)
        return 0

    lax.fori_loop(0, frames, frame_body, 0)
    for copy in merge_in:
        copy.wait()
    for s, n in row_chunks(rows):
        m = n if s + n < rows else pad - s
        hv = dot_nn(o_ref[s : s + m], w_ref[:, 3 * width :]) + vec_ref[4:5]
        hv = hv[:n] + x_ref[s : s + n].astype(F32)
        norm, _ = stats(hv)
        h_ref[s : s + n] = hv
        bv = (norm * (1.0 + vec_ref[5:6]) + vec_ref[6:7]).astype(BF)
        if m != n:
            h_ref[tail:pad] = jnp.zeros((16, width), F32)
            b_ref[tail:pad] = jnp.zeros((16, width), BF)
            h_ref[s : s + n] = hv
        b_ref[s : s + n] = bv


def forward_call(owners, x, vec, pieces):
    rows, width = x.shape
    pad = padded_rows(rows)
    zs = len(pieces)
    return pl.pallas_call(
        functools.partial(forward_kernel, zs),
        out_shape=(
            jax.ShapeDtypeStruct((pad, width), BF),
            jax.ShapeDtypeStruct((pad, 3 * width), BF),
            jax.ShapeDtypeStruct((pad, width), BF),
            jax.ShapeDtypeStruct((pad, width), F32),
            jax.ShapeDtypeStruct((pad, width), BF),
        ),
        in_specs=[SM, VM, VM] + [HB] * zs,
        out_specs=(VM,) * 5,
        scratch_shapes=[pltpu.VMEM((width, 4 * width), BF), pltpu.SemaphoreType.DMA((2, zs))],
        cost_estimate=LIGHT,
        compiler_params=pltpu.CompilerParams(vmem_limit_bytes=32 << 20),
        name="forward_attention",
    )(owners, x, vec, *pieces)


def gelu_parts(u):
    phi = 0.5 * (1.0 + lax.erf(u * INV_SQRT2))
    return u * phi, phi + u * (jnp.exp(u * u * -0.5) * INV_SQRT2PI)


def ffn_kernel(zs, tiles, own_ref, slot_ref, *refs):
    refs = list(refs)
    b_ref, e_ref, h_ref = refs[:3]
    we_in = refs[3 : 3 + zs]
    wr_in = refs[3 + zs : 3 + 2 * zs]
    bu_ref, vec_ref = refs[3 + 2 * zs : 5 + 2 * zs]
    refs = refs[5 + 2 * zs :]
    g_refs = [[refs.pop(0) for _ in range(zs)] for _ in range(tiles)]
    bug_ref, out_ref, dh_ref, dz_ref, sums_ref = refs[:5]
    es_ref, bt_ref, gs_ref, du_ref, we_ref, wr_ref, acc_ref, db_ref = refs[5:]
    rows, width = e_ref.shape
    pad = b_ref.shape[0]
    tf = we_ref.shape[1]
    k, t = pl.program_id(0), pl.program_id(1)
    own_rows = width // zs
    nh = row_halves(zs)
    nwr = tf // BLK
    rbn = own_rows // BLK
    nblk = nwr + (tf * zs // width) * rbn
    chunk = [(0, 256), (256, 256), (512, 256), (768, pad - 768)] if pad == 992 else [(0, pad)]

    @pl.when(jnp.logical_and(k == 0, t == 0))
    def _():
        es_ref[pad - 16 : pad] = jnp.zeros((16, width), BF)
        es_ref[0:rows] = e_ref[...]
        for c in range(0, width, 256):
            bt_ref[c : c + 256, :] = b_ref[:, c : c + 256].T
        acc_ref[...] = jnp.zeros_like(acc_ref)
        db_ref[...] = jnp.zeros_like(db_ref)

    for kk in range(zs):
        rws = pl.ds(pl.multiple_of(own_ref[kk] * own_rows, own_rows), own_rows)
        we_ref[rws, :] = we_in[kk][...]

        @pl.when(k == kk)
        def _(kk=kk):
            wr_ref[...] = wr_in[kk][...]

    total = jnp.zeros((1, tf), F32)
    for s, n in chunk:
        u = dot_nn(b_ref[s : s + n], we_ref[...]) + bu_ref[...]
        g, d = gelu_parts(u)
        gs_ref[s : s + n] = g.astype(BF)
        du = (dot_nt(es_ref[s : s + n], wr_ref[...]) * d).astype(BF)
        du_ref[s : s + n] = du
        total = total + jnp.sum(du.astype(F32), axis=0, keepdims=True)
    owner = own_ref[k]
    bug_ref[pl.ds(owner, 1), pl.ds(pl.multiple_of(t * tf, 128), tf)] = total
    acc_ref[...] += dot_nn(gs_ref[...], wr_ref[...])
    db_ref[...] += dot_nt(du_ref[...], we_ref[...])
    gwr = dot_tn(gs_ref[...], es_ref[...]).astype(BF)
    for tt in range(tiles):
        for kk in range(zs):
            @pl.when((k == kk) & (t == tt))
            def _(kk=kk, tt=tt):
                for i in range(nwr):
                    slot = slot_ref[kk * nblk + i // (nwr // nh) * (nblk // nh) + i % (nwr // nh)]
                    g_refs[tt][kk][pl.ds(pl.multiple_of(slot * BLK, BLK), BLK), :] = gwr[i * BLK : (i + 1) * BLK]
    col = owner * tf
    cb = col // width
    lane = pl.ds(pl.multiple_of(col % width, 128), tf)
    part = rbn // nh
    for kk in range(zs):
        rws = pl.ds(pl.multiple_of(own_ref[kk] * own_rows, own_rows), own_rows)
        gwe = dot_nn(bt_ref[rws, :], du_ref[...]).astype(BF)
        for tt in range(tiles):
            @pl.when(t == tt)
            def _(kk=kk, tt=tt, gwe=gwe):
                for i in range(rbn):
                    slot = slot_ref[kk * nblk + i // part * (nblk // nh) + nwr // nh + cb * part + i % part]
                    g_refs[tt][kk][pl.ds(pl.multiple_of(slot * BLK, BLK), BLK), lane] = gwe[i * BLK : (i + 1) * BLK]

    @pl.when(jnp.logical_and(k == zs - 1, t == tiles - 1))
    def _():
        da = jnp.zeros((1, width), F32)
        dc = jnp.zeros((1, width), F32)
        de = jnp.zeros((1, width), F32)
        for s, n in chunk:
            hv = h_ref[s : s + n]
            norm, r = stats(hv)
            db = db_ref[s : s + n]
            da = da + jnp.sum(db * norm, axis=0, keepdims=True)
            dc = dc + jnp.sum(db, axis=0, keepdims=True)
            g = db * (1.0 + vec_ref[5:6])
            ev = es_ref[s : s + n].astype(F32)
            de = de + jnp.sum(ev, axis=0, keepdims=True)
            dh = ev + r * (
                g - jnp.mean(g, axis=-1, keepdims=True) - norm * jnp.mean(g * norm, axis=-1, keepdims=True)
            )
            dh_ref[s : s + n] = dh
            dz_ref[s : s + n] = dh.astype(BF)
            ov = (hv + (acc_ref[s : s + n] + vec_ref[11:12])).astype(BF)
            m = min(n, rows - s)
            out_ref[s : s + m] = ov[:m]
        sums_ref[0:1] = da
        sums_ref[1:2] = dc
        sums_ref[2:3] = de


def ffn_call(tiles, owners, slots, b, e, h, we, wr, bu, vec):
    zs = owners.shape[0]
    pad, width = b.shape
    rows = e.shape[0]
    per_owner = we[0].shape[1] // zs
    tf = per_owner // tiles
    nrow = tf + tf * zs // width * (width // zs)

    def ffcol(k, t, own, sl):
        return own[k] * tiles + t

    def wr_row(kk, k, t, own, sl):
        return jnp.where(k < kk, 0, jnp.where(k > kk, tiles - 1, t)), 0

    in_specs = [
        VM,
        VM,
        VM,
        *[pl.BlockSpec((width // zs, tf), lambda k, t, own, sl: (0, ffcol(k, t, own, sl)))] * zs,
        *[pl.BlockSpec((tf, width), functools.partial(wr_row, kk)) for kk in range(zs)],
        pl.BlockSpec((1, tf), lambda k, t, own, sl: (0, ffcol(k, t, own, sl))),
        VM,
    ]
    outs = [jax.ShapeDtypeStruct((nrow, width), BF)] * (zs * tiles) + [
        jax.ShapeDtypeStruct((zs, per_owner), F32),
        jax.ShapeDtypeStruct((rows, width), BF),
        jax.ShapeDtypeStruct((pad, width), F32),
        jax.ShapeDtypeStruct((pad, width), BF),
        jax.ShapeDtypeStruct((8, width), F32),
    ]
    return pl.pallas_call(
        functools.partial(ffn_kernel, zs, tiles),
        out_shape=tuple(outs),
        grid_spec=pltpu.PrefetchScalarGridSpec(
            num_scalar_prefetch=2,
            grid=(zs, tiles),
            in_specs=in_specs,
            out_specs=(VM,) * len(outs),
            scratch_shapes=[
                pltpu.VMEM((pad, width), BF),
                pltpu.VMEM((width, pad), BF),
                pltpu.VMEM((pad, tf), BF),
                pltpu.VMEM((pad, tf), BF),
                pltpu.VMEM((width, tf), BF),
                pltpu.VMEM((tf, width), BF),
                pltpu.VMEM((pad, width), F32),
                pltpu.VMEM((pad, width), F32),
            ],
        ),
        cost_estimate=LIGHT,
        compiler_params=pltpu.CompilerParams(vmem_limit_bytes=FFN_MB << 20),
        name="ffn",
    )(owners, slots, b, e, h, *we, *wr, bu, vec)


FFN_MB = 40


def first_frames(frames):
    return (frames + 1) // 2


def attend_back(lo, hi, base, j_ref, do_ref, dj_ref, dj_base, width):
    win = (FRAME + 12 + 15) // 16 * 16
    scale = HD ** (-0.5)
    key_at = lax.broadcasted_iota(jnp.int32, (win, win), 0)
    qry_at = lax.broadcasted_iota(jnp.int32, (win, win), 1)
    low_side = lax.broadcasted_iota(jnp.int32, (win, 2 * HD), 1) < HD

    def frame_body(f, _):
        start = (f * FRAME) // 16 * 16
        off = f * FRAME - start
        rws = pl.ds(pl.multiple_of(start - base, 16), win)
        drws = pl.ds(pl.multiple_of(start - dj_base, 16), win)
        kkeep = (key_at >= off) & (key_at < off + FRAME)
        keep = kkeep & (qry_at >= off) & (qry_at < off + FRAME)
        for p in range(width // HD // 2):
            sl = [slice(w * width + 2 * HD * p, w * width + 2 * HD * (p + 1)) for w in range(3)]
            q2, k2, v2 = (j_ref[rws, sl[w]] for w in range(3))
            do2 = do_ref[rws, sl[0]]
            res = []
            for side in range(2):
                m = low_side if side == 0 else jnp.logical_not(low_side)
                zero = jnp.zeros_like(k2)
                sc = jnp.where(kkeep, dot_nt(jnp.where(m, k2, zero), q2) * scale, -1e30)
                e = jnp.exp(sc - jnp.max(sc, axis=0, keepdims=True))
                pt = jnp.where(keep, e / jnp.sum(e, axis=0, keepdims=True), 0.0)
                dp = dot_nt(jnp.where(m, v2, zero), do2)
                ds = (pt * (dp - jnp.sum(pt * dp, axis=0, keepdims=True))).astype(BF)
                res.append((dot_tn(ds, k2) * scale, dot_nn(ds, q2) * scale, dot_nn(pt.astype(BF), do2)))
            for w in range(3):
                val = jnp.where(low_side, res[0][w], res[1][w])
                dj_ref[drws, sl[w]] = (dj_ref[drws, sl[w]].astype(F32) + val).astype(BF)
        return 0

    lax.fori_loop(lo, hi, frame_body, 0)


def merge_copies(own_ref, pieces, w_ref, sems, width, first, count):
    own_rows = width // len(pieces)
    copies = []
    for kk, piece in enumerate(pieces):
        rws = pl.ds(pl.multiple_of(own_ref[kk] * own_rows, own_rows), own_rows)
        copies.append(
            pltpu.make_async_copy(piece.at[pl.ds(0, own_rows), pl.ds(first, count)], w_ref.at[rws, :], sems.at[kk])
        )
    return copies


def back_first_kernel(zs, frames, own_ref, j_ref, dz_ref, *refs):
    pieces = refs[:zs]
    dj_ref, do_ref, w_ref, sems = refs[zs:]
    width = dz_ref.shape[1]
    copies = merge_copies(own_ref, pieces, w_ref, sems, width, 3 * width, width)
    for copy in copies:
        copy.start()
    dj_ref[...] = jnp.zeros_like(dj_ref)
    for copy in copies:
        copy.wait()
    do_ref[...] = dot_nt(dz_ref[...], w_ref[...]).astype(BF)
    attend_back(0, first_frames(frames), 0, j_ref, do_ref, dj_ref, 0, width)


def back_first_call(owners, j, dz, pieces, frames):
    zs = len(pieces)
    width = dz.shape[1]
    last = first_frames(frames) - 1
    rows = (last * FRAME) // 16 * 16 + (FRAME + 12 + 15) // 16 * 16
    return pl.pallas_call(
        functools.partial(back_first_kernel, zs, frames),
        grid=(1,),
        out_shape=jax.ShapeDtypeStruct((rows, 3 * width), BF),
        in_specs=[
            SM,
            pl.BlockSpec((rows, 3 * width), lambda i: (0, 0)),
            pl.BlockSpec((rows, width), lambda i: (0, 0)),
        ]
        + [HB] * zs,
        out_specs=pl.BlockSpec((rows, 3 * width), lambda i: (0, 0)),
        scratch_shapes=[
            pltpu.VMEM((rows, width), BF),
            pltpu.VMEM((width, width), BF),
            pltpu.SemaphoreType.DMA((zs,)),
        ],
        cost_estimate=LIGHT,
        compiler_params=pltpu.CompilerParams(vmem_limit_bytes=28 << 20),
        name="back_first",
    )(owners, j, dz, *pieces)


def back_second_kernel(zs, frames, own_ref, slot_ref, a_ref, o_ref, dz_ref, j_hbm, djp_hbm, *refs):
    pieces = refs[:zs]
    g_refs = refs[zs : 2 * zs]
    dj_ref, sums_ref, j_ref, do_ref, t_ref, w_ref, sems, more = refs[2 * zs :]
    pad, width = a_ref.shape
    done = djp_hbm.shape[0]
    base = (first_frames(frames) * FRAME) // 16 * 16
    own_rows = width // zs
    rbn = own_rows // BLK
    copies = merge_copies(own_ref, pieces, w_ref, sems, width, 3 * width, width)
    copies.append(pltpu.make_async_copy(j_hbm.at[pl.ds(base, pad - base), :], j_ref, more.at[0]))
    earlier = pltpu.make_async_copy(djp_hbm, dj_ref.at[pl.ds(0, done), :], more.at[1])
    for copy in copies:
        copy.start()
    earlier.start()
    dj_ref[done:pad] = jnp.zeros((pad - done, 3 * width), BF)
    sums_ref[...] = jnp.zeros_like(sums_ref)
    for c in range(0, width, 256):
        t_ref[c : c + 256, :] = o_ref[:, c : c + 256].T
    sums_ref[0:1] = jnp.sum(dz_ref[...].astype(F32), axis=0, keepdims=True)
    part = rbn // row_halves(zs)

    def put(kk, region, i, val):
        slot = slot_ref[kk * 4 * rbn + i // part * (4 * part) + region * part + i % part]
        g_refs[kk][pl.ds(pl.multiple_of(slot * BLK, BLK), BLK), :] = val

    for kk in range(zs):
        rws = pl.ds(pl.multiple_of(own_ref[kk] * own_rows, own_rows), own_rows)
        gm = dot_nn(t_ref[rws, :], dz_ref[...]).astype(BF)
        for i in range(rbn):
            put(kk, 0, i, gm[i * BLK : (i + 1) * BLK])
    for copy in copies:
        copy.wait()
    do_ref[...] = dot_nt(dz_ref[base:pad], w_ref[...]).astype(BF)
    earlier.wait()
    attend_back(first_frames(frames), frames, base, j_ref, do_ref, dj_ref, 0, width)
    for c in range(0, width, 256):
        t_ref[c : c + 256, :] = a_ref[:, c : c + 256].T
    for w in range(3):
        cols = slice(w * width, (w + 1) * width)
        if w != 1:
            row = 1 if w == 0 else 2
            sums_ref[row : row + 1] = jnp.sum(dj_ref[:, cols].astype(F32), axis=0, keepdims=True)
        for kk in range(zs):
            rws = pl.ds(pl.multiple_of(own_ref[kk] * own_rows, own_rows), own_rows)
            gj = dot_nn(t_ref[rws, :], dj_ref[:, cols]).astype(BF)
            for i in range(rbn):
                put(kk, 1 + w, i, gj[i * BLK : (i + 1) * BLK])


def back_second_call(owners, slots, a, o, dz, j, dj_part, pieces, frames):
    zs = len(pieces)
    pad, width = a.shape
    base = (first_frames(frames) * FRAME) // 16 * 16
    nrow = 4 * (width // zs)
    return pl.pallas_call(
        functools.partial(back_second_kernel, zs, frames),
        out_shape=(jax.ShapeDtypeStruct((nrow, width), BF),) * zs
        + (jax.ShapeDtypeStruct((pad, 3 * width), BF), jax.ShapeDtypeStruct((8, width), F32)),
        in_specs=[SM] * 2 + [VM] * 3 + [HB] * (2 + zs),
        out_specs=(VM,) * (zs + 2),
        scratch_shapes=[
            pltpu.VMEM((pad - base, 3 * width), BF),
            pltpu.VMEM((pad - base, width), BF),
            pltpu.VMEM((width, pad), BF),
            pltpu.VMEM((width, width), BF),
            pltpu.SemaphoreType.DMA((zs,)),
            pltpu.SemaphoreType.DMA((2,)),
        ],
        cost_estimate=LIGHT,
        compiler_params=pltpu.CompilerParams(vmem_limit_bytes=36 << 20),
        name="back_second",
    )(owners, slots, a, o, dz, j, dj_part, *pieces)


def back_last_kernel(zs, own_ref, x_ref, dh_ref, dj_ref, vec_ref, *refs):
    pieces = refs[:zs]
    ig_ref, sums_ref, w_ref, sems = refs[zs:]
    rows, width = x_ref.shape
    pad = dj_ref.shape[0]
    copies = merge_copies(own_ref, pieces, w_ref, sems, width, 0, 3 * width)
    for copy in copies:
        copy.start()
    sums_ref[...] = jnp.zeros_like(sums_ref)
    for copy in copies:
        copy.wait()
    chunk = [(0, 256), (256, 256), (512, 256), (768, pad - 768)] if pad == 992 else [(0, pad)]
    da = jnp.zeros((1, width), F32)
    dc = jnp.zeros((1, width), F32)
    for s, n in chunk:
        m = min(n, rows - s)
        dv = dot_nt(dj_ref[s : s + n], w_ref[...])[:m]
        norm, r = stats(x_ref[s : s + m].astype(F32))
        da = da + jnp.sum(dv * norm, axis=0, keepdims=True)
        dc = dc + jnp.sum(dv, axis=0, keepdims=True)
        g = dv * (1.0 + vec_ref[0:1])
        ig_ref[s : s + m] = dh_ref[s : s + m] + r * (
            g - jnp.mean(g, axis=-1, keepdims=True) - norm * jnp.mean(g * norm, axis=-1, keepdims=True)
        )
    sums_ref[0:1] = da
    sums_ref[1:2] = dc


def back_last_call(owners, x, dh, dj, vec, pieces):
    zs = len(pieces)
    rows, width = x.shape
    return pl.pallas_call(
        functools.partial(back_last_kernel, zs),
        out_shape=(jax.ShapeDtypeStruct((rows, width), F32), jax.ShapeDtypeStruct((8, width), F32)),
        in_specs=[SM] + [VM] * 4 + [HB] * zs,
        out_specs=(VM,) * 2,
        scratch_shapes=[pltpu.VMEM((width, 3 * width), BF), pltpu.SemaphoreType.DMA((zs,))],
        cost_estimate=HEAVY,
        compiler_params=pltpu.CompilerParams(vmem_limit_bytes=32 << 20),
        name="back_last",
    )(owners, x, dh, dj, vec, *pieces)


def lamb_math(g, w, m, s, devices):
    scale = 1.0 / (1.0 - decay_rate**STEP)
    g = g.astype(F32) * (1.0 / devices)
    first = decay_rate * m + (1.0 - decay_rate) * g
    second = decay_rate * s + (1.0 - decay_rate) * g * g
    ratio = (first * scale) / (jnp.sqrt(second * scale) + adam_eps)
    return g, first, second, ratio


def norms_kernel(spots, rows, plan, n_sums, devices, meta_ref, *refs):
    sums = refs[:n_sums]
    refs = refs[n_sums:]
    keep_ref, send_ref, out_ref = refs[-3:]
    lane = meta_ref[0]
    half = keep_ref.shape[1]
    out_ref[...] = jnp.zeros_like(out_ref)
    keep_ref[...] = jnp.zeros_like(keep_ref)
    send_ref[...] = jnp.zeros_like(send_ref)
    for row, (k, source, first) in enumerate(plan):
        for target, side in ((keep_ref, meta_ref[2]), (send_ref, 1 - meta_ref[2])):
            cols = pl.ds(pl.multiple_of(first + side * half, 128), half)
            target[row : row + 1] = sums[k][source : source + 1, cols]
    at = 0
    for regions, places in zip(spots, rows):
        y = refs[at][...]
        at += 1
        for inside, row in zip(regions, places):
            w, m, s = (refs[at + k][...] for k in range(3))
            at += 3
            upd = lamb_math(y, w, m, s, devices)[3] + weight_decay * w
            use = jnp.where(inside(lane), 1.0, 0.0)
            for at_row, square in ((row, w * w), (row + 4, upd * upd)):
                lanes = jnp.sum(square, axis=0, keepdims=True)
                out_ref[at_row : at_row + 1] += jnp.sum(lanes, axis=1, keepdims=True) * use
    keep_ref[NORM_ROW : NORM_ROW + 8, 0:128] = out_ref[...]
    send_ref[NORM_ROW : NORM_ROW + 8, 0:128] = out_ref[...]


NORM_ROW = 16


def norms_call(meta, sums, plan, shards, regions, rows, devices):
    width = shards[0].shape[1]
    cols = width // 2 if plan else 128
    both = pl.BlockSpec((NORM_ROW + 8, cols), lambda i, meta: (0, 0))
    specs = [pl.BlockSpec(s.shape, lambda i, meta: (0, 0)) for s in sums]
    args = list(sums)
    for shard, parts in zip(shards, regions):
        specs.append(pl.BlockSpec((BLK, width), lambda i, meta: (0, 0)))
        args.append(shard)
        for _, place, mat in parts:
            specs += [pl.BlockSpec((BLK, width), lambda i, meta, place=place: place(meta[0]))] * 3
            args += list(mat)
    spots = [[part[0] for part in parts] for parts in regions]
    return pl.pallas_call(
        functools.partial(norms_kernel, spots, rows, plan, len(sums), devices),
        out_shape=(jax.ShapeDtypeStruct((NORM_ROW + 8, cols), F32),) * 2,
        grid_spec=pltpu.PrefetchScalarGridSpec(
            num_scalar_prefetch=1,
            grid=(1,),
            in_specs=specs,
            out_specs=(both,) * 2,
            scratch_shapes=[pltpu.VMEM((8, 128), F32)],
        ),
        cost_estimate=LIGHT,
        compiler_params=pltpu.CompilerParams(vmem_limit_bytes=60 << 20),
        name="norms",
    )(meta, *args)


LAMB_IN = 4
LAMB_OUT = 3


def lamb_kernel(counts, places, rows, lead, n_half, devices, n_alias, meta_ref, slot_ref, total_ref, *refs):
    nbh = sum(counts)
    ys = refs[:n_half]
    ins = refs[n_half : n_half + 6]
    outs = refs[n_half + 6 + n_alias : n_half + 16 + n_alias]
    in_buf, y_buf, out_buf, copy_buf, in_sem, y_sem, out_sem = refs[n_half + 16 + n_alias :]
    bs = in_buf.shape[2]
    width = in_buf.shape[3]
    per = bs // BLK
    steps = nbh * n_half
    half_blk = ys[0].shape[0] // BLK

    def where(i):
        rel, q = i // nbh, i % nbh
        return rel, (rel + lead) ^ meta_ref[1], q

    def window(p, half, q):
        row, col = places[p](half, q - (counts[0] if p else 0))
        return pl.ds(pl.multiple_of(row * bs, bs), bs), pl.ds(pl.multiple_of(col * width, width), width)

    def loads(i, start):
        rel, half, q = where(i)
        b = i % LAMB_IN
        for p in range(2):
            @pl.when((q >= counts[0]) == (p == 1))
            def _(p=p):
                at = window(p, half, q)
                for k in range(3):
                    copy = pltpu.make_async_copy(ins[3 * p + k].at[at], in_buf.at[b, k], in_sem.at[b, k])
                    copy.start() if start else copy.wait()
        for r in range(n_half):
            @pl.when(rel == r)
            def _(r=r):
                for k in range(per):
                    slot = slot_ref[half * half_blk + q * per + k] - (r + lead) * half_blk
                    copy = pltpu.make_async_copy(
                        ys[r].at[pl.ds(pl.multiple_of(slot * BLK, BLK), BLK), :],
                        y_buf.at[b, pl.ds(k * BLK, BLK)], y_sem.at[b, k],
                    )
                    copy.start() if start else copy.wait()

    def stores(i, start):
        _, half, q = where(i)
        b = i % LAMB_OUT
        for p in range(2):
            @pl.when((q >= counts[0]) == (p == 1))
            def _(p=p):
                at = window(p, half, q)
                for k in range(5):
                    src = copy_buf.at[b] if k == 4 else out_buf.at[b, k]
                    copy = pltpu.make_async_copy(src, outs[5 * p + k].at[at], out_sem.at[b, k])
                    copy.start() if start else copy.wait()

    for i in range(LAMB_IN - 1):
        loads(jnp.int32(i), True)

    def step(i, _):
        b, o = i % LAMB_IN, i % LAMB_OUT

        @pl.when(i + LAMB_IN - 1 < steps)
        def _():
            loads(i + LAMB_IN - 1, True)

        loads(i, False)

        @pl.when(i >= LAMB_OUT)
        def _():
            stores(i - LAMB_OUT, False)

        _, _, q = where(i)
        trusts = []
        for row in rows:
            at = NORM_ROW + row
            trusts.append(jnp.sqrt(total_ref[at : at + 1, 0:1]) / jnp.sqrt(total_ref[at + 4 : at + 5, 0:1]))
        trust = jnp.where(q >= counts[0], trusts[1], trusts[0])

        def chunk(c, _):
            at = pl.ds(pl.multiple_of(c * 32, 32), 32)
            w = in_buf[b, 0, at]
            g, first, second, ratio = lamb_math(y_buf[b, at], w, in_buf[b, 1, at], in_buf[b, 2, at], devices)
            weight = w - (matrix_rate * trust) * (ratio + weight_decay * w)
            out_buf[o, 0, at] = g
            out_buf[o, 1, at] = weight
            out_buf[o, 2, at] = first
            out_buf[o, 3, at] = second
            copy_buf[o, at] = weight.astype(BF)
            return 0

        lax.fori_loop(0, bs // 32, chunk, 0)
        stores(i, True)
        return 0

    lax.fori_loop(0, steps, step, 0)
    for i in range(max(0, steps - LAMB_OUT), steps):
        stores(jnp.int32(i), False)


def lamb_call(meta, slots, ys, lead, total, counts, places, rows, mats, bs, devices, before):
    width = ys[0].shape[1]
    flat = [array for mat in mats for array in mat]
    dtypes = (F32, F32, F32, F32, BF)
    out_shape = tuple(jax.ShapeDtypeStruct(mat[0].shape, dt) for mat in mats for dt in dtypes)
    aliased = list(before) if before is not None else []
    aliases = {3 + len(ys) + len(flat) + i: i for i in range(len(aliased))}
    return pl.pallas_call(
        functools.partial(lamb_kernel, counts, places, rows, lead, len(ys), devices, len(aliased)),
        out_shape=out_shape,
        in_specs=[SM, SM, VM] + [HB] * (len(ys) + len(flat) + len(aliased)),
        out_specs=(HB,) * len(out_shape),
        scratch_shapes=[
            pltpu.VMEM((LAMB_IN, 3, bs, width), F32),
            pltpu.VMEM((LAMB_IN, bs, width), BF),
            pltpu.VMEM((LAMB_OUT, 4, bs, width), F32),
            pltpu.VMEM((LAMB_OUT, bs, width), BF),
            pltpu.SemaphoreType.DMA((LAMB_IN, 3)),
            pltpu.SemaphoreType.DMA((LAMB_IN, bs // BLK)),
            pltpu.SemaphoreType.DMA((LAMB_OUT, 5)),
        ],
        input_output_aliases=aliases,
        cost_estimate=LIGHT,
        compiler_params=pltpu.CompilerParams(vmem_limit_bytes=60 << 20),
        name="lamb",
    )(meta, slots, total, *ys, *flat, *aliased)


def bits_of(n):
    return n.bit_length() - 1


class Order:

    def __init__(self):
        self.last = None

    def run(self, fn, *args):
        if self.last is not None:
            args, _ = lax.optimization_barrier((args, self.last))
        out = fn(*args)
        leaves = jax.tree.leaves(out)
        self.last = leaves[0]
        return out


def add_bf(a, b):
    return (a.astype(F32) + b.astype(F32)).astype(BF)


def add_split(a, b):
    half = a.shape[0] // 2
    return add_bf(a[:half], b[:half]), add_bf(a[half:], b[half:])


class Exchange:

    def __init__(self, ds):
        self.ds = ds
        self.z, self.d = lax.axis_index("zero"), lax.axis_index("dp")
        self.stages = bits_of(ds)
        order = list(range(self.stages))
        self.orders = [order, [1, 0] + order[2:]]
        lanes = [
            sum((((self.d >> bit) & 1) << (self.stages - 1 - k)) for k, bit in enumerate(order)) for order in self.orders
        ]
        self.mine = jnp.where(self.z == 0, lanes[0], lanes[1]).astype(jnp.int32)
        self.other = jnp.where(self.z == 0, lanes[1], lanes[0]).astype(jnp.int32)
        self.owners = jnp.stack([1 - self.z, self.z]).astype(jnp.int32)
        base = jnp.arange(ds, dtype=jnp.int32)
        self.own_slots = base ^ self.mine
        self.slots = jnp.concatenate([base ^ self.other, self.own_slots])
        self.meta = jnp.stack([self.mine, self.mine >> (self.stages - 1), self.z]).astype(jnp.int32)

    def swap(self, a):
        return lax.ppermute(a, "zero", [(0, 1), (1, 0)])

    def hop(self, a, stage):
        pairs = []
        for d in range(self.ds):
            for c in range(2):
                pairs.append((d * 2 + c, (d ^ (1 << self.orders[c][stage])) * 2 + c))
        return lax.ppermute(a, ("dp", "zero"), pairs)


class Chain:

    def __init__(self, ex, parts):
        self.ex, self.mine, self.stage = ex, parts[1], 0
        self.recv = ex.swap(parts[0])

    def reduce(self, order):
        ex = self.ex
        if self.stage == ex.stages:
            self.shard = self.own = order.run(add_bf, self.mine, self.recv)
            self.recv = ex.hop(self.own, ex.stages - 1)
        else:
            self.mine, send = order.run(add_split, self.mine, self.recv)
            self.recv = ex.hop(send, self.stage)
        self.stage += 1

    def gather(self, order):
        ex = self.ex
        self.own = order.run(lambda a, b: jnp.concatenate([a, b], axis=0), self.own, self.recv)
        self.stage += 1
        self.recv = ex.hop(self.own, 2 * ex.stages - self.stage)


    def step(self, order):
        self.reduce(order) if self.stage <= self.ex.stages else self.gather(order)


class Total:

    def __init__(self, ex, mine, theirs):
        self.ex, self.total, self.stage = ex, mine, 0
        self.recv = ex.swap(theirs)

    def step(self, order):
        self.total = order.run(jnp.add, self.total, self.recv)
        if self.stage < self.ex.stages:
            self.recv = self.ex.hop(self.total, self.stage)
        self.stage += 1


PLAN = (
    "3", "1", "2", "1", "2", "3", "1", "2", "nf", "3", "f", "1",
    "2", "f", "3", "f", "1", "2", "f", "3", "na", "2", "f", "3",
    "a", "L10", "3", "a", "L11", "a", "3", "a", "L20", "a", "L21", "L30",
    "L31",
)


def lamb_moments(gradient, first_old, second_old):
    correction = 1.0 - decay_rate**STEP
    first_new = decay_rate * first_old + (1.0 - decay_rate) * gradient
    second_new = decay_rate * second_old + (1.0 - decay_rate) * gradient * gradient
    direction = first_new / correction / (jnp.sqrt(second_new / correction) + adam_eps)
    return (first_new, second_new, direction)


def low(v):
    return lax.reduce_precision(v, exponent_bits=8, mantissa_bits=7)


def per_device(
    inputs,
    cotangent,
    master_joint,
    master_merge,
    master_expand,
    master_reduce,
    master_vectors,
    moment_joint,
    moment_merge,
    moment_expand,
    moment_reduce,
    moment_vectors,
    square_joint,
    square_merge,
    square_expand,
    square_reduce,
    square_vectors,
):
    zs = lax.axis_size("zero")
    ds = lax.axis_size("dp")
    devices = zs * ds
    width = inputs.shape[1]
    own_rows = master_joint.shape[0]
    ff = master_expand.shape[1]
    per_owner = ff // zs
    halves = 2 if zs == 2 else 1
    per = per_owner // halves
    rbn = own_rows // BLK
    nwr = per // BLK
    ncb = per * zs // width
    fast = zs == 2 and ds & (ds - 1) == 0 and 4 * rbn == ds and nwr + ncb * rbn == ds
    masters = [master_joint, master_merge, master_expand, master_reduce]
    moments = [moment_joint, moment_merge, moment_expand, moment_reduce]
    squares = [square_joint, square_merge, square_expand, square_reduce]
    mats = list(zip(masters, moments, squares))

    if fast:
        ex = Exchange(ds)
        owners, ffn_slots, attn_slots = ex.owners, ex.slots, ex.slots
        pieces = lambda own: [ex.swap(own), own]
    else:
        owners = jnp.arange(zs, dtype=jnp.int32)
        ffn_slots = jnp.tile(jnp.arange(nwr + ncb * rbn, dtype=jnp.int32), zs)
        attn_slots = jnp.tile(jnp.arange(4 * rbn, dtype=jnp.int32), zs)

        def pieces(own):
            full = lax.all_gather(own, "zero", axis=0)
            return [full[i] for i in range(zs)]

    head = jnp.pad(low(master_vectors), ((0, 4), (0, 4 * width - master_vectors.shape[1])))
    attn_own = jnp.concatenate([jnp.concatenate([master_joint, master_merge], axis=1), head], axis=0).astype(BF)
    attn = pieces(attn_own)
    expand = pieces(master_expand.astype(BF))
    reduce = pieces(master_reduce.astype(BF))
    vecs = [piece[own_rows : own_rows + 12, : width // zs].astype(F32) for piece in attn]
    if fast:
        vecs[1] = low(master_vectors)
        vec = jnp.where(ex.z == 0, jnp.concatenate([vecs[1], vecs[0]], 1), jnp.concatenate(vecs, 1))
    else:
        vec = jnp.concatenate(vecs, axis=1)
    bias_up = vec[7:11].reshape(1, ff)

    order = Order()
    normed, joint, mixed, middle, normed_two = order.run(forward_call, owners, inputs, vec, attn)
    res = order.run(
        functools.partial(ffn_call, halves), owners, ffn_slots, normed_two, cotangent, middle, expand, reduce, bias_up, vec
    )
    ffn_grads = [list(res[zs * half : zs * (half + 1)]) for half in range(halves)]
    bias_sums, outputs, middle_grad, merge_grad, ffn_sums = res[zs * halves :]
    chains = [Chain(ex, parts) for parts in ffn_grads] if fast else []
    frames = inputs.shape[0] // FRAME
    if fast:
        chains[0].reduce(order)
    joint_part = order.run(functools.partial(back_first_call, frames=frames), owners, joint, merge_grad, attn)
    if fast:
        chains[1].reduce(order)
        chains[0].reduce(order)
    res = order.run(
        functools.partial(back_second_call, frames=frames),
        owners, attn_slots, normed, mixed, merge_grad, joint, joint_part, attn,
    )
    attn_grads = list(res[:zs])
    joint_grad, attn_sums = res[zs:]
    if fast:
        chains.append(Chain(ex, attn_grads))
        chains[1].reduce(order)
        chains[0].reduce(order)
    input_grad, last_sums = order.run(back_last_call, owners, inputs, middle_grad, joint_grad, vec, attn)
    if fast:
        ffn_one, ffn_two, attn_chain = chains

        def reduce_place(half):
            return lambda lane: (half * nwr + lane // (ds // 2) * (nwr // 2) + jnp.clip(lane % (ds // 2), 0, nwr // 2 - 1), 0)

        def expand_place(half):
            def place(lane):
                q = jnp.clip(lane % (ds // 2) - nwr // 2, 0, ncb * rbn // 2 - 1)
                cb, i = q // (rbn // 2), q % (rbn // 2)
                return lane // (ds // 2) * (rbn // 2) + i, cb * (per_owner // width) + half * (per // width)
            return place

        def joint_place(lane):
            q = jnp.clip(lane % (ds // 2) - rbn // 2, 0, 3 * rbn // 2 - 1)
            return lane // (ds // 2) * (rbn // 2) + q % (rbn // 2), q // (rbn // 2)

        def merge_place(lane):
            return lane // (ds // 2) * (rbn // 2) + jnp.clip(lane % (ds // 2), 0, rbn // 2 - 1), 0

        in_reduce = lambda lane: lane % (ds // 2) < nwr // 2
        in_expand = lambda lane: lane % (ds // 2) >= nwr // 2
        in_merge = lambda lane: lane % (ds // 2) < rbn // 2
        in_joint = lambda lane: lane % (ds // 2) >= rbn // 2
        regions = [
            [(in_merge, merge_place, mats[1]), (in_joint, joint_place, mats[0])],
            [(in_reduce, reduce_place(0), mats[3]), (in_expand, expand_place(0), mats[2])],
            [(in_reduce, reduce_place(1), mats[3]), (in_expand, expand_place(1), mats[2])],
        ]
        bs = 2 * BLK
        count_r = per // bs // 2
        nrb = own_rows // bs // 2

        def lamb_reduce(half):
            return lambda h, q: (half * (per // bs) + h * count_r + q, 0)

        def lamb_expand(half):
            return lambda h, q: (
                h * nrb + q % nrb, q // nrb * (per_owner // width) + half * (per // width)
            )

        lamb_merge = lambda h, q: (h * nrb + q, 0)
        lamb_joint = lambda h, q: (h * nrb + q % nrb, q // nrb)
        state = {"f": None, "a": None}
        sums = {}

        def ffn_lamb(half, lead):
            chain = chains[half]
            state["f"] = order.run(
                lambda meta, slots, y, total, mats, before: lamb_call(
                    meta, slots, [y], lead, total, [count_r, ncb * nrb], [lamb_reduce(half), lamb_expand(half)],
                    [3, 2], mats, bs, devices, before,
                ),
                ex.meta, ex.own_slots, (chain.own, chain.recv)[lead], sums["f"].total, (mats[3], mats[2]), state["f"],
            )

        def attn_lamb(lead):
            state["a"] = order.run(
                lambda meta, slots, y, total, mats, before: lamb_call(
                    meta, slots, [y], lead, total, [nrb, 3 * nrb], [lamb_merge, lamb_joint], [1, 0], mats, bs,
                    devices, before,
                ),
                ex.meta, ex.own_slots, (attn_chain.own, attn_chain.recv)[lead], sums["a"].total, (mats[1], mats[0]),
                state["a"],
            )

        def norms_of(key):
            if key == "f":
                groups, parts, at = (ffn_one, ffn_two), regions[1:], [[3, 2]] * 2
                small = (last_sums, attn_sums, ffn_sums, bias_sums)
                plan = [(0, 0, 0), (0, 1, 0), (1, 1, 0), (1, 2, 0), (1, 0, 0), (2, 0, 0), (2, 1, 0)]
                plan += [(3, k // halves, k % halves * width) for k in range(ff // width)] + [(2, 2, 0)]
            else:
                groups, parts, at, small, plan = (attn_chain,), regions[:1], [[1, 0]], (), []
            keep, send = order.run(
                lambda meta, small, *shards: norms_call(meta, small, plan, shards, parts, at, devices),
                ex.meta, small, *[chain.shard for chain in groups],
            )
            sums[key] = Total(ex, keep, send)

        for act in PLAN:
            if act[0] == "n":
                norms_of(act[1])
            elif act in "fa":
                sums[act].step(order)
            elif act in "123":
                chains[int(act) - 1].step(order)
            else:
                stack, lead = int(act[1]), int(act[2])
                attn_lamb(lead) if stack == 3 else ffn_lamb(stack - 1, lead)
        ffn_out, attn_out = state["f"], state["a"]
        vec_total = sums["f"].total[:12]
        norm_values = jnp.sqrt(sums["f"].total[NORM_ROW:, 0] + sums["a"].total[NORM_ROW:, 0])
        outs = [attn_out[5:10], attn_out[0:5], ffn_out[5:10], ffn_out[0:5]]
    else:
        def summed(parts):
            stack = lax.psum_scatter(jnp.concatenate(parts, axis=0), "zero", scatter_dimension=0, tiled=True)
            stack = lax.psum_scatter(stack, "dp", scatter_dimension=0, tiled=True)
            return lax.all_gather(stack, "dp", axis=0, tiled=True).astype(F32) / devices

        def side_by_side(stack):
            return stack.reshape(-1, own_rows, width).transpose(1, 0, 2).reshape(own_rows, -1)

        ffn = summed(ffn_grads[0])
        attn_sum = summed(attn_grads)
        grads = [
            side_by_side(attn_sum[own_rows:]), attn_sum[:own_rows], side_by_side(ffn[per:]), ffn[:per]
        ]
        rows = jnp.concatenate(
            [
                last_sums[0:2],
                attn_sums[1:3],
                attn_sums[0:1],
                ffn_sums[0:2],
                bias_sums.reshape(ff // width, width),
                ffn_sums[2:3],
            ],
            axis=0,
        )
        blocks = rows.reshape(12, zs, width // zs).transpose(1, 0, 2)
        vec_total = lax.psum(lax.psum_scatter(blocks, "zero", scatter_dimension=0, tiled=True)[0], "dp")
        moved = [lamb_moments(g, m, s) for g, m, s in zip(grads, moments, squares)]
        upds = [move[2] + weight_decay * w for move, w in zip(moved, masters)]
        local = jnp.stack([jnp.sum(w * w) for w in masters] + [jnp.sum(u * u) for u in upds])
        norm_values = jnp.sqrt(lax.psum(local, "zero"))
        outs = []
        for k in range(4):
            weight = masters[k] - matrix_rate * (norm_values[k] / norm_values[k + 4]) * upds[k]
            outs.append((grads[k], weight, moved[k][0], moved[k][1], weight.astype(BF)))

    grad_vec = vec_total / devices
    first_vec, second_vec, vec_direction = lamb_moments(grad_vec, moment_vectors, square_vectors)
    new_vectors = master_vectors - vector_rate * vec_direction
    vector_out = (grad_vec, new_vectors, first_vec, second_vec, new_vectors.astype(BF))
    result = [outputs, input_grad]
    for k in range(5):
        result += [out[k] for out in outs] + [vector_out[k]]
    return (*result, norm_values)


def solution(mesh):
    tokens = P(("dp", "zero"), None)
    matrix = P("zero", None)
    vector = P(None, "zero")
    five = (matrix,) * 4 + (vector,)
    return jax.shard_map(
        per_device,
        mesh=mesh,
        in_specs=(tokens, tokens) + five * 3,
        out_specs=(tokens, tokens) + five * 5 + (P(),),
        check_vma=False,
    )
```

```python
import functools

import jax
import jax.numpy as jnp
from jax import lax
from jax.experimental import pallas as pl
from jax.experimental.pallas import tpu as pltpu
from jax.sharding import PartitionSpec as P

HD = 64
FRAME = 196
STEP = 4
BLK = 96

norm_eps = 1e-06
adam_eps = 1e-06
decay_rate = 0.5
weight_decay = 0.01
matrix_rate = 0.5
vector_rate = 0.1
BF = jnp.bfloat16
F32 = jnp.float32
VM = pl.BlockSpec(memory_space=pltpu.VMEM)
SM = pl.BlockSpec(memory_space=pltpu.SMEM)
HB = pl.BlockSpec(memory_space=pl.ANY)
HM = pl.BlockSpec(memory_space=pltpu.HBM)
HEAVY = pl.CostEstimate(flops=5 * 10**10, bytes_accessed=10**8, transcendentals=0)
LIGHT = pl.CostEstimate(flops=1000, bytes_accessed=1000, transcendentals=0)
INV_SQRT2 = 0.7071067811865476
INV_SQRT2PI = 0.3989422804014327


def padded_rows(rows):
    return (rows + 15) // 16 * 16


def row_chunks(rows):
    edges = list(range(0, rows, 192))
    if rows - edges[-1] < 96 and len(edges) > 1:
        edges.pop()
    return [(s, (edges[i + 1] if i + 1 < len(edges) else rows) - s) for i, s in enumerate(edges)]


def row_halves(zs):
    return 2 if zs == 2 else 1


def dot_nn(a, b):
    return lax.dot_general(a, b, (((1,), (0,)), ((), ())), preferred_element_type=F32)


def dot_nt(a, b):
    return lax.dot_general(a, b, (((1,), (1,)), ((), ())), preferred_element_type=F32)


def dot_tn(a, b):
    return lax.dot_general(a, b, (((0,), (0,)), ((), ())), preferred_element_type=F32)


def stats(v):
    mean = jnp.mean(v, axis=-1, keepdims=True)
    c = v - mean
    r = lax.rsqrt(jnp.mean(c * c, axis=-1, keepdims=True) + norm_eps)
    return c * r, r


def piece_copies(own_ref, pieces, w_ref, sems, width):
    own_rows = width // len(pieces)
    copies = []
    for col, (first, count) in enumerate(((0, 3 * width), (3 * width, width))):
        cols = pl.ds(first, count)
        for kk, piece in enumerate(pieces):
            rws = pl.ds(pl.multiple_of(own_ref[kk] * own_rows, own_rows), own_rows)
            copies.append(
                pltpu.make_async_copy(
                    piece.at[pl.ds(0, own_rows), cols], w_ref.at[rws, cols], sems.at[col, kk]
                )
            )
    return copies[: len(pieces)], copies[len(pieces) :]


def forward_kernel(zs, own_ref, x_ref, vec_ref, *refs):
    pieces = refs[:zs]
    a_ref, j_ref, o_ref, h_ref, b_ref, w_ref, sems = refs[zs:]
    rows, width = x_ref.shape
    joint_in, merge_in = piece_copies(own_ref, pieces, w_ref, sems, width)
    for copy in joint_in + merge_in:
        copy.start()
    pad = a_ref.shape[0]
    frames = rows // FRAME
    heads = width // HD
    win = (FRAME + 12 + 15) // 16 * 16
    scale = HD ** (-0.5)
    tail = pad - 16
    a_ref[tail:pad] = jnp.zeros((16, width), BF)
    o_ref[tail:pad] = jnp.zeros((16, width), BF)
    for s, n in row_chunks(rows):
        norm, _ = stats(x_ref[s : s + n].astype(F32))
        a_ref[s : s + n] = (norm * (1.0 + vec_ref[0:1]) + vec_ref[1:2]).astype(BF)
    for copy in joint_in:
        copy.wait()
    step = 256

    def joint_cols(c, _):
        cols = pl.ds(pl.multiple_of(c * step, step), step)
        per = width // step
        which = c // per
        lane = pl.ds(pl.multiple_of((c % per) * step, step), step)
        row = jnp.where(which == 0, vec_ref[2:3, lane], jnp.where(which == 2, vec_ref[3:4, lane], 0.0))
        j_ref[:, cols] = (dot_nn(a_ref[...], w_ref[:, cols]) + row).astype(BF)
        return 0

    lax.fori_loop(0, 3 * width // step, joint_cols, 0)
    key_at = lax.broadcasted_iota(jnp.int32, (win, win), 1)
    row_at = lax.broadcasted_iota(jnp.int32, (win, 2 * HD), 0)
    low = lax.broadcasted_iota(jnp.int32, (win, 2 * HD), 1) < HD

    def frame_body(f, _):
        start = pl.multiple_of((f * FRAME) // 16 * 16, 16)
        off = f * FRAME - start
        rws = pl.ds(start, win)
        keep = (key_at >= off) & (key_at < off + FRAME)
        rkeep = (row_at >= off) & (row_at < off + FRAME)
        for p in range(heads // 2):
            q2 = j_ref[rws, 2 * HD * p : 2 * HD * (p + 1)]
            k2 = j_ref[rws, width + 2 * HD * p : width + 2 * HD * (p + 1)]
            v2 = j_ref[rws, 2 * width + 2 * HD * p : 2 * width + 2 * HD * (p + 1)]
            parts = []
            for side in range(2):
                qs = jnp.where(low if side == 0 else jnp.logical_not(low), q2, jnp.zeros_like(q2))
                sc = jnp.where(keep, dot_nt(qs, k2) * scale, -1e30)
                e = jnp.exp(sc - jnp.max(sc, axis=-1, keepdims=True))
                pb = (e / jnp.sum(e, axis=-1, keepdims=True)).astype(BF)
                parts.append(dot_nn(pb, v2))
            o2 = jnp.where(low, parts[0], parts[1])
            sl = slice(2 * HD * p, 2 * HD * (p + 1))
            o_ref[rws, sl] = jnp.where(rkeep, o2, o_ref[rws, sl].astype(F32)).astype(BF)
        return 0

    lax.fori_loop(0, frames, frame_body, 0)
    for copy in merge_in:
        copy.wait()
    for s, n in row_chunks(rows):
        m = n if s + n < rows else pad - s
        hv = dot_nn(o_ref[s : s + m], w_ref[:, 3 * width :]) + vec_ref[4:5]
        hv = hv[:n] + x_ref[s : s + n].astype(F32)
        norm, _ = stats(hv)
        h_ref[s : s + n] = hv
        bv = (norm * (1.0 + vec_ref[5:6]) + vec_ref[6:7]).astype(BF)
        if m != n:
            h_ref[tail:pad] = jnp.zeros((16, width), F32)
            b_ref[tail:pad] = jnp.zeros((16, width), BF)
            h_ref[s : s + n] = hv
        b_ref[s : s + n] = bv


def forward_call(owners, x, vec, pieces):
    rows, width = x.shape
    pad = padded_rows(rows)
    zs = len(pieces)
    return pl.pallas_call(
        functools.partial(forward_kernel, zs),
        out_shape=(
            jax.ShapeDtypeStruct((pad, width), BF),
            jax.ShapeDtypeStruct((pad, 3 * width), BF),
            jax.ShapeDtypeStruct((pad, width), BF),
            jax.ShapeDtypeStruct((pad, width), F32),
            jax.ShapeDtypeStruct((pad, width), BF),
        ),
        in_specs=[SM, VM, VM] + [HB] * zs,
        out_specs=(VM,) * 5,
        scratch_shapes=[pltpu.VMEM((width, 4 * width), BF), pltpu.SemaphoreType.DMA((2, zs))],
        cost_estimate=LIGHT,
        compiler_params=pltpu.CompilerParams(vmem_limit_bytes=24 << 20),
        name="forward_attention",
    )(owners, x, vec, *pieces)


def gelu_parts(u):
    phi = 0.5 * (1.0 + lax.erf(u * INV_SQRT2))
    return u * phi, phi + u * (jnp.exp(u * u * -0.5) * INV_SQRT2PI)


def ffn_kernel(zs, tiles, own_ref, slot_ref, *refs):
    refs = list(refs)
    b_ref, e_ref, h_ref = refs[:3]
    we_in = refs[3 : 3 + zs]
    wr_in = refs[3 + zs : 3 + 2 * zs]
    bu_ref, vec_ref = refs[3 + 2 * zs : 5 + 2 * zs]
    refs = refs[5 + 2 * zs :]
    g_refs = [[refs.pop(0) for _ in range(zs)] for _ in range(tiles)]
    bug_ref, out_ref, dh_ref, dz_ref, sums_ref = refs[:5]
    es_ref, bt_ref, gs_ref, du_ref, we_bufs, wr_bufs, acc_ref, db_ref, sems = refs[5:]
    rows, width = e_ref.shape
    pad = b_ref.shape[0]
    tf = we_bufs.shape[2]
    k, t = pl.program_id(0), pl.program_id(1)
    own_rows = width // zs
    now = k * tiles + t

    def weights(n, start):
        nk, nt = n // tiles, n % tiles
        buf = n % 2
        cols = pl.ds(pl.multiple_of((own_ref[nk] * tiles + nt) * tf, 128), tf)
        for kk in range(zs):
            rws = pl.ds(pl.multiple_of(own_ref[kk] * own_rows, own_rows), own_rows)
            copy = pltpu.make_async_copy(we_in[kk].at[:, cols], we_bufs.at[buf, rws], sems.at[buf, kk])
            copy.start() if start else copy.wait()

            @pl.when(nk == kk)
            def _(kk=kk):
                rows_in = pl.ds(pl.multiple_of(nt * tf, 16), tf)
                copy = pltpu.make_async_copy(wr_in[kk].at[rows_in, :], wr_bufs.at[buf], sems.at[buf, zs])
                copy.start() if start else copy.wait()

    @pl.when(now == 0)
    def _():
        weights(now, True)

    @pl.when(now + 1 < zs * tiles)
    def _():
        weights(now + 1, True)

    nh = row_halves(zs)
    nwr = tf // BLK
    rbn = own_rows // BLK
    nblk = nwr + (tf * zs // width) * rbn
    chunk = [(0, 256), (256, 256), (512, 256), (768, pad - 768)] if pad == 992 else [(0, pad)]

    @pl.when(jnp.logical_and(k == 0, t == 0))
    def _():
        es_ref[pad - 16 : pad] = jnp.zeros((16, width), BF)
        es_ref[0:rows] = e_ref[...]
        for c in range(0, width, 256):
            bt_ref[c : c + 256, :] = b_ref[:, c : c + 256].T
        acc_ref[...] = jnp.zeros_like(acc_ref)
        db_ref[...] = jnp.zeros_like(db_ref)

    weights(now, False)
    we_ref, wr_ref = we_bufs.at[now % 2], wr_bufs.at[now % 2]
    total = jnp.zeros((1, tf), F32)
    for s, n in chunk:
        u = dot_nn(b_ref[s : s + n], we_ref[...]) + bu_ref[...]
        g, d = gelu_parts(u)
        gs_ref[s : s + n] = g.astype(BF)
        du = (dot_nt(es_ref[s : s + n], wr_ref[...]) * d).astype(BF)
        du_ref[s : s + n] = du
        total = total + jnp.sum(du.astype(F32), axis=0, keepdims=True)
    owner = own_ref[k]
    bug_ref[pl.ds(owner, 1), pl.ds(pl.multiple_of(t * tf, 128), tf)] = total
    acc_ref[...] += dot_nn(gs_ref[...], wr_ref[...])
    db_ref[...] += dot_nt(du_ref[...], we_ref[...])
    gwr = dot_tn(gs_ref[...], es_ref[...]).astype(BF)
    for tt in range(tiles):
        for kk in range(zs):
            @pl.when((k == kk) & (t == tt))
            def _(kk=kk, tt=tt):
                for i in range(nwr):
                    slot = slot_ref[kk * nblk + i // (nwr // nh) * (nblk // nh) + i % (nwr // nh)]
                    g_refs[tt][kk][pl.ds(pl.multiple_of(slot * BLK, BLK), BLK), :] = gwr[i * BLK : (i + 1) * BLK]
    col = owner * tf
    cb = col // width
    lane = pl.ds(pl.multiple_of(col % width, 128), tf)
    part = rbn // nh
    for kk in range(zs):
        rws = pl.ds(pl.multiple_of(own_ref[kk] * own_rows, own_rows), own_rows)
        gwe = dot_nn(bt_ref[rws, :], du_ref[...]).astype(BF)
        for tt in range(tiles):
            @pl.when(t == tt)
            def _(kk=kk, tt=tt, gwe=gwe):
                for i in range(rbn):
                    slot = slot_ref[kk * nblk + i // part * (nblk // nh) + nwr // nh + cb * part + i % part]
                    g_refs[tt][kk][pl.ds(pl.multiple_of(slot * BLK, BLK), BLK), lane] = gwe[i * BLK : (i + 1) * BLK]

    @pl.when(jnp.logical_and(k == zs - 1, t == tiles - 1))
    def _():
        da = jnp.zeros((1, width), F32)
        dc = jnp.zeros((1, width), F32)
        de = jnp.zeros((1, width), F32)
        for s, n in chunk:
            hv = h_ref[s : s + n]
            norm, r = stats(hv)
            db = db_ref[s : s + n]
            da = da + jnp.sum(db * norm, axis=0, keepdims=True)
            dc = dc + jnp.sum(db, axis=0, keepdims=True)
            g = db * (1.0 + vec_ref[5:6])
            ev = es_ref[s : s + n].astype(F32)
            de = de + jnp.sum(ev, axis=0, keepdims=True)
            dh = ev + r * (
                g - jnp.mean(g, axis=-1, keepdims=True) - norm * jnp.mean(g * norm, axis=-1, keepdims=True)
            )
            dh_ref[s : s + n] = dh
            dz_ref[s : s + n] = dh.astype(BF)
            ov = (hv + (acc_ref[s : s + n] + vec_ref[11:12])).astype(BF)
            m = min(n, rows - s)
            out_ref[s : s + m] = ov[:m]
        sums_ref[0:1] = da
        sums_ref[1:2] = dc
        sums_ref[2:3] = de


def ffn_call(tiles, owners, slots, b, e, h, we, wr, bu, vec):
    zs = owners.shape[0]
    pad, width = b.shape
    rows = e.shape[0]
    per_owner = we[0].shape[1] // zs
    tf = per_owner // tiles
    nrow = tf + tf * zs // width * (width // zs)

    def ffcol(k, t, own, sl):
        return own[k] * tiles + t

    in_specs = [
        VM,
        VM,
        VM,
        *[HB] * (2 * zs),
        pl.BlockSpec((1, tf), lambda k, t, own, sl: (0, ffcol(k, t, own, sl))),
        VM,
    ]
    outs = [jax.ShapeDtypeStruct((nrow, width), BF)] * (zs * tiles) + [
        jax.ShapeDtypeStruct((zs, per_owner), F32),
        jax.ShapeDtypeStruct((rows, width), BF),
        jax.ShapeDtypeStruct((pad, width), F32),
        jax.ShapeDtypeStruct((pad, width), BF),
        jax.ShapeDtypeStruct((8, width), F32),
    ]
    return pl.pallas_call(
        functools.partial(ffn_kernel, zs, tiles),
        out_shape=tuple(outs),
        grid_spec=pltpu.PrefetchScalarGridSpec(
            num_scalar_prefetch=2,
            grid=(zs, tiles),
            in_specs=in_specs,
            out_specs=(VM,) * len(outs),
            scratch_shapes=[
                pltpu.VMEM((pad, width), BF),
                pltpu.VMEM((width, pad), BF),
                pltpu.VMEM((pad, tf), BF),
                pltpu.VMEM((pad, tf), BF),
                pltpu.VMEM((2, width, tf), BF),
                pltpu.VMEM((2, tf, width), BF),
                pltpu.VMEM((pad, width), F32),
                pltpu.VMEM((pad, width), F32),
                pltpu.SemaphoreType.DMA((2, zs + 1)),
            ],
        ),
        cost_estimate=LIGHT,
        compiler_params=pltpu.CompilerParams(vmem_limit_bytes=FFN_MB << 20),
        name="ffn",
    )(owners, slots, b, e, h, *we, *wr, bu, vec)


FFN_MB = 33


def first_frames(frames):
    return (frames + 1) // 2


def attend_back(lo, hi, base, j_ref, do_ref, dj_ref, dj_base, width):
    win = (FRAME + 12 + 15) // 16 * 16
    scale = HD ** (-0.5)
    key_at = lax.broadcasted_iota(jnp.int32, (win, win), 0)
    qry_at = lax.broadcasted_iota(jnp.int32, (win, win), 1)
    low_side = lax.broadcasted_iota(jnp.int32, (win, 2 * HD), 1) < HD

    def frame_body(f, _):
        start = (f * FRAME) // 16 * 16
        off = f * FRAME - start
        rws = pl.ds(pl.multiple_of(start - base, 16), win)
        drws = pl.ds(pl.multiple_of(start - dj_base, 16), win)
        kkeep = (key_at >= off) & (key_at < off + FRAME)
        keep = kkeep & (qry_at >= off) & (qry_at < off + FRAME)
        for p in range(width // HD // 2):
            sl = [slice(w * width + 2 * HD * p, w * width + 2 * HD * (p + 1)) for w in range(3)]
            q2, k2, v2 = (j_ref[rws, sl[w]] for w in range(3))
            do2 = do_ref[rws, sl[0]]
            res = []
            for side in range(2):
                m = low_side if side == 0 else jnp.logical_not(low_side)
                zero = jnp.zeros_like(k2)
                sc = jnp.where(kkeep, dot_nt(jnp.where(m, k2, zero), q2) * scale, -1e30)
                e = jnp.exp(sc - jnp.max(sc, axis=0, keepdims=True))
                pt = jnp.where(keep, e / jnp.sum(e, axis=0, keepdims=True), 0.0)
                dp = dot_nt(jnp.where(m, v2, zero), do2)
                ds = (pt * (dp - jnp.sum(pt * dp, axis=0, keepdims=True))).astype(BF)
                res.append((dot_tn(ds, k2) * scale, dot_nn(ds, q2) * scale, dot_nn(pt.astype(BF), do2)))
            for w in range(3):
                val = jnp.where(low_side, res[0][w], res[1][w])
                dj_ref[drws, sl[w]] = (dj_ref[drws, sl[w]].astype(F32) + val).astype(BF)
        return 0

    lax.fori_loop(lo, hi, frame_body, 0)


def merge_copies(own_ref, pieces, w_ref, sems, width, first, count):
    own_rows = width // len(pieces)
    copies = []
    for kk, piece in enumerate(pieces):
        rws = pl.ds(pl.multiple_of(own_ref[kk] * own_rows, own_rows), own_rows)
        copies.append(
            pltpu.make_async_copy(piece.at[pl.ds(0, own_rows), pl.ds(first, count)], w_ref.at[rws, :], sems.at[kk])
        )
    return copies


def back_first_kernel(zs, frames, own_ref, j_ref, dz_ref, *refs):
    pieces = refs[:zs]
    dj_ref, do_ref, w_ref, sems = refs[zs:]
    width = dz_ref.shape[1]
    copies = merge_copies(own_ref, pieces, w_ref, sems, width, 3 * width, width)
    for copy in copies:
        copy.start()
    dj_ref[...] = jnp.zeros_like(dj_ref)
    for copy in copies:
        copy.wait()
    do_ref[...] = dot_nt(dz_ref[...], w_ref[...]).astype(BF)
    attend_back(0, first_frames(frames), 0, j_ref, do_ref, dj_ref, 0, width)


def back_first_call(owners, j, dz, pieces, frames):
    zs = len(pieces)
    width = dz.shape[1]
    last = first_frames(frames) - 1
    rows = (last * FRAME) // 16 * 16 + (FRAME + 12 + 15) // 16 * 16
    return pl.pallas_call(
        functools.partial(back_first_kernel, zs, frames),
        grid=(1,),
        out_shape=jax.ShapeDtypeStruct((rows, 3 * width), BF),
        in_specs=[
            SM,
            pl.BlockSpec((rows, 3 * width), lambda i: (0, 0)),
            pl.BlockSpec((rows, width), lambda i: (0, 0)),
        ]
        + [HB] * zs,
        out_specs=pl.BlockSpec((rows, 3 * width), lambda i: (0, 0)),
        scratch_shapes=[
            pltpu.VMEM((rows, width), BF),
            pltpu.VMEM((width, width), BF),
            pltpu.SemaphoreType.DMA((zs,)),
        ],
        cost_estimate=LIGHT,
        compiler_params=pltpu.CompilerParams(vmem_limit_bytes=20 << 20),
        name="back_first",
    )(owners, j, dz, *pieces)


def back_second_kernel(zs, frames, own_ref, slot_ref, a_ref, o_ref, dz_ref, j_hbm, djp_hbm, *refs):
    pieces = refs[:zs]
    g_refs = refs[zs : 2 * zs]
    dj_ref, sums_ref, j_ref, do_ref, t_ref, w_ref, sems, more = refs[2 * zs :]
    pad, width = a_ref.shape
    done = djp_hbm.shape[0]
    base = (first_frames(frames) * FRAME) // 16 * 16
    own_rows = width // zs
    rbn = own_rows // BLK
    copies = merge_copies(own_ref, pieces, w_ref, sems, width, 3 * width, width)
    copies.append(pltpu.make_async_copy(j_hbm.at[pl.ds(base, pad - base), :], j_ref, more.at[0]))
    earlier = pltpu.make_async_copy(djp_hbm, dj_ref.at[pl.ds(0, done), :], more.at[1])
    for copy in copies:
        copy.start()
    earlier.start()
    dj_ref[done:pad] = jnp.zeros((pad - done, 3 * width), BF)
    sums_ref[...] = jnp.zeros_like(sums_ref)
    for c in range(0, width, 256):
        t_ref[c : c + 256, :] = o_ref[:, c : c + 256].T
    sums_ref[0:1] = jnp.sum(dz_ref[...].astype(F32), axis=0, keepdims=True)
    part = rbn // row_halves(zs)

    def put(kk, region, i, val):
        slot = slot_ref[kk * 4 * rbn + i // part * (4 * part) + region * part + i % part]
        g_refs[kk][pl.ds(pl.multiple_of(slot * BLK, BLK), BLK), :] = val

    for kk in range(zs):
        rws = pl.ds(pl.multiple_of(own_ref[kk] * own_rows, own_rows), own_rows)
        gm = dot_nn(t_ref[rws, :], dz_ref[...]).astype(BF)
        for i in range(rbn):
            put(kk, 0, i, gm[i * BLK : (i + 1) * BLK])
    for copy in copies:
        copy.wait()
    do_ref[...] = dot_nt(dz_ref[base:pad], w_ref[...]).astype(BF)
    earlier.wait()
    attend_back(first_frames(frames), frames, base, j_ref, do_ref, dj_ref, 0, width)
    for c in range(0, width, 256):
        t_ref[c : c + 256, :] = a_ref[:, c : c + 256].T
    for w in range(3):
        cols = slice(w * width, (w + 1) * width)
        if w != 1:
            row = 1 if w == 0 else 2
            sums_ref[row : row + 1] = jnp.sum(dj_ref[:, cols].astype(F32), axis=0, keepdims=True)
        for kk in range(zs):
            rws = pl.ds(pl.multiple_of(own_ref[kk] * own_rows, own_rows), own_rows)
            gj = dot_nn(t_ref[rws, :], dj_ref[:, cols]).astype(BF)
            for i in range(rbn):
                put(kk, 1 + w, i, gj[i * BLK : (i + 1) * BLK])


def back_second_call(owners, slots, a, o, dz, j, dj_part, pieces, frames):
    zs = len(pieces)
    pad, width = a.shape
    base = (first_frames(frames) * FRAME) // 16 * 16
    nrow = 4 * (width // zs)
    return pl.pallas_call(
        functools.partial(back_second_kernel, zs, frames),
        out_shape=(jax.ShapeDtypeStruct((nrow, width), BF),) * zs
        + (jax.ShapeDtypeStruct((pad, 3 * width), BF), jax.ShapeDtypeStruct((8, width), F32)),
        in_specs=[SM] * 2 + [VM] * 3 + [HB] * (2 + zs),
        out_specs=(VM,) * (zs + 2),
        scratch_shapes=[
            pltpu.VMEM((pad - base, 3 * width), BF),
            pltpu.VMEM((pad - base, width), BF),
            pltpu.VMEM((width, pad), BF),
            pltpu.VMEM((width, width), BF),
            pltpu.SemaphoreType.DMA((zs,)),
            pltpu.SemaphoreType.DMA((2,)),
        ],
        cost_estimate=LIGHT,
        compiler_params=pltpu.CompilerParams(vmem_limit_bytes=26 << 20),
        name="back_second",
    )(owners, slots, a, o, dz, j, dj_part, *pieces)


def back_last_kernel(zs, own_ref, x_ref, dh_ref, dj_ref, vec_ref, *refs):
    pieces = refs[:zs]
    ig_ref, sums_ref, w_ref, sems = refs[zs:]
    rows, width = x_ref.shape
    pad = dj_ref.shape[0]
    copies = merge_copies(own_ref, pieces, w_ref, sems, width, 0, 3 * width)
    for copy in copies:
        copy.start()
    sums_ref[...] = jnp.zeros_like(sums_ref)
    for copy in copies:
        copy.wait()
    chunk = [(0, 256), (256, 256), (512, 256), (768, pad - 768)] if pad == 992 else [(0, pad)]
    da = jnp.zeros((1, width), F32)
    dc = jnp.zeros((1, width), F32)
    for s, n in chunk:
        m = min(n, rows - s)
        dv = dot_nt(dj_ref[s : s + n], w_ref[...])[:m]
        norm, r = stats(x_ref[s : s + m].astype(F32))
        da = da + jnp.sum(dv * norm, axis=0, keepdims=True)
        dc = dc + jnp.sum(dv, axis=0, keepdims=True)
        g = dv * (1.0 + vec_ref[0:1])
        ig_ref[s : s + m] = dh_ref[s : s + m] + r * (
            g - jnp.mean(g, axis=-1, keepdims=True) - norm * jnp.mean(g * norm, axis=-1, keepdims=True)
        )
    sums_ref[0:1] = da
    sums_ref[1:2] = dc


def back_last_call(owners, x, dh, dj, vec, pieces):
    zs = len(pieces)
    rows, width = x.shape
    return pl.pallas_call(
        functools.partial(back_last_kernel, zs),
        out_shape=(jax.ShapeDtypeStruct((rows, width), F32), jax.ShapeDtypeStruct((8, width), F32)),
        in_specs=[SM] + [VM] * 4 + [HB] * zs,
        out_specs=(VM,) * 2,
        scratch_shapes=[pltpu.VMEM((width, 3 * width), BF), pltpu.SemaphoreType.DMA((zs,))],
        cost_estimate=HEAVY,
        compiler_params=pltpu.CompilerParams(vmem_limit_bytes=18 << 20),
        name="back_last",
    )(owners, x, dh, dj, vec, *pieces)


def lamb_math(g, w, m, s, devices):
    scale = 1.0 / (1.0 - decay_rate**STEP)
    g = g.astype(F32) * (1.0 / devices)
    first = decay_rate * m + (1.0 - decay_rate) * g
    second = decay_rate * s + (1.0 - decay_rate) * g * g
    ratio = (first * scale) / (jnp.sqrt(second * scale) + adam_eps)
    return g, first, second, ratio


def norms_kernel(spots, rows, plan, n_sums, devices, meta_ref, *refs):
    sums = refs[:n_sums]
    y_refs = refs[n_sums : n_sums + len(spots)]
    mats = refs[n_sums + len(spots) : -5]
    keep_ref, send_ref, out_ref, buf, sems = refs[-5:]
    lane = meta_ref[0]
    half = keep_ref.shape[1]
    out_ref[...] = jnp.zeros_like(out_ref)
    keep_ref[...] = jnp.zeros_like(keep_ref)
    send_ref[...] = jnp.zeros_like(send_ref)
    for row, (k, source, first) in enumerate(plan):
        for target, side in ((keep_ref, meta_ref[2]), (send_ref, 1 - meta_ref[2])):
            cols = pl.ds(pl.multiple_of(first + side * half, 128), half)
            target[row : row + 1] = sums[k][source : source + 1, cols]
    width = y_refs[0].shape[1]

    def each(act):
        at = 0
        for n, (regions, places) in enumerate(zip(spots, rows)):
            for (inside, place), row in zip(regions, places):
                mat = mats[at : at + 3]
                at += 3

                @pl.when(inside(lane))
                def _(n=n, place=place, mat=mat, row=row):
                    r, c = place(lane)
                    window = pl.ds(pl.multiple_of(r * BLK, 32), BLK), pl.ds(pl.multiple_of(c * width, 128), width)
                    act(n, [pltpu.make_async_copy(mat[k].at[window], buf.at[n, k], sems.at[n, k]) for k in range(3)], row)

    def begin(n, copies, row):
        for copy in copies:
            copy.start()

    def measure(n, copies, row):
        for copy in copies:
            copy.wait()
        w = buf[n, 0]
        upd = lamb_math(y_refs[n][...], w, buf[n, 1], buf[n, 2], devices)[3] + weight_decay * w
        for at_row, square in ((row, w * w), (row + 4, upd * upd)):
            lanes = jnp.sum(square, axis=0, keepdims=True)
            out_ref[at_row : at_row + 1] += jnp.sum(lanes, axis=1, keepdims=True)

    each(begin)
    each(measure)
    keep_ref[NORM_ROW : NORM_ROW + 8, 0:128] = out_ref[...]
    send_ref[NORM_ROW : NORM_ROW + 8, 0:128] = out_ref[...]


NORM_ROW = 16


def norms_call(meta, sums, plan, shards, regions, rows, devices):
    width = shards[0].shape[1]
    cols = width // 2 if plan else 128
    mats = [array for parts in regions for part in parts for array in part[2]]
    spots = [[part[:2] for part in parts] for parts in regions]
    return pl.pallas_call(
        functools.partial(norms_kernel, spots, rows, plan, len(sums), devices),
        out_shape=(jax.ShapeDtypeStruct((NORM_ROW + 8, cols), F32),) * 2,
        in_specs=[SM] + [VM] * (len(sums) + len(shards)) + [HM] * len(mats),
        out_specs=(VM,) * 2,
        scratch_shapes=[
            pltpu.VMEM((8, 128), F32),
            pltpu.VMEM((len(shards), 3, BLK, width), F32),
            pltpu.SemaphoreType.DMA((len(shards), 3)),
        ],
        cost_estimate=LIGHT,
        compiler_params=pltpu.CompilerParams(vmem_limit_bytes=60 << 20),
        name="norms",
    )(meta, *sums, *shards, *mats)


LAMB_IN = 4
LAMB_OUT = 3


def lamb_kernel(counts, places, rows, lead, n_half, devices, n_alias, meta_ref, slot_ref, total_ref, *refs):
    nbh = sum(counts)
    ys = refs[:n_half]
    ins = refs[n_half : n_half + 6]
    outs = refs[n_half + 6 + n_alias : n_half + 16 + n_alias]
    in_buf, y_buf, out_buf, copy_buf, in_sem, y_sem, out_sem = refs[n_half + 16 + n_alias :]
    bs = in_buf.shape[2]
    width = in_buf.shape[3]
    per = bs // BLK
    steps = nbh * n_half
    half_blk = ys[0].shape[0] // BLK

    def where(i):
        rel, q = i // nbh, i % nbh
        return rel, (rel + lead) ^ meta_ref[1], q

    def window(p, half, q):
        row, col = places[p](half, q - (counts[0] if p else 0))
        return pl.ds(pl.multiple_of(row * bs, bs), bs), pl.ds(pl.multiple_of(col * width, width), width)

    def loads(i, start):
        rel, half, q = where(i)
        b = i % LAMB_IN
        for p in range(2):
            @pl.when((q >= counts[0]) == (p == 1))
            def _(p=p):
                at = window(p, half, q)
                for k in range(3):
                    copy = pltpu.make_async_copy(ins[3 * p + k].at[at], in_buf.at[b, k], in_sem.at[b, k])
                    copy.start() if start else copy.wait()
        for r in range(n_half):
            @pl.when(rel == r)
            def _(r=r):
                for k in range(per):
                    slot = slot_ref[half * half_blk + q * per + k] - (r + lead) * half_blk
                    copy = pltpu.make_async_copy(
                        ys[r].at[pl.ds(pl.multiple_of(slot * BLK, BLK), BLK), :],
                        y_buf.at[b, pl.ds(k * BLK, BLK)], y_sem.at[b, k],
                    )
                    copy.start() if start else copy.wait()

    def stores(i, start):
        _, half, q = where(i)
        b = i % LAMB_OUT
        for p in range(2):
            @pl.when((q >= counts[0]) == (p == 1))
            def _(p=p):
                at = window(p, half, q)
                for k in range(5):
                    src = copy_buf.at[b] if k == 4 else out_buf.at[b, k]
                    copy = pltpu.make_async_copy(src, outs[5 * p + k].at[at], out_sem.at[b, k])
                    copy.start() if start else copy.wait()

    for i in range(LAMB_IN - 1):
        loads(jnp.int32(i), True)

    def step(i, _):
        b, o = i % LAMB_IN, i % LAMB_OUT

        @pl.when(i + LAMB_IN - 1 < steps)
        def _():
            loads(i + LAMB_IN - 1, True)

        loads(i, False)

        @pl.when(i >= LAMB_OUT)
        def _():
            stores(i - LAMB_OUT, False)

        _, _, q = where(i)
        trusts = []
        for row in rows:
            at = NORM_ROW + row
            trusts.append(jnp.sqrt(total_ref[at : at + 1, 0:1]) / jnp.sqrt(total_ref[at + 4 : at + 5, 0:1]))
        trust = jnp.where(q >= counts[0], trusts[1], trusts[0])

        def chunk(c, _):
            at = pl.ds(pl.multiple_of(c * 32, 32), 32)
            w = in_buf[b, 0, at]
            g, first, second, ratio = lamb_math(y_buf[b, at], w, in_buf[b, 1, at], in_buf[b, 2, at], devices)
            weight = w - (matrix_rate * trust) * (ratio + weight_decay * w)
            out_buf[o, 0, at] = g
            out_buf[o, 1, at] = weight
            out_buf[o, 2, at] = first
            out_buf[o, 3, at] = second
            copy_buf[o, at] = weight.astype(BF)
            return 0

        lax.fori_loop(0, bs // 32, chunk, 0)
        stores(i, True)
        return 0

    lax.fori_loop(0, steps, step, 0)
    for i in range(max(0, steps - LAMB_OUT), steps):
        stores(jnp.int32(i), False)


def lamb_call(meta, slots, ys, lead, total, counts, places, rows, mats, bs, devices, before):
    width = ys[0].shape[1]
    flat = [array for mat in mats for array in mat]
    dtypes = (F32, F32, F32, F32, BF)
    out_shape = tuple(jax.ShapeDtypeStruct(mat[0].shape, dt) for mat in mats for dt in dtypes)
    aliased = list(before) if before is not None else []
    aliases = {3 + len(ys) + len(flat) + i: i for i in range(len(aliased))}
    return pl.pallas_call(
        functools.partial(lamb_kernel, counts, places, rows, lead, len(ys), devices, len(aliased)),
        out_shape=out_shape,
        in_specs=[SM, SM, VM] + [HB] * len(ys) + [HM] * (len(flat) + len(aliased)),
        out_specs=(HM,) * len(out_shape),
        scratch_shapes=[
            pltpu.VMEM((LAMB_IN, 3, bs, width), F32),
            pltpu.VMEM((LAMB_IN, bs, width), BF),
            pltpu.VMEM((LAMB_OUT, 4, bs, width), F32),
            pltpu.VMEM((LAMB_OUT, bs, width), BF),
            pltpu.SemaphoreType.DMA((LAMB_IN, 3)),
            pltpu.SemaphoreType.DMA((LAMB_IN, bs // BLK)),
            pltpu.SemaphoreType.DMA((LAMB_OUT, 5)),
        ],
        input_output_aliases=aliases,
        cost_estimate=LIGHT,
        compiler_params=pltpu.CompilerParams(vmem_limit_bytes=60 << 20),
        name="lamb",
    )(meta, slots, total, *ys, *flat, *aliased)


def bits_of(n):
    return n.bit_length() - 1


class Order:

    def __init__(self):
        self.last = None

    def run(self, fn, *args):
        if self.last is not None:
            args, _ = lax.optimization_barrier((args, self.last))
        out = fn(*args)
        leaves = jax.tree.leaves(out)
        self.last = leaves[0]
        return out


def add_bf(a, b):
    return (a.astype(F32) + b.astype(F32)).astype(BF)


def add_split(a, b):
    half = a.shape[0] // 2
    return add_bf(a[:half], b[:half]), add_bf(a[half:], b[half:])


class Exchange:

    def __init__(self, ds):
        self.ds = ds
        self.z, self.d = lax.axis_index("zero"), lax.axis_index("dp")
        self.stages = bits_of(ds)
        order = list(range(self.stages))
        self.orders = [order, [1, 0] + order[2:]]
        lanes = [
            sum((((self.d >> bit) & 1) << (self.stages - 1 - k)) for k, bit in enumerate(order)) for order in self.orders
        ]
        self.mine = jnp.where(self.z == 0, lanes[0], lanes[1]).astype(jnp.int32)
        self.other = jnp.where(self.z == 0, lanes[1], lanes[0]).astype(jnp.int32)
        self.owners = jnp.stack([1 - self.z, self.z]).astype(jnp.int32)
        base = jnp.arange(ds, dtype=jnp.int32)
        self.own_slots = base ^ self.mine
        self.slots = jnp.concatenate([base ^ self.other, self.own_slots])
        self.meta = jnp.stack([self.mine, self.mine >> (self.stages - 1), self.z]).astype(jnp.int32)

    def swap(self, a):
        return lax.ppermute(a, "zero", [(0, 1), (1, 0)])

    def hop(self, a, stage):
        pairs = []
        for d in range(self.ds):
            for c in range(2):
                pairs.append((d * 2 + c, (d ^ (1 << self.orders[c][stage])) * 2 + c))
        return lax.ppermute(a, ("dp", "zero"), pairs)


class Chain:

    def __init__(self, ex, parts):
        self.ex, self.mine, self.stage = ex, parts[1], 0
        self.recv = ex.swap(parts[0])

    def reduce(self, order):
        ex = self.ex
        if self.stage == ex.stages:
            self.shard = self.own = order.run(add_bf, self.mine, self.recv)
            self.recv = ex.hop(self.own, ex.stages - 1)
        else:
            self.mine, send = order.run(add_split, self.mine, self.recv)
            self.recv = ex.hop(send, self.stage)
        self.stage += 1

    def gather(self, order):
        ex = self.ex
        self.own = order.run(lambda a, b: jnp.concatenate([a, b], axis=0), self.own, self.recv)
        self.stage += 1
        self.recv = ex.hop(self.own, 2 * ex.stages - self.stage)


    def step(self, order):
        self.reduce(order) if self.stage <= self.ex.stages else self.gather(order)


class Total:

    def __init__(self, ex, mine, theirs):
        self.ex, self.total, self.stage = ex, mine, 0
        self.recv = ex.swap(theirs)

    def step(self, order):
        self.total = order.run(jnp.add, self.total, self.recv)
        if self.stage < self.ex.stages:
            self.recv = self.ex.hop(self.total, self.stage)
        self.stage += 1


PLAN = (
    "2", "1", "K", "3", "1", "2", "1", "2", "3", "1", "2", "nf",
    "3", "f", "1", "2", "f", "3", "f", "1", "2", "f", "3", "na",
    "2", "f", "3", "a", "L10", "3", "a", "L11", "a", "3", "a", "L20",
    "a", "L21", "L30", "L31",
)


def lamb_moments(gradient, first_old, second_old):
    correction = 1.0 - decay_rate**STEP
    first_new = decay_rate * first_old + (1.0 - decay_rate) * gradient
    second_new = decay_rate * second_old + (1.0 - decay_rate) * gradient * gradient
    direction = first_new / correction / (jnp.sqrt(second_new / correction) + adam_eps)
    return (first_new, second_new, direction)


def low(v):
    return lax.reduce_precision(v, exponent_bits=8, mantissa_bits=7)


def per_device(
    inputs,
    cotangent,
    master_joint,
    master_merge,
    master_expand,
    master_reduce,
    master_vectors,
    moment_joint,
    moment_merge,
    moment_expand,
    moment_reduce,
    moment_vectors,
    square_joint,
    square_merge,
    square_expand,
    square_reduce,
    square_vectors,
):
    zs = lax.axis_size("zero")
    ds = lax.axis_size("dp")
    devices = zs * ds
    width = inputs.shape[1]
    own_rows = master_joint.shape[0]
    ff = master_expand.shape[1]
    per_owner = ff // zs
    halves = 2 if zs == 2 else 1
    per = per_owner // halves
    rbn = own_rows // BLK
    nwr = per // BLK
    ncb = per * zs // width
    fast = zs == 2 and ds & (ds - 1) == 0 and 4 * rbn == ds and nwr + ncb * rbn == ds
    masters = [master_joint, master_merge, master_expand, master_reduce]
    moments = [moment_joint, moment_merge, moment_expand, moment_reduce]
    squares = [square_joint, square_merge, square_expand, square_reduce]
    mats = list(zip(masters, moments, squares))

    if fast:
        ex = Exchange(ds)
        owners, ffn_slots, attn_slots = ex.owners, ex.slots, ex.slots
        pieces = lambda own: [ex.swap(own), own]
    else:
        owners = jnp.arange(zs, dtype=jnp.int32)
        ffn_slots = jnp.tile(jnp.arange(nwr + ncb * rbn, dtype=jnp.int32), zs)
        attn_slots = jnp.tile(jnp.arange(4 * rbn, dtype=jnp.int32), zs)

        def pieces(own):
            full = lax.all_gather(own, "zero", axis=0)
            return [full[i] for i in range(zs)]

    head = jnp.pad(low(master_vectors), ((0, 4), (0, 4 * width - master_vectors.shape[1])))
    attn_own = jnp.concatenate([jnp.concatenate([master_joint, master_merge], axis=1), head], axis=0).astype(BF)
    attn = pieces(attn_own)
    expand = pieces(master_expand.astype(BF))
    reduce = pieces(master_reduce.astype(BF))
    vecs = [piece[own_rows : own_rows + 12, : width // zs].astype(F32) for piece in attn]
    if fast:
        vecs[1] = low(master_vectors)
        vec = jnp.where(ex.z == 0, jnp.concatenate([vecs[1], vecs[0]], 1), jnp.concatenate(vecs, 1))
    else:
        vec = jnp.concatenate(vecs, axis=1)
    bias_up = vec[7:11].reshape(1, ff)

    order = Order()
    normed, joint, mixed, middle, normed_two = order.run(forward_call, owners, inputs, vec, attn)
    res = order.run(
        functools.partial(ffn_call, halves), owners, ffn_slots, normed_two, cotangent, middle, expand, reduce, bias_up, vec
    )
    ffn_grads = [list(res[zs * half : zs * (half + 1)]) for half in range(halves)]
    bias_sums, outputs, middle_grad, merge_grad, ffn_sums = res[zs * halves :]
    chains = [Chain(ex, parts) for parts in ffn_grads] if fast else []
    frames = inputs.shape[0] // FRAME
    if fast:
        chains[0].reduce(order)
    joint_part = order.run(functools.partial(back_first_call, frames=frames), owners, joint, merge_grad, attn)
    if fast:
        chains[1].reduce(order)
        chains[0].reduce(order)
    res = order.run(
        functools.partial(back_second_call, frames=frames),
        owners, attn_slots, normed, mixed, merge_grad, joint, joint_part, attn,
    )
    attn_grads = list(res[:zs])
    joint_grad, attn_sums = res[zs:]
    if fast:
        chains.append(Chain(ex, attn_grads))
    held = {}

    def back_last():
        held["grad"], sums = order.run(back_last_call, owners, inputs, middle_grad, joint_grad, vec, attn)
        return sums

    if not fast:
        last_sums = back_last()
    if fast:
        ffn_one, ffn_two, attn_chain = chains

        def reduce_place(half):
            return lambda lane: (half * nwr + lane // (ds // 2) * (nwr // 2) + jnp.clip(lane % (ds // 2), 0, nwr // 2 - 1), 0)

        def expand_place(half):
            def place(lane):
                q = jnp.clip(lane % (ds // 2) - nwr // 2, 0, ncb * rbn // 2 - 1)
                cb, i = q // (rbn // 2), q % (rbn // 2)
                return lane // (ds // 2) * (rbn // 2) + i, cb * (per_owner // width) + half * (per // width)
            return place

        def joint_place(lane):
            q = jnp.clip(lane % (ds // 2) - rbn // 2, 0, 3 * rbn // 2 - 1)
            return lane // (ds // 2) * (rbn // 2) + q % (rbn // 2), q // (rbn // 2)

        def merge_place(lane):
            return lane // (ds // 2) * (rbn // 2) + jnp.clip(lane % (ds // 2), 0, rbn // 2 - 1), 0

        in_reduce = lambda lane: lane % (ds // 2) < nwr // 2
        in_expand = lambda lane: lane % (ds // 2) >= nwr // 2
        in_merge = lambda lane: lane % (ds // 2) < rbn // 2
        in_joint = lambda lane: lane % (ds // 2) >= rbn // 2
        regions = [
            [(in_merge, merge_place, mats[1]), (in_joint, joint_place, mats[0])],
            [(in_reduce, reduce_place(0), mats[3]), (in_expand, expand_place(0), mats[2])],
            [(in_reduce, reduce_place(1), mats[3]), (in_expand, expand_place(1), mats[2])],
        ]
        bs = 2 * BLK
        count_r = per // bs // 2
        nrb = own_rows // bs // 2

        def lamb_reduce(half):
            return lambda h, q: (half * (per // bs) + h * count_r + q, 0)

        def lamb_expand(half):
            return lambda h, q: (
                h * nrb + q % nrb, q // nrb * (per_owner // width) + half * (per // width)
            )

        lamb_merge = lambda h, q: (h * nrb + q, 0)
        lamb_joint = lambda h, q: (h * nrb + q % nrb, q // nrb)
        state = {"f": None, "a": None}
        sums = {}

        def ffn_lamb(half, lead):
            chain = chains[half]
            state["f"] = order.run(
                lambda meta, slots, y, total, mats, before: lamb_call(
                    meta, slots, [y], lead, total, [count_r, ncb * nrb], [lamb_reduce(half), lamb_expand(half)],
                    [3, 2], mats, bs, devices, before,
                ),
                ex.meta, ex.own_slots, (chain.own, chain.recv)[lead], sums["f"].total, (mats[3], mats[2]), state["f"],
            )

        def attn_lamb(lead):
            state["a"] = order.run(
                lambda meta, slots, y, total, mats, before: lamb_call(
                    meta, slots, [y], lead, total, [nrb, 3 * nrb], [lamb_merge, lamb_joint], [1, 0], mats, bs,
                    devices, before,
                ),
                ex.meta, ex.own_slots, (attn_chain.own, attn_chain.recv)[lead], sums["a"].total, (mats[1], mats[0]),
                state["a"],
            )

        def norms_of(key):
            if key == "f":
                groups, parts, at = (ffn_one, ffn_two), regions[1:], [[3, 2]] * 2
                small = (last_sums, attn_sums, ffn_sums, bias_sums)
                plan = [(0, 0, 0), (0, 1, 0), (1, 1, 0), (1, 2, 0), (1, 0, 0), (2, 0, 0), (2, 1, 0)]
                plan += [(3, k // halves, k % halves * width) for k in range(ff // width)] + [(2, 2, 0)]
            else:
                groups, parts, at, small, plan = (attn_chain,), regions[:1], [[1, 0]], (), []
            keep, send = order.run(
                lambda meta, small, *shards: norms_call(meta, small, plan, shards, parts, at, devices),
                ex.meta, small, *[chain.shard for chain in groups],
            )
            sums[key] = Total(ex, keep, send)

        for act in PLAN:
            if act == "K":
                last_sums = back_last()
            elif act[0] == "n":
                norms_of(act[1])
            elif act in "fa":
                sums[act].step(order)
            elif act in "123":
                chains[int(act) - 1].step(order)
            else:
                stack, lead = int(act[1]), int(act[2])
                attn_lamb(lead) if stack == 3 else ffn_lamb(stack - 1, lead)
        ffn_out, attn_out = state["f"], state["a"]
        vec_total = sums["f"].total[:12]
        norm_values = jnp.sqrt(sums["f"].total[NORM_ROW:, 0] + sums["a"].total[NORM_ROW:, 0])
        outs = [attn_out[5:10], attn_out[0:5], ffn_out[5:10], ffn_out[0:5]]
    else:
        def summed(parts):
            stack = lax.psum_scatter(jnp.concatenate(parts, axis=0), "zero", scatter_dimension=0, tiled=True)
            stack = lax.psum_scatter(stack, "dp", scatter_dimension=0, tiled=True)
            return lax.all_gather(stack, "dp", axis=0, tiled=True).astype(F32) / devices

        def side_by_side(stack):
            return stack.reshape(-1, own_rows, width).transpose(1, 0, 2).reshape(own_rows, -1)

        ffn = summed(ffn_grads[0])
        attn_sum = summed(attn_grads)
        grads = [
            side_by_side(attn_sum[own_rows:]), attn_sum[:own_rows], side_by_side(ffn[per:]), ffn[:per]
        ]
        rows = jnp.concatenate(
            [
                last_sums[0:2],
                attn_sums[1:3],
                attn_sums[0:1],
                ffn_sums[0:2],
                bias_sums.reshape(ff // width, width),
                ffn_sums[2:3],
            ],
            axis=0,
        )
        blocks = rows.reshape(12, zs, width // zs).transpose(1, 0, 2)
        vec_total = lax.psum(lax.psum_scatter(blocks, "zero", scatter_dimension=0, tiled=True)[0], "dp")
        moved = [lamb_moments(g, m, s) for g, m, s in zip(grads, moments, squares)]
        upds = [move[2] + weight_decay * w for move, w in zip(moved, masters)]
        local = jnp.stack([jnp.sum(w * w) for w in masters] + [jnp.sum(u * u) for u in upds])
        norm_values = jnp.sqrt(lax.psum(local, "zero"))
        outs = []
        for k in range(4):
            weight = masters[k] - matrix_rate * (norm_values[k] / norm_values[k + 4]) * upds[k]
            outs.append((grads[k], weight, moved[k][0], moved[k][1], weight.astype(BF)))

    grad_vec = vec_total / devices
    first_vec, second_vec, vec_direction = lamb_moments(grad_vec, moment_vectors, square_vectors)
    new_vectors = master_vectors - vector_rate * vec_direction
    vector_out = (grad_vec, new_vectors, first_vec, second_vec, new_vectors.astype(BF))
    result = [outputs, held["grad"]]
    for k in range(5):
        result += [out[k] for out in outs] + [vector_out[k]]
    return (*result, norm_values)


def solution(mesh):
    tokens = P(("dp", "zero"), None)
    matrix = P("zero", None)
    vector = P(None, "zero")
    five = (matrix,) * 4 + (vector,)
    return jax.shard_map(
        per_device,
        mesh=mesh,
        in_specs=(tokens, tokens) + five * 3,
        out_specs=(tokens, tokens) + five * 5 + (P(),),
        check_vma=False,
    )
```

```python
import functools

import jax
import jax.numpy as jnp
from jax import lax
from jax.experimental import pallas as pl
from jax.experimental.pallas import tpu as pltpu
from jax.sharding import PartitionSpec as P

HD = 64
FRAME = 196
STEP = 4
BLK = 96

norm_eps = 1e-06
adam_eps = 1e-06
decay_rate = 0.5
weight_decay = 0.01
matrix_rate = 0.5
vector_rate = 0.1
BF = jnp.bfloat16
F32 = jnp.float32
VM = pl.BlockSpec(memory_space=pltpu.VMEM)
SM = pl.BlockSpec(memory_space=pltpu.SMEM)
HB = pl.BlockSpec(memory_space=pl.ANY)
HM = pl.BlockSpec(memory_space=pltpu.HBM)
HEAVY = pl.CostEstimate(flops=5 * 10**10, bytes_accessed=10**8, transcendentals=0)
LIGHT = pl.CostEstimate(flops=1000, bytes_accessed=1000, transcendentals=0)
INV_SQRT2 = 0.7071067811865476
INV_SQRT2PI = 0.3989422804014327


def padded_rows(rows):
    return (rows + 15) // 16 * 16


def row_chunks(rows):
    edges = list(range(0, rows, 192))
    if rows - edges[-1] < 96 and len(edges) > 1:
        edges.pop()
    return [(s, (edges[i + 1] if i + 1 < len(edges) else rows) - s) for i, s in enumerate(edges)]


def row_halves(zs):
    return 2 if zs == 2 else 1


def dot_nn(a, b):
    return lax.dot_general(a, b, (((1,), (0,)), ((), ())), preferred_element_type=F32)


def dot_nt(a, b):
    return lax.dot_general(a, b, (((1,), (1,)), ((), ())), preferred_element_type=F32)


def dot_tn(a, b):
    return lax.dot_general(a, b, (((0,), (0,)), ((), ())), preferred_element_type=F32)


def stats(v):
    mean = jnp.mean(v, axis=-1, keepdims=True)
    c = v - mean
    r = lax.rsqrt(jnp.mean(c * c, axis=-1, keepdims=True) + norm_eps)
    return c * r, r


def piece_copies(own_ref, pieces, w_ref, sems, width):
    own_rows = width // len(pieces)
    copies = []
    for col, (first, count) in enumerate(((0, 3 * width), (3 * width, width))):
        cols = pl.ds(first, count)
        for kk, piece in enumerate(pieces):
            rws = pl.ds(pl.multiple_of(own_ref[kk] * own_rows, own_rows), own_rows)
            copies.append(
                pltpu.make_async_copy(
                    piece.at[pl.ds(0, own_rows), cols], w_ref.at[rws, cols], sems.at[col, kk]
                )
            )
    return copies[: len(pieces)], copies[len(pieces) :]


def forward_kernel(zs, own_ref, x_ref, vec_ref, *refs):
    pieces = refs[:zs]
    a_ref, j_ref, o_ref, h_ref, b_ref, w_ref, sems = refs[zs:]
    rows, width = x_ref.shape
    joint_in, merge_in = piece_copies(own_ref, pieces, w_ref, sems, width)
    for copy in joint_in + merge_in:
        copy.start()
    pad = a_ref.shape[0]
    frames = rows // FRAME
    heads = width // HD
    win = (FRAME + 12 + 15) // 16 * 16
    scale = HD ** (-0.5)
    tail = pad - 16
    a_ref[tail:pad] = jnp.zeros((16, width), BF)
    o_ref[tail:pad] = jnp.zeros((16, width), BF)
    for s, n in row_chunks(rows):
        norm, _ = stats(x_ref[s : s + n].astype(F32))
        a_ref[s : s + n] = (norm * (1.0 + vec_ref[0:1]) + vec_ref[1:2]).astype(BF)
    for copy in joint_in:
        copy.wait()
    step = 256

    def joint_cols(c, _):
        cols = pl.ds(pl.multiple_of(c * step, step), step)
        per = width // step
        which = c // per
        lane = pl.ds(pl.multiple_of((c % per) * step, step), step)
        row = jnp.where(which == 0, vec_ref[2:3, lane], jnp.where(which == 2, vec_ref[3:4, lane], 0.0))
        j_ref[:, cols] = (dot_nn(a_ref[...], w_ref[:, cols]) + row).astype(BF)
        return 0

    lax.fori_loop(0, 3 * width // step, joint_cols, 0)
    key_at = lax.broadcasted_iota(jnp.int32, (win, win), 1)
    row_at = lax.broadcasted_iota(jnp.int32, (win, 2 * HD), 0)
    low = lax.broadcasted_iota(jnp.int32, (win, 2 * HD), 1) < HD

    def frame_body(f, _):
        start = pl.multiple_of((f * FRAME) // 16 * 16, 16)
        off = f * FRAME - start
        rws = pl.ds(start, win)
        keep = (key_at >= off) & (key_at < off + FRAME)
        rkeep = (row_at >= off) & (row_at < off + FRAME)
        for p in range(heads // 2):
            q2 = j_ref[rws, 2 * HD * p : 2 * HD * (p + 1)]
            k2 = j_ref[rws, width + 2 * HD * p : width + 2 * HD * (p + 1)]
            v2 = j_ref[rws, 2 * width + 2 * HD * p : 2 * width + 2 * HD * (p + 1)]
            parts = []
            for side in range(2):
                qs = jnp.where(low if side == 0 else jnp.logical_not(low), q2, jnp.zeros_like(q2))
                sc = jnp.where(keep, dot_nt(qs, k2) * scale, -1e30)
                e = jnp.exp(sc - jnp.max(sc, axis=-1, keepdims=True))
                pb = (e / jnp.sum(e, axis=-1, keepdims=True)).astype(BF)
                parts.append(dot_nn(pb, v2))
            o2 = jnp.where(low, parts[0], parts[1])
            sl = slice(2 * HD * p, 2 * HD * (p + 1))
            o_ref[rws, sl] = jnp.where(rkeep, o2, o_ref[rws, sl].astype(F32)).astype(BF)
        return 0

    lax.fori_loop(0, frames, frame_body, 0)
    for copy in merge_in:
        copy.wait()
    for s, n in row_chunks(rows):
        m = n if s + n < rows else pad - s
        hv = dot_nn(o_ref[s : s + m], w_ref[:, 3 * width :]) + vec_ref[4:5]
        hv = hv[:n] + x_ref[s : s + n].astype(F32)
        norm, _ = stats(hv)
        h_ref[s : s + n] = hv
        bv = (norm * (1.0 + vec_ref[5:6]) + vec_ref[6:7]).astype(BF)
        if m != n:
            h_ref[tail:pad] = jnp.zeros((16, width), F32)
            b_ref[tail:pad] = jnp.zeros((16, width), BF)
            h_ref[s : s + n] = hv
        b_ref[s : s + n] = bv


def forward_call(owners, x, vec, pieces):
    rows, width = x.shape
    pad = padded_rows(rows)
    zs = len(pieces)
    return pl.pallas_call(
        functools.partial(forward_kernel, zs),
        out_shape=(
            jax.ShapeDtypeStruct((pad, width), BF),
            jax.ShapeDtypeStruct((pad, 3 * width), BF),
            jax.ShapeDtypeStruct((pad, width), BF),
            jax.ShapeDtypeStruct((pad, width), F32),
            jax.ShapeDtypeStruct((pad, width), BF),
        ),
        in_specs=[SM, VM, VM] + [HB] * zs,
        out_specs=(VM,) * 5,
        scratch_shapes=[pltpu.VMEM((width, 4 * width), BF), pltpu.SemaphoreType.DMA((2, zs))],
        cost_estimate=LIGHT,
        compiler_params=pltpu.CompilerParams(vmem_limit_bytes=24 << 20),
        name="forward_attention",
    )(owners, x, vec, *pieces)


def gelu_parts(u):
    phi = 0.5 * (1.0 + lax.erf(u * INV_SQRT2))
    return u * phi, phi + u * (jnp.exp(u * u * -0.5) * INV_SQRT2PI)


def ffn_kernel(zs, tiles, own_ref, slot_ref, *refs):
    refs = list(refs)
    b_ref, e_ref, h_ref = refs[:3]
    we_in = refs[3 : 3 + zs]
    wr_in = refs[3 + zs : 3 + 2 * zs]
    bu_ref, vec_ref = refs[3 + 2 * zs : 5 + 2 * zs]
    refs = refs[5 + 2 * zs :]
    g_refs = [[refs.pop(0) for _ in range(zs)] for _ in range(tiles)]
    bug_ref, out_ref, dh_ref, dz_ref, sums_ref = refs[:5]
    es_ref, bt_ref, gs_ref, du_ref, we_bufs, wr_bufs, acc_ref, db_ref, sems = refs[5:]
    rows, width = e_ref.shape
    pad = b_ref.shape[0]
    tf = we_bufs.shape[2]
    k, t = pl.program_id(0), pl.program_id(1)
    own_rows = width // zs
    now = k * tiles + t

    def weights(n, start):
        nk, nt = n // tiles, n % tiles
        buf = n % 2
        cols = pl.ds(pl.multiple_of((own_ref[nk] * tiles + nt) * tf, 128), tf)
        for kk in range(zs):
            rws = pl.ds(pl.multiple_of(own_ref[kk] * own_rows, own_rows), own_rows)
            copy = pltpu.make_async_copy(we_in[kk].at[:, cols], we_bufs.at[buf, rws], sems.at[buf, kk])
            copy.start() if start else copy.wait()

            @pl.when(nk == kk)
            def _(kk=kk):
                rows_in = pl.ds(pl.multiple_of(nt * tf, 16), tf)
                copy = pltpu.make_async_copy(wr_in[kk].at[rows_in, :], wr_bufs.at[buf], sems.at[buf, zs])
                copy.start() if start else copy.wait()

    @pl.when(now == 0)
    def _():
        weights(now, True)

    @pl.when(now + 1 < zs * tiles)
    def _():
        weights(now + 1, True)

    nh = row_halves(zs)
    nwr = tf // BLK
    rbn = own_rows // BLK
    nblk = nwr + (tf * zs // width) * rbn
    chunk = [(0, 256), (256, 256), (512, 256), (768, pad - 768)] if pad == 992 else [(0, pad)]

    @pl.when(jnp.logical_and(k == 0, t == 0))
    def _():
        es_ref[pad - 16 : pad] = jnp.zeros((16, width), BF)
        es_ref[0:rows] = e_ref[...]
        for c in range(0, width, 256):
            bt_ref[c : c + 256, :] = b_ref[:, c : c + 256].T
        acc_ref[...] = jnp.zeros_like(acc_ref)
        db_ref[...] = jnp.zeros_like(db_ref)

    weights(now, False)
    we_ref, wr_ref = we_bufs.at[now % 2], wr_bufs.at[now % 2]
    total = jnp.zeros((1, tf), F32)
    for s, n in chunk:
        u = dot_nn(b_ref[s : s + n], we_ref[...]) + bu_ref[...]
        g, d = gelu_parts(u)
        gs_ref[s : s + n] = g.astype(BF)
        du = (dot_nt(es_ref[s : s + n], wr_ref[...]) * d).astype(BF)
        du_ref[s : s + n] = du
        total = total + jnp.sum(du.astype(F32), axis=0, keepdims=True)
    owner = own_ref[k]
    bug_ref[pl.ds(owner, 1), pl.ds(pl.multiple_of(t * tf, 128), tf)] = total
    acc_ref[...] += dot_nn(gs_ref[...], wr_ref[...])
    db_ref[...] += dot_nt(du_ref[...], we_ref[...])
    gwr = dot_tn(gs_ref[...], es_ref[...]).astype(BF)
    for tt in range(tiles):
        for kk in range(zs):
            @pl.when((k == kk) & (t == tt))
            def _(kk=kk, tt=tt):
                for i in range(nwr):
                    slot = slot_ref[kk * nblk + i // (nwr // nh) * (nblk // nh) + i % (nwr // nh)]
                    g_refs[tt][kk][pl.ds(pl.multiple_of(slot * BLK, BLK), BLK), :] = gwr[i * BLK : (i + 1) * BLK]
    col = owner * tf
    cb = col // width
    lane = pl.ds(pl.multiple_of(col % width, 128), tf)
    part = rbn // nh
    for kk in range(zs):
        rws = pl.ds(pl.multiple_of(own_ref[kk] * own_rows, own_rows), own_rows)
        gwe = dot_nn(bt_ref[rws, :], du_ref[...]).astype(BF)
        for tt in range(tiles):
            @pl.when(t == tt)
            def _(kk=kk, tt=tt, gwe=gwe):
                for i in range(rbn):
                    slot = slot_ref[kk * nblk + i // part * (nblk // nh) + nwr // nh + cb * part + i % part]
                    g_refs[tt][kk][pl.ds(pl.multiple_of(slot * BLK, BLK), BLK), lane] = gwe[i * BLK : (i + 1) * BLK]

    @pl.when(jnp.logical_and(k == zs - 1, t == tiles - 1))
    def _():
        da = jnp.zeros((1, width), F32)
        dc = jnp.zeros((1, width), F32)
        de = jnp.zeros((1, width), F32)
        for s, n in chunk:
            hv = h_ref[s : s + n]
            norm, r = stats(hv)
            db = db_ref[s : s + n]
            da = da + jnp.sum(db * norm, axis=0, keepdims=True)
            dc = dc + jnp.sum(db, axis=0, keepdims=True)
            g = db * (1.0 + vec_ref[5:6])
            ev = es_ref[s : s + n].astype(F32)
            de = de + jnp.sum(ev, axis=0, keepdims=True)
            dh = ev + r * (
                g - jnp.mean(g, axis=-1, keepdims=True) - norm * jnp.mean(g * norm, axis=-1, keepdims=True)
            )
            dh_ref[s : s + n] = dh
            dz_ref[s : s + n] = dh.astype(BF)
            ov = (hv + (acc_ref[s : s + n] + vec_ref[11:12])).astype(BF)
            m = min(n, rows - s)
            out_ref[s : s + m] = ov[:m]
        sums_ref[0:1] = da
        sums_ref[1:2] = dc
        sums_ref[2:3] = de


def ffn_call(tiles, owners, slots, b, e, h, we, wr, bu, vec):
    zs = owners.shape[0]
    pad, width = b.shape
    rows = e.shape[0]
    per_owner = we[0].shape[1] // zs
    tf = per_owner // tiles
    nrow = tf + tf * zs // width * (width // zs)

    def ffcol(k, t, own, sl):
        return own[k] * tiles + t

    in_specs = [
        VM,
        VM,
        VM,
        *[HB] * (2 * zs),
        pl.BlockSpec((1, tf), lambda k, t, own, sl: (0, ffcol(k, t, own, sl))),
        VM,
    ]
    outs = [jax.ShapeDtypeStruct((nrow, width), BF)] * (zs * tiles) + [
        jax.ShapeDtypeStruct((zs, per_owner), F32),
        jax.ShapeDtypeStruct((rows, width), BF),
        jax.ShapeDtypeStruct((pad, width), F32),
        jax.ShapeDtypeStruct((pad, width), BF),
        jax.ShapeDtypeStruct((8, width), F32),
    ]
    return pl.pallas_call(
        functools.partial(ffn_kernel, zs, tiles),
        out_shape=tuple(outs),
        grid_spec=pltpu.PrefetchScalarGridSpec(
            num_scalar_prefetch=2,
            grid=(zs, tiles),
            in_specs=in_specs,
            out_specs=(VM,) * len(outs),
            scratch_shapes=[
                pltpu.VMEM((pad, width), BF),
                pltpu.VMEM((width, pad), BF),
                pltpu.VMEM((pad, tf), BF),
                pltpu.VMEM((pad, tf), BF),
                pltpu.VMEM((2, width, tf), BF),
                pltpu.VMEM((2, tf, width), BF),
                pltpu.VMEM((pad, width), F32),
                pltpu.VMEM((pad, width), F32),
                pltpu.SemaphoreType.DMA((2, zs + 1)),
            ],
        ),
        cost_estimate=LIGHT,
        compiler_params=pltpu.CompilerParams(vmem_limit_bytes=FFN_MB << 20),
        name="ffn",
    )(owners, slots, b, e, h, *we, *wr, bu, vec)


FFN_MB = 33


def first_frames(frames):
    return (frames + 1) // 2


def attend_back(lo, hi, base, j_ref, do_ref, dj_ref, dj_base, width):
    win = (FRAME + 12 + 15) // 16 * 16
    scale = HD ** (-0.5)
    key_at = lax.broadcasted_iota(jnp.int32, (win, win), 0)
    qry_at = lax.broadcasted_iota(jnp.int32, (win, win), 1)
    low_side = lax.broadcasted_iota(jnp.int32, (win, 2 * HD), 1) < HD

    def frame_body(f, _):
        start = (f * FRAME) // 16 * 16
        off = f * FRAME - start
        rws = pl.ds(pl.multiple_of(start - base, 16), win)
        drws = pl.ds(pl.multiple_of(start - dj_base, 16), win)
        kkeep = (key_at >= off) & (key_at < off + FRAME)
        keep = kkeep & (qry_at >= off) & (qry_at < off + FRAME)
        for p in range(width // HD // 2):
            sl = [slice(w * width + 2 * HD * p, w * width + 2 * HD * (p + 1)) for w in range(3)]
            q2, k2, v2 = (j_ref[rws, sl[w]] for w in range(3))
            do2 = do_ref[rws, sl[0]]
            res = []
            for side in range(2):
                m = low_side if side == 0 else jnp.logical_not(low_side)
                zero = jnp.zeros_like(k2)
                sc = jnp.where(kkeep, dot_nt(jnp.where(m, k2, zero), q2) * scale, -1e30)
                e = jnp.exp(sc - jnp.max(sc, axis=0, keepdims=True))
                pt = jnp.where(keep, e / jnp.sum(e, axis=0, keepdims=True), 0.0)
                dp = dot_nt(jnp.where(m, v2, zero), do2)
                ds = (pt * (dp - jnp.sum(pt * dp, axis=0, keepdims=True))).astype(BF)
                res.append((dot_tn(ds, k2) * scale, dot_nn(ds, q2) * scale, dot_nn(pt.astype(BF), do2)))
            for w in range(3):
                val = jnp.where(low_side, res[0][w], res[1][w])
                dj_ref[drws, sl[w]] = (dj_ref[drws, sl[w]].astype(F32) + val).astype(BF)
        return 0

    lax.fori_loop(lo, hi, frame_body, 0)


def merge_copies(own_ref, pieces, w_ref, sems, width, first, count):
    own_rows = width // len(pieces)
    copies = []
    for kk, piece in enumerate(pieces):
        rws = pl.ds(pl.multiple_of(own_ref[kk] * own_rows, own_rows), own_rows)
        copies.append(
            pltpu.make_async_copy(piece.at[pl.ds(0, own_rows), pl.ds(first, count)], w_ref.at[rws, :], sems.at[kk])
        )
    return copies


def back_first_kernel(zs, frames, own_ref, j_ref, dz_ref, *refs):
    pieces = refs[:zs]
    dj_ref, do_ref, w_ref, sems = refs[zs:]
    width = dz_ref.shape[1]
    copies = merge_copies(own_ref, pieces, w_ref, sems, width, 3 * width, width)
    for copy in copies:
        copy.start()
    dj_ref[...] = jnp.zeros_like(dj_ref)
    for copy in copies:
        copy.wait()
    do_ref[...] = dot_nt(dz_ref[...], w_ref[...]).astype(BF)
    attend_back(0, first_frames(frames), 0, j_ref, do_ref, dj_ref, 0, width)


def back_first_call(owners, j, dz, pieces, frames):
    zs = len(pieces)
    width = dz.shape[1]
    last = first_frames(frames) - 1
    rows = (last * FRAME) // 16 * 16 + (FRAME + 12 + 15) // 16 * 16
    return pl.pallas_call(
        functools.partial(back_first_kernel, zs, frames),
        grid=(1,),
        out_shape=jax.ShapeDtypeStruct((rows, 3 * width), BF),
        in_specs=[
            SM,
            pl.BlockSpec((rows, 3 * width), lambda i: (0, 0)),
            pl.BlockSpec((rows, width), lambda i: (0, 0)),
        ]
        + [HB] * zs,
        out_specs=pl.BlockSpec((rows, 3 * width), lambda i: (0, 0)),
        scratch_shapes=[
            pltpu.VMEM((rows, width), BF),
            pltpu.VMEM((width, width), BF),
            pltpu.SemaphoreType.DMA((zs,)),
        ],
        cost_estimate=LIGHT,
        compiler_params=pltpu.CompilerParams(vmem_limit_bytes=20 << 20),
        name="back_first",
    )(owners, j, dz, *pieces)


def back_second_kernel(zs, frames, own_ref, slot_ref, a_ref, o_ref, dz_ref, j_hbm, djp_hbm, *refs):
    pieces = refs[:zs]
    g_refs = refs[zs : 2 * zs]
    dj_ref, sums_ref, j_ref, do_ref, t_ref, w_ref, sems, more = refs[2 * zs :]
    pad, width = a_ref.shape
    done = djp_hbm.shape[0]
    base = (first_frames(frames) * FRAME) // 16 * 16
    own_rows = width // zs
    rbn = own_rows // BLK
    copies = merge_copies(own_ref, pieces, w_ref, sems, width, 3 * width, width)
    copies.append(pltpu.make_async_copy(j_hbm.at[pl.ds(base, pad - base), :], j_ref, more.at[0]))
    earlier = pltpu.make_async_copy(djp_hbm, dj_ref.at[pl.ds(0, done), :], more.at[1])
    for copy in copies:
        copy.start()
    earlier.start()
    dj_ref[done:pad] = jnp.zeros((pad - done, 3 * width), BF)
    sums_ref[...] = jnp.zeros_like(sums_ref)
    for c in range(0, width, 256):
        t_ref[c : c + 256, :] = o_ref[:, c : c + 256].T
    sums_ref[0:1] = jnp.sum(dz_ref[...].astype(F32), axis=0, keepdims=True)
    part = rbn // row_halves(zs)

    def put(kk, region, i, val):
        slot = slot_ref[kk * 4 * rbn + i // part * (4 * part) + region * part + i % part]
        g_refs[kk][pl.ds(pl.multiple_of(slot * BLK, BLK), BLK), :] = val

    for kk in range(zs):
        rws = pl.ds(pl.multiple_of(own_ref[kk] * own_rows, own_rows), own_rows)
        gm = dot_nn(t_ref[rws, :], dz_ref[...]).astype(BF)
        for i in range(rbn):
            put(kk, 0, i, gm[i * BLK : (i + 1) * BLK])
    for copy in copies:
        copy.wait()
    do_ref[...] = dot_nt(dz_ref[base:pad], w_ref[...]).astype(BF)
    earlier.wait()
    attend_back(first_frames(frames), frames, base, j_ref, do_ref, dj_ref, 0, width)
    for c in range(0, width, 256):
        t_ref[c : c + 256, :] = a_ref[:, c : c + 256].T
    for w in range(3):
        cols = slice(w * width, (w + 1) * width)
        if w != 1:
            row = 1 if w == 0 else 2
            sums_ref[row : row + 1] = jnp.sum(dj_ref[:, cols].astype(F32), axis=0, keepdims=True)
        for kk in range(zs):
            rws = pl.ds(pl.multiple_of(own_ref[kk] * own_rows, own_rows), own_rows)
            gj = dot_nn(t_ref[rws, :], dj_ref[:, cols]).astype(BF)
            for i in range(rbn):
                put(kk, 1 + w, i, gj[i * BLK : (i + 1) * BLK])


def back_second_call(owners, slots, a, o, dz, j, dj_part, pieces, frames):
    zs = len(pieces)
    pad, width = a.shape
    base = (first_frames(frames) * FRAME) // 16 * 16
    nrow = 4 * (width // zs)
    return pl.pallas_call(
        functools.partial(back_second_kernel, zs, frames),
        out_shape=(jax.ShapeDtypeStruct((nrow, width), BF),) * zs
        + (jax.ShapeDtypeStruct((pad, 3 * width), BF), jax.ShapeDtypeStruct((8, width), F32)),
        in_specs=[SM] * 2 + [VM] * 3 + [HB] * (2 + zs),
        out_specs=(VM,) * (zs + 2),
        scratch_shapes=[
            pltpu.VMEM((pad - base, 3 * width), BF),
            pltpu.VMEM((pad - base, width), BF),
            pltpu.VMEM((width, pad), BF),
            pltpu.VMEM((width, width), BF),
            pltpu.SemaphoreType.DMA((zs,)),
            pltpu.SemaphoreType.DMA((2,)),
        ],
        cost_estimate=LIGHT,
        compiler_params=pltpu.CompilerParams(vmem_limit_bytes=26 << 20),
        name="back_second",
    )(owners, slots, a, o, dz, j, dj_part, *pieces)


def back_last_kernel(zs, own_ref, x_ref, dh_ref, dj_ref, vec_ref, *refs):
    pieces = refs[:zs]
    ig_ref, sums_ref, w_ref, sems = refs[zs:]
    rows, width = x_ref.shape
    pad = dj_ref.shape[0]
    copies = merge_copies(own_ref, pieces, w_ref, sems, width, 0, 3 * width)
    for copy in copies:
        copy.start()
    sums_ref[...] = jnp.zeros_like(sums_ref)
    for copy in copies:
        copy.wait()
    chunk = [(0, 256), (256, 256), (512, 256), (768, pad - 768)] if pad == 992 else [(0, pad)]
    da = jnp.zeros((1, width), F32)
    dc = jnp.zeros((1, width), F32)
    for s, n in chunk:
        m = min(n, rows - s)
        dv = dot_nt(dj_ref[s : s + n], w_ref[...])[:m]
        norm, r = stats(x_ref[s : s + m].astype(F32))
        da = da + jnp.sum(dv * norm, axis=0, keepdims=True)
        dc = dc + jnp.sum(dv, axis=0, keepdims=True)
        g = dv * (1.0 + vec_ref[0:1])
        ig_ref[s : s + m] = dh_ref[s : s + m] + r * (
            g - jnp.mean(g, axis=-1, keepdims=True) - norm * jnp.mean(g * norm, axis=-1, keepdims=True)
        )
    sums_ref[0:1] = da
    sums_ref[1:2] = dc


def back_last_call(owners, x, dh, dj, vec, pieces):
    zs = len(pieces)
    rows, width = x.shape
    return pl.pallas_call(
        functools.partial(back_last_kernel, zs),
        out_shape=(jax.ShapeDtypeStruct((rows, width), F32), jax.ShapeDtypeStruct((8, width), F32)),
        in_specs=[SM] + [VM] * 4 + [HB] * zs,
        out_specs=(VM,) * 2,
        scratch_shapes=[pltpu.VMEM((width, 3 * width), BF), pltpu.SemaphoreType.DMA((zs,))],
        cost_estimate=HEAVY,
        compiler_params=pltpu.CompilerParams(vmem_limit_bytes=18 << 20),
        name="back_last",
    )(owners, x, dh, dj, vec, *pieces)


def lamb_math(g, w, m, s, devices):
    scale = 1.0 / (1.0 - decay_rate**STEP)
    g = g.astype(F32) * (1.0 / devices)
    first = decay_rate * m + (1.0 - decay_rate) * g
    second = decay_rate * s + (1.0 - decay_rate) * g * g
    ratio = (first * scale) / (jnp.sqrt(second * scale) + adam_eps)
    return g, first, second, ratio


def norms_kernel(spots, rows, plan, n_sums, devices, meta_ref, *refs):
    sums = refs[:n_sums]
    y_refs = refs[n_sums : n_sums + len(spots)]
    mats = refs[n_sums + len(spots) : -5]
    keep_ref, send_ref, out_ref, buf, sems = refs[-5:]
    lane = meta_ref[0]
    half = keep_ref.shape[1]
    out_ref[...] = jnp.zeros_like(out_ref)
    keep_ref[...] = jnp.zeros_like(keep_ref)
    send_ref[...] = jnp.zeros_like(send_ref)
    for row, (k, source, first) in enumerate(plan):
        for target, side in ((keep_ref, meta_ref[2]), (send_ref, 1 - meta_ref[2])):
            cols = pl.ds(pl.multiple_of(first + side * half, 128), half)
            target[row : row + 1] = sums[k][source : source + 1, cols]
    width = y_refs[0].shape[1]

    def each(act):
        at = 0
        for n, (regions, places) in enumerate(zip(spots, rows)):
            for (inside, place), row in zip(regions, places):
                mat = mats[at : at + 3]
                at += 3

                @pl.when(inside(lane))
                def _(n=n, place=place, mat=mat, row=row):
                    r, c = place(lane)
                    window = pl.ds(pl.multiple_of(r * BLK, 32), BLK), pl.ds(pl.multiple_of(c * width, 128), width)
                    act(n, [pltpu.make_async_copy(mat[k].at[window], buf.at[n, k], sems.at[n, k]) for k in range(3)], row)

    def begin(n, copies, row):
        for copy in copies:
            copy.start()

    def measure(n, copies, row):
        for copy in copies:
            copy.wait()
        w = buf[n, 0]
        upd = lamb_math(y_refs[n][...], w, buf[n, 1], buf[n, 2], devices)[3] + weight_decay * w
        for at_row, square in ((row, w * w), (row + 4, upd * upd)):
            lanes = jnp.sum(square, axis=0, keepdims=True)
            out_ref[at_row : at_row + 1] += jnp.sum(lanes, axis=1, keepdims=True)

    each(begin)
    each(measure)
    keep_ref[NORM_ROW : NORM_ROW + 8, 0:128] = out_ref[...]
    send_ref[NORM_ROW : NORM_ROW + 8, 0:128] = out_ref[...]


NORM_ROW = 16


def norms_call(meta, sums, plan, shards, regions, rows, devices):
    width = shards[0].shape[1]
    cols = width // 2 if plan else 128
    mats = [array for parts in regions for part in parts for array in part[2]]
    spots = [[part[:2] for part in parts] for parts in regions]
    return pl.pallas_call(
        functools.partial(norms_kernel, spots, rows, plan, len(sums), devices),
        out_shape=(jax.ShapeDtypeStruct((NORM_ROW + 8, cols), F32),) * 2,
        in_specs=[SM] + [VM] * (len(sums) + len(shards)) + [HM] * len(mats),
        out_specs=(VM,) * 2,
        scratch_shapes=[
            pltpu.VMEM((8, 128), F32),
            pltpu.VMEM((len(shards), 3, BLK, width), F32),
            pltpu.SemaphoreType.DMA((len(shards), 3)),
        ],
        cost_estimate=LIGHT,
        compiler_params=pltpu.CompilerParams(vmem_limit_bytes=60 << 20),
        name="norms",
    )(meta, *sums, *shards, *mats)


LAMB_IN = 4
LAMB_OUT = 3


def lamb_kernel(counts, places, rows, lead, n_half, devices, n_alias, meta_ref, slot_ref, total_ref, *refs):
    nbh = sum(counts)
    ys = refs[:n_half]
    ins = refs[n_half : n_half + 6]
    outs = refs[n_half + 6 + n_alias : n_half + 16 + n_alias]
    in_buf, y_buf, out_buf, copy_buf, in_sem, y_sem, out_sem = refs[n_half + 16 + n_alias :]
    bs = in_buf.shape[2]
    width = in_buf.shape[3]
    per = bs // BLK
    steps = nbh * n_half
    half_blk = ys[0].shape[0] // BLK

    def where(i):
        rel, q = i // nbh, i % nbh
        return rel, (rel + lead) ^ meta_ref[1], q

    def window(p, half, q):
        row, col = places[p](half, q - (counts[0] if p else 0))
        return pl.ds(pl.multiple_of(row * bs, bs), bs), pl.ds(pl.multiple_of(col * width, width), width)

    def loads(i, start):
        rel, half, q = where(i)
        b = i % LAMB_IN
        for p in range(2):
            @pl.when((q >= counts[0]) == (p == 1))
            def _(p=p):
                at = window(p, half, q)
                for k in range(3):
                    copy = pltpu.make_async_copy(ins[3 * p + k].at[at], in_buf.at[b, k], in_sem.at[b, k])
                    copy.start() if start else copy.wait()
        for r in range(n_half):
            @pl.when(rel == r)
            def _(r=r):
                for k in range(per):
                    slot = slot_ref[half * half_blk + q * per + k] - (r + lead) * half_blk
                    copy = pltpu.make_async_copy(
                        ys[r].at[pl.ds(pl.multiple_of(slot * BLK, BLK), BLK), :],
                        y_buf.at[b, pl.ds(k * BLK, BLK)], y_sem.at[b, k],
                    )
                    copy.start() if start else copy.wait()

    def stores(i, start):
        _, half, q = where(i)
        b = i % LAMB_OUT
        for p in range(2):
            @pl.when((q >= counts[0]) == (p == 1))
            def _(p=p):
                at = window(p, half, q)
                for k in range(5):
                    src = copy_buf.at[b] if k == 4 else out_buf.at[b, k]
                    copy = pltpu.make_async_copy(src, outs[5 * p + k].at[at], out_sem.at[b, k])
                    copy.start() if start else copy.wait()

    for i in range(LAMB_IN - 1):
        loads(jnp.int32(i), True)

    def step(i, _):
        b, o = i % LAMB_IN, i % LAMB_OUT

        @pl.when(i + LAMB_IN - 1 < steps)
        def _():
            loads(i + LAMB_IN - 1, True)

        loads(i, False)

        @pl.when(i >= LAMB_OUT)
        def _():
            stores(i - LAMB_OUT, False)

        _, _, q = where(i)
        trusts = []
        for row in rows:
            at = NORM_ROW + row
            trusts.append(jnp.sqrt(total_ref[at : at + 1, 0:1]) / jnp.sqrt(total_ref[at + 4 : at + 5, 0:1]))
        trust = jnp.where(q >= counts[0], trusts[1], trusts[0])

        def chunk(c, _):
            at = pl.ds(pl.multiple_of(c * 32, 32), 32)
            w = in_buf[b, 0, at]
            g, first, second, ratio = lamb_math(y_buf[b, at], w, in_buf[b, 1, at], in_buf[b, 2, at], devices)
            weight = w - (matrix_rate * trust) * (ratio + weight_decay * w)
            out_buf[o, 0, at] = g
            out_buf[o, 1, at] = weight
            out_buf[o, 2, at] = first
            out_buf[o, 3, at] = second
            copy_buf[o, at] = weight.astype(BF)
            return 0

        lax.fori_loop(0, bs // 32, chunk, 0)
        stores(i, True)
        return 0

    lax.fori_loop(0, steps, step, 0)
    for i in range(max(0, steps - LAMB_OUT), steps):
        stores(jnp.int32(i), False)


def lamb_call(meta, slots, ys, lead, total, counts, places, rows, mats, bs, devices, before):
    width = ys[0].shape[1]
    flat = [array for mat in mats for array in mat]
    dtypes = (F32, F32, F32, F32, BF)
    out_shape = tuple(jax.ShapeDtypeStruct(mat[0].shape, dt) for mat in mats for dt in dtypes)
    aliased = list(before) if before is not None else []
    aliases = {3 + len(ys) + len(flat) + i: i for i in range(len(aliased))}
    return pl.pallas_call(
        functools.partial(lamb_kernel, counts, places, rows, lead, len(ys), devices, len(aliased)),
        out_shape=out_shape,
        in_specs=[SM, SM, VM] + [HB] * len(ys) + [HM] * (len(flat) + len(aliased)),
        out_specs=(HM,) * len(out_shape),
        scratch_shapes=[
            pltpu.VMEM((LAMB_IN, 3, bs, width), F32),
            pltpu.VMEM((LAMB_IN, bs, width), BF),
            pltpu.VMEM((LAMB_OUT, 4, bs, width), F32),
            pltpu.VMEM((LAMB_OUT, bs, width), BF),
            pltpu.SemaphoreType.DMA((LAMB_IN, 3)),
            pltpu.SemaphoreType.DMA((LAMB_IN, bs // BLK)),
            pltpu.SemaphoreType.DMA((LAMB_OUT, 5)),
        ],
        input_output_aliases=aliases,
        cost_estimate=LIGHT,
        compiler_params=pltpu.CompilerParams(vmem_limit_bytes=60 << 20),
        name="lamb",
    )(meta, slots, total, *ys, *flat, *aliased)


def bits_of(n):
    return n.bit_length() - 1


class Order:

    def __init__(self):
        self.last = None

    def run(self, fn, *args):
        if self.last is not None:
            args, _ = lax.optimization_barrier((args, self.last))
        out = fn(*args)
        leaves = jax.tree.leaves(out)
        self.last = leaves[0]
        return out


def add_bf(a, b):
    return (a.astype(F32) + b.astype(F32)).astype(BF)


def add_split(a, b):
    half = a.shape[0] // 2
    return add_bf(a[:half], b[:half]), add_bf(a[half:], b[half:])


class Exchange:

    def __init__(self, ds):
        self.ds = ds
        self.z, self.d = lax.axis_index("zero"), lax.axis_index("dp")
        self.stages = bits_of(ds)
        order = list(range(self.stages))
        self.orders = [order, [1, 0] + order[2:]]
        lanes = [
            sum((((self.d >> bit) & 1) << (self.stages - 1 - k)) for k, bit in enumerate(order)) for order in self.orders
        ]
        self.mine = jnp.where(self.z == 0, lanes[0], lanes[1]).astype(jnp.int32)
        self.other = jnp.where(self.z == 0, lanes[1], lanes[0]).astype(jnp.int32)
        self.owners = jnp.stack([1 - self.z, self.z]).astype(jnp.int32)
        base = jnp.arange(ds, dtype=jnp.int32)
        self.own_slots = base ^ self.mine
        self.slots = jnp.concatenate([base ^ self.other, self.own_slots])
        self.meta = jnp.stack([self.mine, self.mine >> (self.stages - 1), self.z]).astype(jnp.int32)

    def swap(self, a):
        return lax.ppermute(a, "zero", [(0, 1), (1, 0)])

    def hop(self, a, stage):
        pairs = []
        for d in range(self.ds):
            for c in range(2):
                pairs.append((d * 2 + c, (d ^ (1 << self.orders[c][stage])) * 2 + c))
        return lax.ppermute(a, ("dp", "zero"), pairs)


class Chain:

    def __init__(self, ex, parts):
        self.ex, self.mine, self.stage = ex, parts[1], 0
        self.recv = ex.swap(parts[0])

    def reduce(self, order):
        ex = self.ex
        if self.stage == ex.stages:
            self.shard = self.own = order.run(add_bf, self.mine, self.recv)
            self.recv = ex.hop(self.own, ex.stages - 1)
        else:
            self.mine, send = order.run(add_split, self.mine, self.recv)
            self.recv = ex.hop(send, self.stage)
        self.stage += 1

    def gather(self, order):
        ex = self.ex
        self.own = order.run(lambda a, b: jnp.concatenate([a, b], axis=0), self.own, self.recv)
        self.stage += 1
        self.recv = ex.hop(self.own, 2 * ex.stages - self.stage)


    def step(self, order):
        self.reduce(order) if self.stage <= self.ex.stages else self.gather(order)


class Total:

    def __init__(self, ex, mine, theirs):
        self.ex, self.total, self.stage = ex, mine, 0
        self.recv = ex.swap(theirs)

    def step(self, order):
        self.total = order.run(jnp.add, self.total, self.recv)
        if self.stage < self.ex.stages:
            self.recv = self.ex.hop(self.total, self.stage)
        self.stage += 1


PLAN = (
    "2", "1", "K", "3", "1", "2", "1", "2", "3", "1", "2", "nf",
    "3", "f", "1", "2", "f", "3", "f", "1", "2", "f", "3", "na",
    "2", "f", "3", "a", "L10", "3", "a", "L11", "a", "3", "a", "L201",
    "a", "L301",
)


def lamb_moments(gradient, first_old, second_old):
    correction = 1.0 - decay_rate**STEP
    first_new = decay_rate * first_old + (1.0 - decay_rate) * gradient
    second_new = decay_rate * second_old + (1.0 - decay_rate) * gradient * gradient
    direction = first_new / correction / (jnp.sqrt(second_new / correction) + adam_eps)
    return (first_new, second_new, direction)


def low(v):
    return lax.reduce_precision(v, exponent_bits=8, mantissa_bits=7)


def per_device(
    inputs,
    cotangent,
    master_joint,
    master_merge,
    master_expand,
    master_reduce,
    master_vectors,
    moment_joint,
    moment_merge,
    moment_expand,
    moment_reduce,
    moment_vectors,
    square_joint,
    square_merge,
    square_expand,
    square_reduce,
    square_vectors,
):
    zs = lax.axis_size("zero")
    ds = lax.axis_size("dp")
    devices = zs * ds
    width = inputs.shape[1]
    own_rows = master_joint.shape[0]
    ff = master_expand.shape[1]
    per_owner = ff // zs
    halves = 2 if zs == 2 else 1
    per = per_owner // halves
    rbn = own_rows // BLK
    nwr = per // BLK
    ncb = per * zs // width
    fast = zs == 2 and ds & (ds - 1) == 0 and 4 * rbn == ds and nwr + ncb * rbn == ds
    masters = [master_joint, master_merge, master_expand, master_reduce]
    moments = [moment_joint, moment_merge, moment_expand, moment_reduce]
    squares = [square_joint, square_merge, square_expand, square_reduce]
    mats = list(zip(masters, moments, squares))

    if fast:
        ex = Exchange(ds)
        owners, ffn_slots, attn_slots = ex.owners, ex.slots, ex.slots
        pieces = lambda own: [ex.swap(own), own]
    else:
        owners = jnp.arange(zs, dtype=jnp.int32)
        ffn_slots = jnp.tile(jnp.arange(nwr + ncb * rbn, dtype=jnp.int32), zs)
        attn_slots = jnp.tile(jnp.arange(4 * rbn, dtype=jnp.int32), zs)

        def pieces(own):
            full = lax.all_gather(own, "zero", axis=0)
            return [full[i] for i in range(zs)]

    head = jnp.pad(low(master_vectors), ((0, 4), (0, 4 * width - master_vectors.shape[1])))
    attn_own = jnp.concatenate([jnp.concatenate([master_joint, master_merge], axis=1), head], axis=0).astype(BF)
    attn = pieces(attn_own)
    expand = pieces(master_expand.astype(BF))
    reduce = pieces(master_reduce.astype(BF))
    vecs = [piece[own_rows : own_rows + 12, : width // zs].astype(F32) for piece in attn]
    if fast:
        vecs[1] = low(master_vectors)
        vec = jnp.where(ex.z == 0, jnp.concatenate([vecs[1], vecs[0]], 1), jnp.concatenate(vecs, 1))
    else:
        vec = jnp.concatenate(vecs, axis=1)
    bias_up = vec[7:11].reshape(1, ff)

    order = Order()
    normed, joint, mixed, middle, normed_two = order.run(forward_call, owners, inputs, vec, attn)
    res = order.run(
        functools.partial(ffn_call, halves), owners, ffn_slots, normed_two, cotangent, middle, expand, reduce, bias_up, vec
    )
    ffn_grads = [list(res[zs * half : zs * (half + 1)]) for half in range(halves)]
    bias_sums, outputs, middle_grad, merge_grad, ffn_sums = res[zs * halves :]
    chains = [Chain(ex, parts) for parts in ffn_grads] if fast else []
    frames = inputs.shape[0] // FRAME
    if fast:
        chains[0].reduce(order)
    joint_part = order.run(functools.partial(back_first_call, frames=frames), owners, joint, merge_grad, attn)
    if fast:
        chains[1].reduce(order)
        chains[0].reduce(order)
    res = order.run(
        functools.partial(back_second_call, frames=frames),
        owners, attn_slots, normed, mixed, merge_grad, joint, joint_part, attn,
    )
    attn_grads = list(res[:zs])
    joint_grad, attn_sums = res[zs:]
    if fast:
        chains.append(Chain(ex, attn_grads))
    held = {}

    def back_last():
        held["grad"], sums = order.run(back_last_call, owners, inputs, middle_grad, joint_grad, vec, attn)
        return sums

    if not fast:
        last_sums = back_last()
    if fast:
        ffn_one, ffn_two, attn_chain = chains

        def reduce_place(half):
            return lambda lane: (half * nwr + lane // (ds // 2) * (nwr // 2) + jnp.clip(lane % (ds // 2), 0, nwr // 2 - 1), 0)

        def expand_place(half):
            def place(lane):
                q = jnp.clip(lane % (ds // 2) - nwr // 2, 0, ncb * rbn // 2 - 1)
                cb, i = q // (rbn // 2), q % (rbn // 2)
                return lane // (ds // 2) * (rbn // 2) + i, cb * (per_owner // width) + half * (per // width)
            return place

        def joint_place(lane):
            q = jnp.clip(lane % (ds // 2) - rbn // 2, 0, 3 * rbn // 2 - 1)
            return lane // (ds // 2) * (rbn // 2) + q % (rbn // 2), q // (rbn // 2)

        def merge_place(lane):
            return lane // (ds // 2) * (rbn // 2) + jnp.clip(lane % (ds // 2), 0, rbn // 2 - 1), 0

        in_reduce = lambda lane: lane % (ds // 2) < nwr // 2
        in_expand = lambda lane: lane % (ds // 2) >= nwr // 2
        in_merge = lambda lane: lane % (ds // 2) < rbn // 2
        in_joint = lambda lane: lane % (ds // 2) >= rbn // 2
        regions = [
            [(in_merge, merge_place, mats[1]), (in_joint, joint_place, mats[0])],
            [(in_reduce, reduce_place(0), mats[3]), (in_expand, expand_place(0), mats[2])],
            [(in_reduce, reduce_place(1), mats[3]), (in_expand, expand_place(1), mats[2])],
        ]
        bs = 2 * BLK
        count_r = per // bs // 2
        nrb = own_rows // bs // 2

        def lamb_reduce(half):
            return lambda h, q: (half * (per // bs) + h * count_r + q, 0)

        def lamb_expand(half):
            return lambda h, q: (
                h * nrb + q % nrb, q // nrb * (per_owner // width) + half * (per // width)
            )

        lamb_merge = lambda h, q: (h * nrb + q, 0)
        lamb_joint = lambda h, q: (h * nrb + q % nrb, q // nrb)
        state = {"f": None, "a": None}
        sums = {}

        def ffn_lamb(half, leads):
            chain = chains[half]
            state["f"] = order.run(
                lambda meta, slots, ys, total, mats, before: lamb_call(
                    meta, slots, ys, leads[0], total, [count_r, ncb * nrb], [lamb_reduce(half), lamb_expand(half)],
                    [3, 2], mats, bs, devices, before,
                ),
                ex.meta, ex.own_slots, [(chain.own, chain.recv)[lead] for lead in leads], sums["f"].total, (mats[3], mats[2]), state["f"],
            )

        def attn_lamb(leads):
            state["a"] = order.run(
                lambda meta, slots, ys, total, mats, before: lamb_call(
                    meta, slots, ys, leads[0], total, [nrb, 3 * nrb], [lamb_merge, lamb_joint], [1, 0], mats, bs,
                    devices, before,
                ),
                ex.meta, ex.own_slots, [(attn_chain.own, attn_chain.recv)[lead] for lead in leads], sums["a"].total, (mats[1], mats[0]),
                state["a"],
            )

        def norms_of(key):
            if key == "f":
                groups, parts, at = (ffn_one, ffn_two), regions[1:], [[3, 2]] * 2
                small = (last_sums, attn_sums, ffn_sums, bias_sums)
                plan = [(0, 0, 0), (0, 1, 0), (1, 1, 0), (1, 2, 0), (1, 0, 0), (2, 0, 0), (2, 1, 0)]
                plan += [(3, k // halves, k % halves * width) for k in range(ff // width)] + [(2, 2, 0)]
            else:
                groups, parts, at, small, plan = (attn_chain,), regions[:1], [[1, 0]], (), []
            keep, send = order.run(
                lambda meta, small, *shards: norms_call(meta, small, plan, shards, parts, at, devices),
                ex.meta, small, *[chain.shard for chain in groups],
            )
            sums[key] = Total(ex, keep, send)

        for act in PLAN:
            if act == "K":
                last_sums = back_last()
            elif act[0] == "n":
                norms_of(act[1])
            elif act in "fa":
                sums[act].step(order)
            elif act in "123":
                chains[int(act) - 1].step(order)
            else:
                stack, leads = int(act[1]), [int(lead) for lead in act[2:]]
                attn_lamb(leads) if stack == 3 else ffn_lamb(stack - 1, leads)
        ffn_out, attn_out = state["f"], state["a"]
        vec_total = sums["f"].total[:12]
        norm_values = jnp.sqrt(sums["f"].total[NORM_ROW:, 0] + sums["a"].total[NORM_ROW:, 0])
        outs = [attn_out[5:10], attn_out[0:5], ffn_out[5:10], ffn_out[0:5]]
    else:
        def summed(parts):
            stack = lax.psum_scatter(jnp.concatenate(parts, axis=0), "zero", scatter_dimension=0, tiled=True)
            stack = lax.psum_scatter(stack, "dp", scatter_dimension=0, tiled=True)
            return lax.all_gather(stack, "dp", axis=0, tiled=True).astype(F32) / devices

        def side_by_side(stack):
            return stack.reshape(-1, own_rows, width).transpose(1, 0, 2).reshape(own_rows, -1)

        ffn = summed(ffn_grads[0])
        attn_sum = summed(attn_grads)
        grads = [
            side_by_side(attn_sum[own_rows:]), attn_sum[:own_rows], side_by_side(ffn[per:]), ffn[:per]
        ]
        rows = jnp.concatenate(
            [
                last_sums[0:2],
                attn_sums[1:3],
                attn_sums[0:1],
                ffn_sums[0:2],
                bias_sums.reshape(ff // width, width),
                ffn_sums[2:3],
            ],
            axis=0,
        )
        blocks = rows.reshape(12, zs, width // zs).transpose(1, 0, 2)
        vec_total = lax.psum(lax.psum_scatter(blocks, "zero", scatter_dimension=0, tiled=True)[0], "dp")
        moved = [lamb_moments(g, m, s) for g, m, s in zip(grads, moments, squares)]
        upds = [move[2] + weight_decay * w for move, w in zip(moved, masters)]
        local = jnp.stack([jnp.sum(w * w) for w in masters] + [jnp.sum(u * u) for u in upds])
        norm_values = jnp.sqrt(lax.psum(local, "zero"))
        outs = []
        for k in range(4):
            weight = masters[k] - matrix_rate * (norm_values[k] / norm_values[k + 4]) * upds[k]
            outs.append((grads[k], weight, moved[k][0], moved[k][1], weight.astype(BF)))

    grad_vec = vec_total / devices
    first_vec, second_vec, vec_direction = lamb_moments(grad_vec, moment_vectors, square_vectors)
    new_vectors = master_vectors - vector_rate * vec_direction
    vector_out = (grad_vec, new_vectors, first_vec, second_vec, new_vectors.astype(BF))
    result = [outputs, held["grad"]]
    for k in range(5):
        result += [out[k] for out in outs] + [vector_out[k]]
    return (*result, norm_values)


def solution(mesh):
    tokens = P(("dp", "zero"), None)
    matrix = P("zero", None)
    vector = P(None, "zero")
    five = (matrix,) * 4 + (vector,)
    return jax.shard_map(
        per_device,
        mesh=mesh,
        in_specs=(tokens, tokens) + five * 3,
        out_specs=(tokens, tokens) + five * 5 + (P(),),
        check_vma=False,
    )
```

```python
import functools

import jax
import jax.numpy as jnp
from jax import lax
from jax.experimental import pallas as pl
from jax.experimental.pallas import tpu as pltpu
from jax.sharding import PartitionSpec as P

HD = 64
FRAME = 196
STEP = 4
BLK = 96

norm_eps = 1e-06
adam_eps = 1e-06
decay_rate = 0.5
weight_decay = 0.01
matrix_rate = 0.5
vector_rate = 0.1
BF = jnp.bfloat16
F32 = jnp.float32
VM = pl.BlockSpec(memory_space=pltpu.VMEM)
SM = pl.BlockSpec(memory_space=pltpu.SMEM)
HB = pl.BlockSpec(memory_space=pl.ANY)
HM = pl.BlockSpec(memory_space=pltpu.HBM)
HEAVY = pl.CostEstimate(flops=5 * 10**10, bytes_accessed=10**8, transcendentals=0)
LIGHT = pl.CostEstimate(flops=1000, bytes_accessed=1000, transcendentals=0)
INV_SQRT2 = 0.7071067811865476
INV_SQRT2PI = 0.3989422804014327


def padded_rows(rows):
    return (rows + 15) // 16 * 16


def row_chunks(rows):
    edges = list(range(0, rows, 192))
    if rows - edges[-1] < 96 and len(edges) > 1:
        edges.pop()
    return [(s, (edges[i + 1] if i + 1 < len(edges) else rows) - s) for i, s in enumerate(edges)]


def row_halves(zs):
    return 2 if zs == 2 else 1


def dot_nn(a, b):
    return lax.dot_general(a, b, (((1,), (0,)), ((), ())), preferred_element_type=F32)


def dot_nt(a, b):
    return lax.dot_general(a, b, (((1,), (1,)), ((), ())), preferred_element_type=F32)


def dot_tn(a, b):
    return lax.dot_general(a, b, (((0,), (0,)), ((), ())), preferred_element_type=F32)


def stats(v):
    mean = jnp.mean(v, axis=-1, keepdims=True)
    c = v - mean
    r = lax.rsqrt(jnp.mean(c * c, axis=-1, keepdims=True) + norm_eps)
    return c * r, r


def piece_copies(own_ref, pieces, w_ref, sems, width):
    own_rows = width // len(pieces)
    copies = []
    for col, (first, count) in enumerate(((0, 3 * width), (3 * width, width))):
        cols = pl.ds(first, count)
        for kk, piece in enumerate(pieces):
            rws = pl.ds(pl.multiple_of(own_ref[kk] * own_rows, own_rows), own_rows)
            copies.append(
                pltpu.make_async_copy(
                    piece.at[pl.ds(0, own_rows), cols], w_ref.at[rws, cols], sems.at[col, kk]
                )
            )
    return copies[: len(pieces)], copies[len(pieces) :]


def forward_kernel(zs, own_ref, x_ref, vec_ref, *refs):
    pieces = refs[:zs]
    a_ref, j_ref, o_ref, h_ref, b_ref, w_ref, sems = refs[zs:]
    rows, width = x_ref.shape
    joint_in, merge_in = piece_copies(own_ref, pieces, w_ref, sems, width)
    for copy in joint_in + merge_in:
        copy.start()
    pad = a_ref.shape[0]
    frames = rows // FRAME
    heads = width // HD
    win = (FRAME + 12 + 15) // 16 * 16
    scale = HD ** (-0.5)
    tail = pad - 16
    a_ref[tail:pad] = jnp.zeros((16, width), BF)
    o_ref[tail:pad] = jnp.zeros((16, width), BF)
    for s, n in row_chunks(rows):
        norm, _ = stats(x_ref[s : s + n].astype(F32))
        a_ref[s : s + n] = (norm * (1.0 + vec_ref[0:1]) + vec_ref[1:2]).astype(BF)
    for copy in joint_in:
        copy.wait()
    step = width

    def joint_cols(c, _):
        cols = pl.ds(pl.multiple_of(c * step, step), step)
        per = width // step
        which = c // per
        lane = pl.ds(pl.multiple_of((c % per) * step, step), step)
        row = jnp.where(which == 0, vec_ref[2:3, lane], jnp.where(which == 2, vec_ref[3:4, lane], 0.0))
        j_ref[:, cols] = (dot_nn(a_ref[...], w_ref[:, cols]) + row).astype(BF)
        return 0

    lax.fori_loop(0, 3 * width // step, joint_cols, 0)
    key_at = lax.broadcasted_iota(jnp.int32, (win, win), 1)
    row_at = lax.broadcasted_iota(jnp.int32, (win, 2 * HD), 0)
    low = lax.broadcasted_iota(jnp.int32, (win, 2 * HD), 1) < HD

    def frame_body(f, _):
        start = pl.multiple_of((f * FRAME) // 16 * 16, 16)
        off = f * FRAME - start
        rws = pl.ds(start, win)
        keep = (key_at >= off) & (key_at < off + FRAME)
        rkeep = (row_at >= off) & (row_at < off + FRAME)
        for p in range(heads // 2):
            q2 = j_ref[rws, 2 * HD * p : 2 * HD * (p + 1)]
            k2 = j_ref[rws, width + 2 * HD * p : width + 2 * HD * (p + 1)]
            v2 = j_ref[rws, 2 * width + 2 * HD * p : 2 * width + 2 * HD * (p + 1)]
            parts = []
            for side in range(2):
                qs = jnp.where(low if side == 0 else jnp.logical_not(low), q2, jnp.zeros_like(q2))
                sc = jnp.where(keep, dot_nt(qs, k2) * scale, -1e30)
                e = jnp.exp(sc - jnp.max(sc, axis=-1, keepdims=True))
                pb = (e / jnp.sum(e, axis=-1, keepdims=True)).astype(BF)
                parts.append(dot_nn(pb, v2))
            o2 = jnp.where(low, parts[0], parts[1])
            sl = slice(2 * HD * p, 2 * HD * (p + 1))
            o_ref[rws, sl] = jnp.where(rkeep, o2, o_ref[rws, sl].astype(F32)).astype(BF)
        return 0

    lax.fori_loop(0, frames, frame_body, 0)
    for copy in merge_in:
        copy.wait()
    for s, n in row_chunks(rows):
        m = n if s + n < rows else pad - s
        hv = dot_nn(o_ref[s : s + m], w_ref[:, 3 * width :]) + vec_ref[4:5]
        hv = hv[:n] + x_ref[s : s + n].astype(F32)
        norm, _ = stats(hv)
        h_ref[s : s + n] = hv
        bv = (norm * (1.0 + vec_ref[5:6]) + vec_ref[6:7]).astype(BF)
        if m != n:
            h_ref[tail:pad] = jnp.zeros((16, width), F32)
            b_ref[tail:pad] = jnp.zeros((16, width), BF)
            h_ref[s : s + n] = hv
        b_ref[s : s + n] = bv


def forward_call(owners, x, vec, pieces):
    rows, width = x.shape
    pad = padded_rows(rows)
    zs = len(pieces)
    return pl.pallas_call(
        functools.partial(forward_kernel, zs),
        out_shape=(
            jax.ShapeDtypeStruct((pad, width), BF),
            jax.ShapeDtypeStruct((pad, 3 * width), BF),
            jax.ShapeDtypeStruct((pad, width), BF),
            jax.ShapeDtypeStruct((pad, width), F32),
            jax.ShapeDtypeStruct((pad, width), BF),
        ),
        in_specs=[SM, VM, VM] + [HB] * zs,
        out_specs=(VM,) * 5,
        scratch_shapes=[pltpu.VMEM((width, 4 * width), BF), pltpu.SemaphoreType.DMA((2, zs))],
        cost_estimate=LIGHT,
        compiler_params=pltpu.CompilerParams(vmem_limit_bytes=24 << 20),
        name="forward_attention",
    )(owners, x, vec, *pieces)


def gelu_parts(u):
    phi = 0.5 * (1.0 + lax.erf(u * INV_SQRT2))
    return u * phi, phi + u * (jnp.exp(u * u * -0.5) * INV_SQRT2PI)


def ffn_kernel(zs, tiles, own_ref, slot_ref, *refs):
    refs = list(refs)
    b_ref, e_ref, h_ref = refs[:3]
    we_in = refs[3 : 3 + zs]
    wr_in = refs[3 + zs : 3 + 2 * zs]
    bu_ref, vec_ref = refs[3 + 2 * zs : 5 + 2 * zs]
    refs = refs[5 + 2 * zs :]
    g_refs = [[refs.pop(0) for _ in range(zs)] for _ in range(tiles)]
    bug_ref, out_ref, dh_ref, dz_ref, sums_ref = refs[:5]
    es_ref, bt_ref, gs_ref, du_ref, we_bufs, wr_bufs, acc_ref, db_ref, sems = refs[5:]
    rows, width = e_ref.shape
    pad = b_ref.shape[0]
    tf = we_bufs.shape[2]
    k, t = pl.program_id(0), pl.program_id(1)
    own_rows = width // zs
    now = k * tiles + t

    def weights(n, start):
        nk, nt = n // tiles, n % tiles
        buf = n % 2
        cols = pl.ds(pl.multiple_of((own_ref[nk] * tiles + nt) * tf, 128), tf)
        for kk in range(zs):
            rws = pl.ds(pl.multiple_of(own_ref[kk] * own_rows, own_rows), own_rows)
            copy = pltpu.make_async_copy(we_in[kk].at[:, cols], we_bufs.at[buf, rws], sems.at[buf, kk])
            copy.start() if start else copy.wait()

            @pl.when(nk == kk)
            def _(kk=kk):
                rows_in = pl.ds(pl.multiple_of(nt * tf, 16), tf)
                copy = pltpu.make_async_copy(wr_in[kk].at[rows_in, :], wr_bufs.at[buf], sems.at[buf, zs])
                copy.start() if start else copy.wait()

    @pl.when(now == 0)
    def _():
        weights(now, True)

    @pl.when(now + 1 < zs * tiles)
    def _():
        weights(now + 1, True)

    nh = row_halves(zs)
    nwr = tf // BLK
    rbn = own_rows // BLK
    nblk = nwr + (tf * zs // width) * rbn
    chunk = [(0, 256), (256, 256), (512, 256), (768, pad - 768)] if pad == 992 else [(0, pad)]

    @pl.when(jnp.logical_and(k == 0, t == 0))
    def _():
        es_ref[pad - 16 : pad] = jnp.zeros((16, width), BF)
        es_ref[0:rows] = e_ref[...]
        for c in range(0, width, 256):
            bt_ref[c : c + 256, :] = b_ref[:, c : c + 256].T
        acc_ref[...] = jnp.zeros_like(acc_ref)
        db_ref[...] = jnp.zeros_like(db_ref)

    weights(now, False)
    we_ref, wr_ref = we_bufs.at[now % 2], wr_bufs.at[now % 2]
    total = jnp.zeros((1, tf), F32)
    for s, n in chunk:
        u = dot_nn(b_ref[s : s + n], we_ref[...]) + bu_ref[...]
        g, d = gelu_parts(u)
        gs_ref[s : s + n] = g.astype(BF)
        du = (dot_nt(es_ref[s : s + n], wr_ref[...]) * d).astype(BF)
        du_ref[s : s + n] = du
        total = total + jnp.sum(du.astype(F32), axis=0, keepdims=True)
    owner = own_ref[k]
    bug_ref[pl.ds(owner, 1), pl.ds(pl.multiple_of(t * tf, 128), tf)] = total
    acc_ref[...] += dot_nn(gs_ref[...], wr_ref[...])
    db_ref[...] += dot_nt(du_ref[...], we_ref[...])
    gwr = dot_tn(gs_ref[...], es_ref[...]).astype(BF)
    for tt in range(tiles):
        for kk in range(zs):
            @pl.when((k == kk) & (t == tt))
            def _(kk=kk, tt=tt):
                for i in range(nwr):
                    slot = slot_ref[kk * nblk + i // (nwr // nh) * (nblk // nh) + i % (nwr // nh)]
                    g_refs[tt][kk][pl.ds(pl.multiple_of(slot * BLK, BLK), BLK), :] = gwr[i * BLK : (i + 1) * BLK]
    col = owner * tf
    cb = col // width
    lane = pl.ds(pl.multiple_of(col % width, 128), tf)
    part = rbn // nh
    for kk in range(zs):
        rws = pl.ds(pl.multiple_of(own_ref[kk] * own_rows, own_rows), own_rows)
        gwe = dot_nn(bt_ref[rws, :], du_ref[...]).astype(BF)
        for tt in range(tiles):
            @pl.when(t == tt)
            def _(kk=kk, tt=tt, gwe=gwe):
                for i in range(rbn):
                    slot = slot_ref[kk * nblk + i // part * (nblk // nh) + nwr // nh + cb * part + i % part]
                    g_refs[tt][kk][pl.ds(pl.multiple_of(slot * BLK, BLK), BLK), lane] = gwe[i * BLK : (i + 1) * BLK]

    @pl.when(jnp.logical_and(k == zs - 1, t == tiles - 1))
    def _():
        da = jnp.zeros((1, width), F32)
        dc = jnp.zeros((1, width), F32)
        de = jnp.zeros((1, width), F32)
        for s, n in chunk:
            hv = h_ref[s : s + n]
            norm, r = stats(hv)
            db = db_ref[s : s + n]
            da = da + jnp.sum(db * norm, axis=0, keepdims=True)
            dc = dc + jnp.sum(db, axis=0, keepdims=True)
            g = db * (1.0 + vec_ref[5:6])
            ev = es_ref[s : s + n].astype(F32)
            de = de + jnp.sum(ev, axis=0, keepdims=True)
            dh = ev + r * (
                g - jnp.mean(g, axis=-1, keepdims=True) - norm * jnp.mean(g * norm, axis=-1, keepdims=True)
            )
            dh_ref[s : s + n] = dh
            dz_ref[s : s + n] = dh.astype(BF)
            ov = (hv + (acc_ref[s : s + n] + vec_ref[11:12])).astype(BF)
            m = min(n, rows - s)
            out_ref[s : s + m] = ov[:m]
        sums_ref[0:1] = da
        sums_ref[1:2] = dc
        sums_ref[2:3] = de


def ffn_call(tiles, owners, slots, b, e, h, we, wr, bu, vec):
    zs = owners.shape[0]
    pad, width = b.shape
    rows = e.shape[0]
    per_owner = we[0].shape[1] // zs
    tf = per_owner // tiles
    nrow = tf + tf * zs // width * (width // zs)

    def ffcol(k, t, own, sl):
        return own[k] * tiles + t

    in_specs = [
        VM,
        VM,
        VM,
        *[HB] * (2 * zs),
        pl.BlockSpec((1, tf), lambda k, t, own, sl: (0, ffcol(k, t, own, sl))),
        VM,
    ]
    outs = [jax.ShapeDtypeStruct((nrow, width), BF)] * (zs * tiles) + [
        jax.ShapeDtypeStruct((zs, per_owner), F32),
        jax.ShapeDtypeStruct((rows, width), BF),
        jax.ShapeDtypeStruct((pad, width), F32),
        jax.ShapeDtypeStruct((pad, width), BF),
        jax.ShapeDtypeStruct((8, width), F32),
    ]
    return pl.pallas_call(
        functools.partial(ffn_kernel, zs, tiles),
        out_shape=tuple(outs),
        grid_spec=pltpu.PrefetchScalarGridSpec(
            num_scalar_prefetch=2,
            grid=(zs, tiles),
            in_specs=in_specs,
            out_specs=(VM,) * len(outs),
            scratch_shapes=[
                pltpu.VMEM((pad, width), BF),
                pltpu.VMEM((width, pad), BF),
                pltpu.VMEM((pad, tf), BF),
                pltpu.VMEM((pad, tf), BF),
                pltpu.VMEM((2, width, tf), BF),
                pltpu.VMEM((2, tf, width), BF),
                pltpu.VMEM((pad, width), F32),
                pltpu.VMEM((pad, width), F32),
                pltpu.SemaphoreType.DMA((2, zs + 1)),
            ],
        ),
        cost_estimate=LIGHT,
        compiler_params=pltpu.CompilerParams(vmem_limit_bytes=FFN_MB << 20),
        name="ffn",
    )(owners, slots, b, e, h, *we, *wr, bu, vec)


FFN_MB = 33


def first_frames(frames):
    return (frames + 1) // 2


def attend_back(lo, hi, base, j_ref, do_ref, dj_ref, dj_base, width):
    win = (FRAME + 12 + 15) // 16 * 16
    scale = HD ** (-0.5)
    key_at = lax.broadcasted_iota(jnp.int32, (win, win), 0)
    qry_at = lax.broadcasted_iota(jnp.int32, (win, win), 1)
    low_side = lax.broadcasted_iota(jnp.int32, (win, 2 * HD), 1) < HD

    def frame_body(f, _):
        start = (f * FRAME) // 16 * 16
        off = f * FRAME - start
        rws = pl.ds(pl.multiple_of(start - base, 16), win)
        drws = pl.ds(pl.multiple_of(start - dj_base, 16), win)
        kkeep = (key_at >= off) & (key_at < off + FRAME)
        keep = kkeep & (qry_at >= off) & (qry_at < off + FRAME)
        for p in range(width // HD // 2):
            sl = [slice(w * width + 2 * HD * p, w * width + 2 * HD * (p + 1)) for w in range(3)]
            q2, k2, v2 = (j_ref[rws, sl[w]] for w in range(3))
            do2 = do_ref[rws, sl[0]]
            res = []
            for side in range(2):
                m = low_side if side == 0 else jnp.logical_not(low_side)
                zero = jnp.zeros_like(k2)
                sc = jnp.where(kkeep, dot_nt(jnp.where(m, k2, zero), q2) * scale, -1e30)
                e = jnp.exp(sc - jnp.max(sc, axis=0, keepdims=True))
                pt = jnp.where(keep, e / jnp.sum(e, axis=0, keepdims=True), 0.0)
                dp = dot_nt(jnp.where(m, v2, zero), do2)
                ds = (pt * (dp - jnp.sum(pt * dp, axis=0, keepdims=True))).astype(BF)
                res.append((dot_tn(ds, k2) * scale, dot_nn(ds, q2) * scale, dot_nn(pt.astype(BF), do2)))
            for w in range(3):
                val = jnp.where(low_side, res[0][w], res[1][w])
                dj_ref[drws, sl[w]] = (dj_ref[drws, sl[w]].astype(F32) + val).astype(BF)
        return 0

    lax.fori_loop(lo, hi, frame_body, 0)


def merge_copies(own_ref, pieces, w_ref, sems, width, first, count):
    own_rows = width // len(pieces)
    copies = []
    for kk, piece in enumerate(pieces):
        rws = pl.ds(pl.multiple_of(own_ref[kk] * own_rows, own_rows), own_rows)
        copies.append(
            pltpu.make_async_copy(piece.at[pl.ds(0, own_rows), pl.ds(first, count)], w_ref.at[rws, :], sems.at[kk])
        )
    return copies


def back_first_kernel(zs, frames, own_ref, j_ref, dz_ref, *refs):
    pieces = refs[:zs]
    dj_ref, do_ref, w_ref, sems = refs[zs:]
    width = dz_ref.shape[1]
    copies = merge_copies(own_ref, pieces, w_ref, sems, width, 3 * width, width)
    for copy in copies:
        copy.start()
    dj_ref[...] = jnp.zeros_like(dj_ref)
    for copy in copies:
        copy.wait()
    do_ref[...] = dot_nt(dz_ref[...], w_ref[...]).astype(BF)
    attend_back(0, first_frames(frames), 0, j_ref, do_ref, dj_ref, 0, width)


def back_first_call(owners, j, dz, pieces, frames):
    zs = len(pieces)
    width = dz.shape[1]
    last = first_frames(frames) - 1
    rows = (last * FRAME) // 16 * 16 + (FRAME + 12 + 15) // 16 * 16
    return pl.pallas_call(
        functools.partial(back_first_kernel, zs, frames),
        grid=(1,),
        out_shape=jax.ShapeDtypeStruct((rows, 3 * width), BF),
        in_specs=[
            SM,
            pl.BlockSpec((rows, 3 * width), lambda i: (0, 0)),
            pl.BlockSpec((rows, width), lambda i: (0, 0)),
        ]
        + [HB] * zs,
        out_specs=pl.BlockSpec((rows, 3 * width), lambda i: (0, 0)),
        scratch_shapes=[
            pltpu.VMEM((rows, width), BF),
            pltpu.VMEM((width, width), BF),
            pltpu.SemaphoreType.DMA((zs,)),
        ],
        cost_estimate=LIGHT,
        compiler_params=pltpu.CompilerParams(vmem_limit_bytes=20 << 20),
        name="back_first",
    )(owners, j, dz, *pieces)


def back_second_kernel(zs, frames, own_ref, slot_ref, a_ref, o_ref, dz_ref, j_hbm, djp_hbm, *refs):
    pieces = refs[:zs]
    g_refs = refs[zs : 2 * zs]
    dj_ref, sums_ref, j_ref, do_ref, t_ref, w_ref, sems, more = refs[2 * zs :]
    pad, width = a_ref.shape
    done = djp_hbm.shape[0]
    base = (first_frames(frames) * FRAME) // 16 * 16
    own_rows = width // zs
    rbn = own_rows // BLK
    copies = merge_copies(own_ref, pieces, w_ref, sems, width, 3 * width, width)
    copies.append(pltpu.make_async_copy(j_hbm.at[pl.ds(base, pad - base), :], j_ref, more.at[0]))
    earlier = pltpu.make_async_copy(djp_hbm, dj_ref.at[pl.ds(0, done), :], more.at[1])
    for copy in copies:
        copy.start()
    earlier.start()
    dj_ref[done:pad] = jnp.zeros((pad - done, 3 * width), BF)
    sums_ref[...] = jnp.zeros_like(sums_ref)
    for c in range(0, width, 256):
        t_ref[c : c + 256, :] = o_ref[:, c : c + 256].T
    sums_ref[0:1] = jnp.sum(dz_ref[...].astype(F32), axis=0, keepdims=True)
    part = rbn // row_halves(zs)

    def put(kk, region, i, val):
        slot = slot_ref[kk * 4 * rbn + i // part * (4 * part) + region * part + i % part]
        g_refs[kk][pl.ds(pl.multiple_of(slot * BLK, BLK), BLK), :] = val

    for kk in range(zs):
        rws = pl.ds(pl.multiple_of(own_ref[kk] * own_rows, own_rows), own_rows)
        gm = dot_nn(t_ref[rws, :], dz_ref[...]).astype(BF)
        for i in range(rbn):
            put(kk, 0, i, gm[i * BLK : (i + 1) * BLK])
    for copy in copies:
        copy.wait()
    do_ref[...] = dot_nt(dz_ref[base:pad], w_ref[...]).astype(BF)
    earlier.wait()
    attend_back(first_frames(frames), frames, base, j_ref, do_ref, dj_ref, 0, width)
    for c in range(0, width, 256):
        t_ref[c : c + 256, :] = a_ref[:, c : c + 256].T
    for w in range(3):
        cols = slice(w * width, (w + 1) * width)
        if w != 1:
            row = 1 if w == 0 else 2
            sums_ref[row : row + 1] = jnp.sum(dj_ref[:, cols].astype(F32), axis=0, keepdims=True)
        for kk in range(zs):
            rws = pl.ds(pl.multiple_of(own_ref[kk] * own_rows, own_rows), own_rows)
            gj = dot_nn(t_ref[rws, :], dj_ref[:, cols]).astype(BF)
            for i in range(rbn):
                put(kk, 1 + w, i, gj[i * BLK : (i + 1) * BLK])


def back_second_call(owners, slots, a, o, dz, j, dj_part, pieces, frames):
    zs = len(pieces)
    pad, width = a.shape
    base = (first_frames(frames) * FRAME) // 16 * 16
    nrow = 4 * (width // zs)
    return pl.pallas_call(
        functools.partial(back_second_kernel, zs, frames),
        out_shape=(jax.ShapeDtypeStruct((nrow, width), BF),) * zs
        + (jax.ShapeDtypeStruct((pad, 3 * width), BF), jax.ShapeDtypeStruct((8, width), F32)),
        in_specs=[SM] * 2 + [VM] * 3 + [HB] * (2 + zs),
        out_specs=(VM,) * (zs + 2),
        scratch_shapes=[
            pltpu.VMEM((pad - base, 3 * width), BF),
            pltpu.VMEM((pad - base, width), BF),
            pltpu.VMEM((width, pad), BF),
            pltpu.VMEM((width, width), BF),
            pltpu.SemaphoreType.DMA((zs,)),
            pltpu.SemaphoreType.DMA((2,)),
        ],
        cost_estimate=LIGHT,
        compiler_params=pltpu.CompilerParams(vmem_limit_bytes=26 << 20),
        name="back_second",
    )(owners, slots, a, o, dz, j, dj_part, *pieces)


def back_last_kernel(zs, own_ref, x_ref, dh_ref, dj_ref, vec_ref, *refs):
    pieces = refs[:zs]
    ig_ref, sums_ref, w_ref, sems = refs[zs:]
    rows, width = x_ref.shape
    pad = dj_ref.shape[0]
    copies = merge_copies(own_ref, pieces, w_ref, sems, width, 0, 3 * width)
    for copy in copies:
        copy.start()
    sums_ref[...] = jnp.zeros_like(sums_ref)
    for copy in copies:
        copy.wait()
    chunk = [(0, 256), (256, 256), (512, 256), (768, pad - 768)] if pad == 992 else [(0, pad)]
    da = jnp.zeros((1, width), F32)
    dc = jnp.zeros((1, width), F32)
    for s, n in chunk:
        m = min(n, rows - s)
        dv = dot_nt(dj_ref[s : s + n], w_ref[...])[:m]
        norm, r = stats(x_ref[s : s + m].astype(F32))
        da = da + jnp.sum(dv * norm, axis=0, keepdims=True)
        dc = dc + jnp.sum(dv, axis=0, keepdims=True)
        g = dv * (1.0 + vec_ref[0:1])
        ig_ref[s : s + m] = dh_ref[s : s + m] + r * (
            g - jnp.mean(g, axis=-1, keepdims=True) - norm * jnp.mean(g * norm, axis=-1, keepdims=True)
        )
    sums_ref[0:1] = da
    sums_ref[1:2] = dc


def back_last_call(owners, x, dh, dj, vec, pieces):
    zs = len(pieces)
    rows, width = x.shape
    return pl.pallas_call(
        functools.partial(back_last_kernel, zs),
        out_shape=(jax.ShapeDtypeStruct((rows, width), F32), jax.ShapeDtypeStruct((8, width), F32)),
        in_specs=[SM] + [VM] * 4 + [HB] * zs,
        out_specs=(VM,) * 2,
        scratch_shapes=[pltpu.VMEM((width, 3 * width), BF), pltpu.SemaphoreType.DMA((zs,))],
        cost_estimate=HEAVY,
        compiler_params=pltpu.CompilerParams(vmem_limit_bytes=18 << 20),
        name="back_last",
    )(owners, x, dh, dj, vec, *pieces)


def lamb_math(g, w, m, s, devices):
    scale = 1.0 / (1.0 - decay_rate**STEP)
    g = g.astype(F32) * (1.0 / devices)
    first = decay_rate * m + (1.0 - decay_rate) * g
    second = decay_rate * s + (1.0 - decay_rate) * g * g
    ratio = (first * scale) / (jnp.sqrt(second * scale) + adam_eps)
    return g, first, second, ratio


def norms_kernel(spots, rows, plan, n_sums, devices, meta_ref, *refs):
    sums = refs[:n_sums]
    y_refs = refs[n_sums : n_sums + len(spots)]
    mats = refs[n_sums + len(spots) : -5]
    keep_ref, send_ref, out_ref, buf, sems = refs[-5:]
    lane = meta_ref[0]
    half = keep_ref.shape[1]
    out_ref[...] = jnp.zeros_like(out_ref)
    keep_ref[...] = jnp.zeros_like(keep_ref)
    send_ref[...] = jnp.zeros_like(send_ref)
    for row, (k, source, first) in enumerate(plan):
        for target, side in ((keep_ref, meta_ref[2]), (send_ref, 1 - meta_ref[2])):
            cols = pl.ds(pl.multiple_of(first + side * half, 128), half)
            target[row : row + 1] = sums[k][source : source + 1, cols]
    width = y_refs[0].shape[1]

    def each(act):
        at = 0
        for n, (regions, places) in enumerate(zip(spots, rows)):
            for (inside, place), row in zip(regions, places):
                mat = mats[at : at + 3]
                at += 3

                @pl.when(inside(lane))
                def _(n=n, place=place, mat=mat, row=row):
                    r, c = place(lane)
                    window = pl.ds(pl.multiple_of(r * BLK, 32), BLK), pl.ds(pl.multiple_of(c * width, 128), width)
                    act(n, [pltpu.make_async_copy(mat[k].at[window], buf.at[n, k], sems.at[n, k]) for k in range(3)], row)

    def begin(n, copies, row):
        for copy in copies:
            copy.start()

    def measure(n, copies, row):
        for copy in copies:
            copy.wait()
        w = buf[n, 0]
        upd = lamb_math(y_refs[n][...], w, buf[n, 1], buf[n, 2], devices)[3] + weight_decay * w
        for at_row, square in ((row, w * w), (row + 4, upd * upd)):
            lanes = jnp.sum(square, axis=0, keepdims=True)
            out_ref[at_row : at_row + 1] += jnp.sum(lanes, axis=1, keepdims=True)

    each(begin)
    each(measure)
    keep_ref[NORM_ROW : NORM_ROW + 8, 0:128] = out_ref[...]
    send_ref[NORM_ROW : NORM_ROW + 8, 0:128] = out_ref[...]


NORM_ROW = 16


def norms_call(meta, sums, plan, shards, regions, rows, devices):
    width = shards[0].shape[1]
    cols = width // 2 if plan else 128
    mats = [array for parts in regions for part in parts for array in part[2]]
    spots = [[part[:2] for part in parts] for parts in regions]
    return pl.pallas_call(
        functools.partial(norms_kernel, spots, rows, plan, len(sums), devices),
        out_shape=(jax.ShapeDtypeStruct((NORM_ROW + 8, cols), F32),) * 2,
        in_specs=[SM] + [VM] * (len(sums) + len(shards)) + [HM] * len(mats),
        out_specs=(VM,) * 2,
        scratch_shapes=[
            pltpu.VMEM((8, 128), F32),
            pltpu.VMEM((len(shards), 3, BLK, width), F32),
            pltpu.SemaphoreType.DMA((len(shards), 3)),
        ],
        cost_estimate=LIGHT,
        compiler_params=pltpu.CompilerParams(vmem_limit_bytes=60 << 20),
        name="norms",
    )(meta, *sums, *shards, *mats)


LAMB_IN = 4
LAMB_OUT = 3


def lamb_kernel(counts, places, rows, lead, n_half, devices, n_alias, meta_ref, slot_ref, total_ref, *refs):
    nbh = sum(counts)
    ys = refs[:n_half]
    ins = refs[n_half : n_half + 6]
    outs = refs[n_half + 6 + n_alias : n_half + 16 + n_alias]
    in_buf, y_buf, out_buf, copy_buf, in_sem, y_sem, out_sem = refs[n_half + 16 + n_alias :]
    bs = in_buf.shape[2]
    width = in_buf.shape[3]
    per = bs // BLK
    steps = nbh * n_half
    half_blk = ys[0].shape[0] // BLK

    def where(i):
        rel, q = i // nbh, i % nbh
        return rel, (rel + lead) ^ meta_ref[1], q

    def window(p, half, q):
        row, col = places[p](half, q - (counts[0] if p else 0))
        return pl.ds(pl.multiple_of(row * bs, bs), bs), pl.ds(pl.multiple_of(col * width, width), width)

    def loads(i, start):
        rel, half, q = where(i)
        b = i % LAMB_IN
        for p in range(2):
            @pl.when((q >= counts[0]) == (p == 1))
            def _(p=p):
                at = window(p, half, q)
                for k in range(3):
                    copy = pltpu.make_async_copy(ins[3 * p + k].at[at], in_buf.at[b, k], in_sem.at[b, k])
                    copy.start() if start else copy.wait()
        for r in range(n_half):
            @pl.when(rel == r)
            def _(r=r):
                for k in range(per):
                    slot = slot_ref[half * half_blk + q * per + k] - (r + lead) * half_blk
                    copy = pltpu.make_async_copy(
                        ys[r].at[pl.ds(pl.multiple_of(slot * BLK, BLK), BLK), :],
                        y_buf.at[b, pl.ds(k * BLK, BLK)], y_sem.at[b, k],
                    )
                    copy.start() if start else copy.wait()

    def stores(i, start):
        _, half, q = where(i)
        b = i % LAMB_OUT
        for p in range(2):
            @pl.when((q >= counts[0]) == (p == 1))
            def _(p=p):
                at = window(p, half, q)
                for k in range(5):
                    src = copy_buf.at[b] if k == 4 else out_buf.at[b, k]
                    copy = pltpu.make_async_copy(src, outs[5 * p + k].at[at], out_sem.at[b, k])
                    copy.start() if start else copy.wait()

    for i in range(LAMB_IN - 1):
        loads(jnp.int32(i), True)

    def step(i, _):
        b, o = i % LAMB_IN, i % LAMB_OUT

        @pl.when(i + LAMB_IN - 1 < steps)
        def _():
            loads(i + LAMB_IN - 1, True)

        loads(i, False)

        @pl.when(i >= LAMB_OUT)
        def _():
            stores(i - LAMB_OUT, False)

        _, _, q = where(i)
        trusts = []
        for row in rows:
            at = NORM_ROW + row
            trusts.append(jnp.sqrt(total_ref[at : at + 1, 0:1]) / jnp.sqrt(total_ref[at + 4 : at + 5, 0:1]))
        trust = jnp.where(q >= counts[0], trusts[1], trusts[0])

        def chunk(c, _):
            at = pl.ds(pl.multiple_of(c * 32, 32), 32)
            w = in_buf[b, 0, at]
            g, first, second, ratio = lamb_math(y_buf[b, at], w, in_buf[b, 1, at], in_buf[b, 2, at], devices)
            weight = w - (matrix_rate * trust) * (ratio + weight_decay * w)
            out_buf[o, 0, at] = g
            out_buf[o, 1, at] = weight
            out_buf[o, 2, at] = first
            out_buf[o, 3, at] = second
            copy_buf[o, at] = weight.astype(BF)
            return 0

        lax.fori_loop(0, bs // 32, chunk, 0)
        stores(i, True)
        return 0

    lax.fori_loop(0, steps, step, 0)
    for i in range(max(0, steps - LAMB_OUT), steps):
        stores(jnp.int32(i), False)


def lamb_call(meta, slots, ys, lead, total, counts, places, rows, mats, bs, devices, before):
    width = ys[0].shape[1]
    flat = [array for mat in mats for array in mat]
    dtypes = (F32, F32, F32, F32, BF)
    out_shape = tuple(jax.ShapeDtypeStruct(mat[0].shape, dt) for mat in mats for dt in dtypes)
    aliased = list(before) if before is not None else []
    aliases = {3 + len(ys) + len(flat) + i: i for i in range(len(aliased))}
    return pl.pallas_call(
        functools.partial(lamb_kernel, counts, places, rows, lead, len(ys), devices, len(aliased)),
        out_shape=out_shape,
        in_specs=[SM, SM, VM] + [HB] * len(ys) + [HM] * (len(flat) + len(aliased)),
        out_specs=(HM,) * len(out_shape),
        scratch_shapes=[
            pltpu.VMEM((LAMB_IN, 3, bs, width), F32),
            pltpu.VMEM((LAMB_IN, bs, width), BF),
            pltpu.VMEM((LAMB_OUT, 4, bs, width), F32),
            pltpu.VMEM((LAMB_OUT, bs, width), BF),
            pltpu.SemaphoreType.DMA((LAMB_IN, 3)),
            pltpu.SemaphoreType.DMA((LAMB_IN, bs // BLK)),
            pltpu.SemaphoreType.DMA((LAMB_OUT, 5)),
        ],
        input_output_aliases=aliases,
        cost_estimate=LIGHT,
        compiler_params=pltpu.CompilerParams(vmem_limit_bytes=60 << 20),
        name="lamb",
    )(meta, slots, total, *ys, *flat, *aliased)


def bits_of(n):
    return n.bit_length() - 1


class Order:

    def __init__(self):
        self.last = None

    def run(self, fn, *args):
        if self.last is not None:
            args, _ = lax.optimization_barrier((args, self.last))
        out = fn(*args)
        leaves = jax.tree.leaves(out)
        self.last = leaves[0]
        return out


def add_bf(a, b):
    return (a.astype(F32) + b.astype(F32)).astype(BF)


def add_split(a, b):
    half = a.shape[0] // 2
    return add_bf(a[:half], b[:half]), add_bf(a[half:], b[half:])


class Exchange:

    def __init__(self, ds):
        self.ds = ds
        self.z, self.d = lax.axis_index("zero"), lax.axis_index("dp")
        self.stages = bits_of(ds)
        order = list(range(self.stages))
        self.orders = [order, [1, 0] + order[2:]]
        lanes = [
            sum((((self.d >> bit) & 1) << (self.stages - 1 - k)) for k, bit in enumerate(order)) for order in self.orders
        ]
        self.mine = jnp.where(self.z == 0, lanes[0], lanes[1]).astype(jnp.int32)
        self.other = jnp.where(self.z == 0, lanes[1], lanes[0]).astype(jnp.int32)
        self.owners = jnp.stack([1 - self.z, self.z]).astype(jnp.int32)
        base = jnp.arange(ds, dtype=jnp.int32)
        self.own_slots = base ^ self.mine
        self.slots = jnp.concatenate([base ^ self.other, self.own_slots])
        self.meta = jnp.stack([self.mine, self.mine >> (self.stages - 1), self.z]).astype(jnp.int32)

    def swap(self, a):
        return lax.ppermute(a, "zero", [(0, 1), (1, 0)])

    def hop(self, a, stage):
        pairs = []
        for d in range(self.ds):
            for c in range(2):
                pairs.append((d * 2 + c, (d ^ (1 << self.orders[c][stage])) * 2 + c))
        return lax.ppermute(a, ("dp", "zero"), pairs)


class Chain:

    def __init__(self, ex, parts):
        self.ex, self.mine, self.stage = ex, parts[1], 0
        self.recv = ex.swap(parts[0])

    def reduce(self, order):
        ex = self.ex
        if self.stage == ex.stages:
            self.shard = self.own = order.run(add_bf, self.mine, self.recv)
            self.recv = ex.hop(self.own, ex.stages - 1)
        else:
            self.mine, send = order.run(add_split, self.mine, self.recv)
            self.recv = ex.hop(send, self.stage)
        self.stage += 1

    def gather(self, order):
        ex = self.ex
        self.own = order.run(lambda a, b: jnp.concatenate([a, b], axis=0), self.own, self.recv)
        self.stage += 1
        self.recv = ex.hop(self.own, 2 * ex.stages - self.stage)


    def step(self, order):
        self.reduce(order) if self.stage <= self.ex.stages else self.gather(order)


class Total:

    def __init__(self, ex, mine, theirs):
        self.ex, self.total, self.stage = ex, mine, 0
        self.recv = ex.swap(theirs)

    def step(self, order):
        self.total = order.run(jnp.add, self.total, self.recv)
        if self.stage < self.ex.stages:
            self.recv = self.ex.hop(self.total, self.stage)
        self.stage += 1


PLAN = (
    "2", "1", "K", "3", "1", "2", "1", "2", "3", "1", "2", "nf",
    "3", "f", "1", "2", "f", "3", "f", "1", "2", "f", "3", "na",
    "2", "f", "3", "a", "L10", "3", "a", "L11", "a", "3", "a", "L201",
    "a", "L301",
)


def lamb_moments(gradient, first_old, second_old):
    correction = 1.0 - decay_rate**STEP
    first_new = decay_rate * first_old + (1.0 - decay_rate) * gradient
    second_new = decay_rate * second_old + (1.0 - decay_rate) * gradient * gradient
    direction = first_new / correction / (jnp.sqrt(second_new / correction) + adam_eps)
    return (first_new, second_new, direction)


def low(v):
    return lax.reduce_precision(v, exponent_bits=8, mantissa_bits=7)


def per_device(
    inputs,
    cotangent,
    master_joint,
    master_merge,
    master_expand,
    master_reduce,
    master_vectors,
    moment_joint,
    moment_merge,
    moment_expand,
    moment_reduce,
    moment_vectors,
    square_joint,
    square_merge,
    square_expand,
    square_reduce,
    square_vectors,
):
    zs = lax.axis_size("zero")
    ds = lax.axis_size("dp")
    devices = zs * ds
    width = inputs.shape[1]
    own_rows = master_joint.shape[0]
    ff = master_expand.shape[1]
    per_owner = ff // zs
    halves = 2 if zs == 2 else 1
    per = per_owner // halves
    rbn = own_rows // BLK
    nwr = per // BLK
    ncb = per * zs // width
    fast = zs == 2 and ds & (ds - 1) == 0 and 4 * rbn == ds and nwr + ncb * rbn == ds
    masters = [master_joint, master_merge, master_expand, master_reduce]
    moments = [moment_joint, moment_merge, moment_expand, moment_reduce]
    squares = [square_joint, square_merge, square_expand, square_reduce]
    mats = list(zip(masters, moments, squares))

    if fast:
        ex = Exchange(ds)
        owners, ffn_slots, attn_slots = ex.owners, ex.slots, ex.slots
        pieces = lambda own: [ex.swap(own), own]
    else:
        owners = jnp.arange(zs, dtype=jnp.int32)
        ffn_slots = jnp.tile(jnp.arange(nwr + ncb * rbn, dtype=jnp.int32), zs)
        attn_slots = jnp.tile(jnp.arange(4 * rbn, dtype=jnp.int32), zs)

        def pieces(own):
            full = lax.all_gather(own, "zero", axis=0)
            return [full[i] for i in range(zs)]

    head = jnp.pad(low(master_vectors), ((0, 4), (0, 4 * width - master_vectors.shape[1])))
    attn_own = jnp.concatenate([jnp.concatenate([master_joint, master_merge], axis=1), head], axis=0).astype(BF)
    attn = pieces(attn_own)
    expand = pieces(master_expand.astype(BF))
    reduce = pieces(master_reduce.astype(BF))
    vecs = [piece[own_rows : own_rows + 12, : width // zs].astype(F32) for piece in attn]
    if fast:
        vecs[1] = low(master_vectors)
        vec = jnp.where(ex.z == 0, jnp.concatenate([vecs[1], vecs[0]], 1), jnp.concatenate(vecs, 1))
    else:
        vec = jnp.concatenate(vecs, axis=1)
    bias_up = vec[7:11].reshape(1, ff)

    order = Order()
    normed, joint, mixed, middle, normed_two = order.run(forward_call, owners, inputs, vec, attn)
    res = order.run(
        functools.partial(ffn_call, halves), owners, ffn_slots, normed_two, cotangent, middle, expand, reduce, bias_up, vec
    )
    ffn_grads = [list(res[zs * half : zs * (half + 1)]) for half in range(halves)]
    bias_sums, outputs, middle_grad, merge_grad, ffn_sums = res[zs * halves :]
    chains = [Chain(ex, parts) for parts in ffn_grads] if fast else []
    frames = inputs.shape[0] // FRAME
    if fast:
        chains[0].reduce(order)
    joint_part = order.run(functools.partial(back_first_call, frames=frames), owners, joint, merge_grad, attn)
    if fast:
        chains[1].reduce(order)
        chains[0].reduce(order)
    res = order.run(
        functools.partial(back_second_call, frames=frames),
        owners, attn_slots, normed, mixed, merge_grad, joint, joint_part, attn,
    )
    attn_grads = list(res[:zs])
    joint_grad, attn_sums = res[zs:]
    if fast:
        chains.append(Chain(ex, attn_grads))
    held = {}

    def back_last():
        held["grad"], sums = order.run(back_last_call, owners, inputs, middle_grad, joint_grad, vec, attn)
        return sums

    if not fast:
        last_sums = back_last()
    if fast:
        ffn_one, ffn_two, attn_chain = chains

        def reduce_place(half):
            return lambda lane: (half * nwr + lane // (ds // 2) * (nwr // 2) + jnp.clip(lane % (ds // 2), 0, nwr // 2 - 1), 0)

        def expand_place(half):
            def place(lane):
                q = jnp.clip(lane % (ds // 2) - nwr // 2, 0, ncb * rbn // 2 - 1)
                cb, i = q // (rbn // 2), q % (rbn // 2)
                return lane // (ds // 2) * (rbn // 2) + i, cb * (per_owner // width) + half * (per // width)
            return place

        def joint_place(lane):
            q = jnp.clip(lane % (ds // 2) - rbn // 2, 0, 3 * rbn // 2 - 1)
            return lane // (ds // 2) * (rbn // 2) + q % (rbn // 2), q // (rbn // 2)

        def merge_place(lane):
            return lane // (ds // 2) * (rbn // 2) + jnp.clip(lane % (ds // 2), 0, rbn // 2 - 1), 0

        in_reduce = lambda lane: lane % (ds // 2) < nwr // 2
        in_expand = lambda lane: lane % (ds // 2) >= nwr // 2
        in_merge = lambda lane: lane % (ds // 2) < rbn // 2
        in_joint = lambda lane: lane % (ds // 2) >= rbn // 2
        regions = [
            [(in_merge, merge_place, mats[1]), (in_joint, joint_place, mats[0])],
            [(in_reduce, reduce_place(0), mats[3]), (in_expand, expand_place(0), mats[2])],
            [(in_reduce, reduce_place(1), mats[3]), (in_expand, expand_place(1), mats[2])],
        ]
        bs = 2 * BLK
        count_r = per // bs // 2
        nrb = own_rows // bs // 2

        def lamb_reduce(half):
            return lambda h, q: (half * (per // bs) + h * count_r + q, 0)

        def lamb_expand(half):
            return lambda h, q: (
                h * nrb + q % nrb, q // nrb * (per_owner // width) + half * (per // width)
            )

        lamb_merge = lambda h, q: (h * nrb + q, 0)
        lamb_joint = lambda h, q: (h * nrb + q % nrb, q // nrb)
        state = {"f": None, "a": None}
        sums = {}

        def ffn_lamb(half, leads):
            chain = chains[half]
            state["f"] = order.run(
                lambda meta, slots, ys, total, mats, before: lamb_call(
                    meta, slots, ys, leads[0], total, [count_r, ncb * nrb], [lamb_reduce(half), lamb_expand(half)],
                    [3, 2], mats, bs, devices, before,
                ),
                ex.meta, ex.own_slots, [(chain.own, chain.recv)[lead] for lead in leads], sums["f"].total, (mats[3], mats[2]), state["f"],
            )

        def attn_lamb(leads):
            state["a"] = order.run(
                lambda meta, slots, ys, total, mats, before: lamb_call(
                    meta, slots, ys, leads[0], total, [nrb, 3 * nrb], [lamb_merge, lamb_joint], [1, 0], mats, bs,
                    devices, before,
                ),
                ex.meta, ex.own_slots, [(attn_chain.own, attn_chain.recv)[lead] for lead in leads], sums["a"].total, (mats[1], mats[0]),
                state["a"],
            )

        def norms_of(key):
            if key == "f":
                groups, parts, at = (ffn_one, ffn_two), regions[1:], [[3, 2]] * 2
                small = (last_sums, attn_sums, ffn_sums, bias_sums)
                plan = [(0, 0, 0), (0, 1, 0), (1, 1, 0), (1, 2, 0), (1, 0, 0), (2, 0, 0), (2, 1, 0)]
                plan += [(3, k // halves, k % halves * width) for k in range(ff // width)] + [(2, 2, 0)]
            else:
                groups, parts, at, small, plan = (attn_chain,), regions[:1], [[1, 0]], (), []
            keep, send = order.run(
                lambda meta, small, *shards: norms_call(meta, small, plan, shards, parts, at, devices),
                ex.meta, small, *[chain.shard for chain in groups],
            )
            sums[key] = Total(ex, keep, send)

        for act in PLAN:
            if act == "K":
                last_sums = back_last()
            elif act[0] == "n":
                norms_of(act[1])
            elif act in "fa":
                sums[act].step(order)
            elif act in "123":
                chains[int(act) - 1].step(order)
            else:
                stack, leads = int(act[1]), [int(lead) for lead in act[2:]]
                attn_lamb(leads) if stack == 3 else ffn_lamb(stack - 1, leads)
        ffn_out, attn_out = state["f"], state["a"]
        vec_total = sums["f"].total[:12]
        norm_values = jnp.sqrt(sums["f"].total[NORM_ROW:, 0] + sums["a"].total[NORM_ROW:, 0])
        outs = [attn_out[5:10], attn_out[0:5], ffn_out[5:10], ffn_out[0:5]]
    else:
        def summed(parts):
            stack = lax.psum_scatter(jnp.concatenate(parts, axis=0), "zero", scatter_dimension=0, tiled=True)
            stack = lax.psum_scatter(stack, "dp", scatter_dimension=0, tiled=True)
            return lax.all_gather(stack, "dp", axis=0, tiled=True).astype(F32) / devices

        def side_by_side(stack):
            return stack.reshape(-1, own_rows, width).transpose(1, 0, 2).reshape(own_rows, -1)

        ffn = summed(ffn_grads[0])
        attn_sum = summed(attn_grads)
        grads = [
            side_by_side(attn_sum[own_rows:]), attn_sum[:own_rows], side_by_side(ffn[per:]), ffn[:per]
        ]
        rows = jnp.concatenate(
            [
                last_sums[0:2],
                attn_sums[1:3],
                attn_sums[0:1],
                ffn_sums[0:2],
                bias_sums.reshape(ff // width, width),
                ffn_sums[2:3],
            ],
            axis=0,
        )
        blocks = rows.reshape(12, zs, width // zs).transpose(1, 0, 2)
        vec_total = lax.psum(lax.psum_scatter(blocks, "zero", scatter_dimension=0, tiled=True)[0], "dp")
        moved = [lamb_moments(g, m, s) for g, m, s in zip(grads, moments, squares)]
        upds = [move[2] + weight_decay * w for move, w in zip(moved, masters)]
        local = jnp.stack([jnp.sum(w * w) for w in masters] + [jnp.sum(u * u) for u in upds])
        norm_values = jnp.sqrt(lax.psum(local, "zero"))
        outs = []
        for k in range(4):
            weight = masters[k] - matrix_rate * (norm_values[k] / norm_values[k + 4]) * upds[k]
            outs.append((grads[k], weight, moved[k][0], moved[k][1], weight.astype(BF)))

    grad_vec = vec_total / devices
    first_vec, second_vec, vec_direction = lamb_moments(grad_vec, moment_vectors, square_vectors)
    new_vectors = master_vectors - vector_rate * vec_direction
    vector_out = (grad_vec, new_vectors, first_vec, second_vec, new_vectors.astype(BF))
    result = [outputs, held["grad"]]
    for k in range(5):
        result += [out[k] for out in outs] + [vector_out[k]]
    return (*result, norm_values)


def solution(mesh):
    tokens = P(("dp", "zero"), None)
    matrix = P("zero", None)
    vector = P(None, "zero")
    five = (matrix,) * 4 + (vector,)
    return jax.shard_map(
        per_device,
        mesh=mesh,
        in_specs=(tokens, tokens) + five * 3,
        out_specs=(tokens, tokens) + five * 5 + (P(),),
        check_vma=False,
    )
```
